32 devices in a mesh: dp: 8 (over z, x), tensor: 4 (over y, core).
Axes of the slice: x: 2, y: 2, z: 4, core: 2. Of those that a mesh axis runs over, the one named last changes fastest.
Arguments:
- tokens: bfloat16 [12288, 768], P('dp'), may hold values from -6 to 6
- grad_out: bfloat16 [12288, 768], P('dp'), may hold values from -8 to 8
- token_weight: float32 [12288], P('dp'), may hold values from 0.5 to 2
- lengths: int32 [24], P('dp'), may hold values from 1 to 512, 6144 in all
- step: int32 [1], replicated, may hold values from 2 to 20
- qkv_weight: bfloat16 [3, 768, 768], P(None, 'dp', 'tensor'), may hold values from -0.21875 to 0.21875
- out_weight: bfloat16 [768, 768], P('tensor', 'dp'), may hold values from -1.75 to 1.75
- up_weight: bfloat16 [768, 3072], P('dp', 'tensor'), may hold values from -0.21875 to 0.21875
- down_weight: bfloat16 [3072, 768], P('tensor', 'dp'), may hold values from -0.109375 to 0.109375
- norm_params: bfloat16 [4, 768], P(None, 'dp'), may hold values from 0.5 to 1.5
- first_qkv: float32 [3, 768, 768], P(None, 'dp', 'tensor'), may hold values from -32 to 32
- first_out: float32 [768, 768], P('tensor', 'dp'), may hold values from -4 to 4
- first_up: float32 [768, 3072], P('dp', 'tensor'), may hold values from -20 to 20
- first_down: float32 [3072, 768], P('tensor', 'dp'), may hold values from -40 to 40
- first_norm: float32 [4, 768], P(None, 'dp'), may hold values from -56 to 56
- second_qkv: float32 [3, 768, 768], P(None, 'dp', 'tensor'), may hold values from 143.21678 to 572.8671
- second_out: float32 [768, 768], P('tensor', 'dp'), may hold values from 2.2413425 to 8.951049
- second_up: float32 [768, 3072], P('dp', 'tensor'), may hold values from 57.01632 to 227.9424
- second_down: float32 [3072, 768], P('tensor', 'dp'), may hold values from 191.6928 to 768
- second_norm: float32 [4, 768], P(None, 'dp'), may hold values from 391.3728 to 1566.72
Outputs:
- output: bfloat16 [12288, 768], P('dp')
- grad_input: float32 [12288, 768], P('dp')
- new_qkv: float32 [3, 768, 768], P(None, 'dp', 'tensor')
- moment_qkv: float32 [3, 768, 768], P(None, 'dp', 'tensor')
- square_qkv: float32 [3, 768, 768], P(None, 'dp', 'tensor')
- copy_qkv: bfloat16 [3, 768, 768], P(None, 'dp', 'tensor')
- new_out: float32 [768, 768], P('tensor', 'dp')
- moment_out: float32 [768, 768], P('tensor', 'dp')
- square_out: float32 [768, 768], P('tensor', 'dp')
- copy_out: bfloat16 [768, 768], P('tensor', 'dp')
- new_up: float32 [768, 3072], P('dp', 'tensor')
- moment_up: float32 [768, 3072], P('dp', 'tensor')
- square_up: float32 [768, 3072], P('dp', 'tensor')
- copy_up: bfloat16 [768, 3072], P('dp', 'tensor')
- new_down: float32 [3072, 768], P('tensor', 'dp')
- moment_down: float32 [3072, 768], P('tensor', 'dp')
- square_down: float32 [3072, 768], P('tensor', 'dp')
- copy_down: bfloat16 [3072, 768], P('tensor', 'dp')
- new_norm: float32 [4, 768], P(None, 'dp')
- moment_norm: float32 [4, 768], P(None, 'dp')
- square_norm: float32 [4, 768], P(None, 'dp')
- copy_norm: bfloat16 [4, 768], P(None, 'dp')
The draws below stay inside these ranges and needn't reach their ends.
Inputs may be any that keep to these rules, and one draw needn't show every extreme that they name: `lengths`: used tokens of each sequence; one sequence uses all 512 slots.
All inputs are finite; a program needn't handle non-finite values. No bound on the sum of `lengths` on one device may be relied on, other than what follows from the above.
Results may differ from the reference program's by a relative error of at most 0.014.
Values may be sent and summed in bfloat16 or wider, within the bound.
No kernel may reach another device: no remote copies, remote signals or barrier semaphores. Data moves between devices by JAX's collectives and lax.ppermute only.
A program may use at most 128 MiB of HBM per device.

```python
import math
import jax
import jax.numpy as jnp
import numpy as np
from jax import lax

D = 768
HEADS = 12
HD = 64
FF = 3072
L = 512
SEQS = 24
TOKENS = 12288


def with_spikes(values, stream_key, source, target, parts, factor):
    owner, partner = [(jnp.arange(values.shape[dim]) // (values.shape[dim] // parts)).reshape([-1 if axis == dim else 1 for axis in range(values.ndim)]) for dim in (source, target)]
    chosen = jax.random.permutation(stream_key, parts)[partner]
    strong = (owner == chosen) | (owner == (partner + parts // 2) % parts)
    return jnp.where(strong, factor * values, values)


def level_of(rng, dims, split, smallest, high):
    factor_of, own = 1.0, jax.random.fold_in(rng, 6)
    for position, blocks in split:
        draws = jnp.exp(jax.random.uniform(jax.random.fold_in(own, position), (blocks,), jnp.float32, smallest / len(split), high / len(split)))
        factor_of = factor_of * jnp.repeat(draws, dims[position] // blocks).reshape([-1 if axis == position else 1 for axis in range(len(dims))])
    return factor_of


def split_up(number_of, total, reach, lean):
    weights = [(1 << 20) // math.isqrt(standing ** lean) + 1 for standing in range(2, number_of + 1)]
    spare, given = total - reach - (number_of - 1), [1] * (number_of - 1)
    while spare > 0:
        free = [i for i in range(number_of - 1) if given[i] < reach]
        mass, remaining = sum([weights[i] for i in free]), spare
        for i in free:
            extra = min(reach - given[i], max(1, remaining * weights[i] // mass), spare)
            given[i] = given[i] + extra
            spare = spare - extra
    return np.array([reach] + given)


def uneven_parts(stream_key, number_of, total, bound, slope):
    if number_of == 2:
        one = jax.random.randint(stream_key, (), max(1, total - bound), min(bound, total - 1) + 1)
        return jnp.stack([one, total - one])
    tallies = jnp.asarray(split_up(number_of, total, bound, slope), jnp.int32)
    pairs = (number_of - 1) // 2
    source_of, taker = tallies[1:1 + 2 * pairs:2], tallies[2:2 + 2 * pairs:2]
    slack = jnp.minimum(source_of - 1, bound - taker)
    moved = jax.random.randint(jax.random.fold_in(stream_key, 1), (pairs,), 0, 1 << 20) % (slack + 1)
    tallies = tallies.at[1:1 + 2 * pairs:2].set(source_of - moved).at[2:2 + 2 * pairs:2].set(taker + moved)
    return tallies[jax.random.permutation(jax.random.fold_in(stream_key, 2), number_of)]


def gaussian(stream_key, dims, spread, limit, shards=(), dtype=jnp.bfloat16):
    values = jax.random.normal(stream_key, dims, jnp.float32) * spread
    if len(shards) > 0:
        values = level_of(stream_key, dims, shards, -0.22, 0.18) * values
    return jnp.clip(values, min=-limit, max=limit).astype(dtype)


def noise_with(rng, extent, scale, most, pieces, heavy, dtype=jnp.bfloat16):
    entries = scale * jax.random.normal(rng, extent, jnp.float32)
    if pieces:
        entries = entries * level_of(rng, extent, pieces, -0.22, 0.18)
    return jnp.clip(with_spikes(entries, jax.random.fold_in(rng, 3), *heavy), -most, most).astype(dtype)


def setup_inputs(seed: int = 0) -> dict:
    key_of = jax.random.split(jax.random.key(seed), 21)
    return {
        "tokens": gaussian(key_of[0], (TOKENS, D), 1.0, 6.0, ((0, 8),)),
        "grad_out": noise_with(key_of[1], (TOKENS, D), 1.0, 8.0, ((0, 8),), (0, 1, 8, 2.0)),
        "token_weight": jnp.clip(jnp.exp(math.log(2.0) - 1.3862944 * jax.random.uniform(key_of[2], (TOKENS,), jnp.float32) ** level_of(key_of[2], (TOKENS,), ((0, 8),), -0.2, 0.2)), 0.5, 2.0),
        "lengths": uneven_parts(key_of[3], SEQS, SEQS * L // 2, L, 2).astype(jnp.int32),
        "step": jax.random.randint(key_of[4], (1,), 2, 21).astype(jnp.int32),
        "qkv_weight": gaussian(key_of[5], (3, D, D), D ** -0.5, 0.21875, ((1, 8), (2, 4))),
        "out_weight": gaussian(key_of[6], (D, D), (D // 64) ** -0.5, 1.75, ((0, 4), (1, 8))),
        "up_weight": gaussian(key_of[7], (D, FF), D ** -0.5, 0.21875, ((0, 8), (1, 4))),
        "down_weight": gaussian(key_of[8], (FF, D), FF ** -0.5, 0.109375, ((0, 4), (1, 8))),
        "norm_params": jnp.clip(1.0 + 0.1 * jax.random.normal(key_of[9], (4, D), jnp.float32), 0.5, 1.5).astype(jnp.bfloat16),
        "first_qkv": gaussian(key_of[10], (3, D, D), (2.16 * ((TOKENS // 2) / (L + 346)) ** 0.5), 32.0, ((1, 8), (2, 4)), jnp.float32),
        "first_out": gaussian(key_of[11], (D, D), (0.271 * ((TOKENS // 2) / (L + 346)) ** 0.5), 4.0, ((0, 4), (1, 8)), jnp.float32),
        "first_up": gaussian(key_of[12], (D, FF), (0.047 * (TOKENS // 2) ** 0.5), 20.0, ((0, 8), (1, 4)), jnp.float32),
        "first_down": gaussian(key_of[13], (FF, D), (0.085 * (TOKENS // 2) ** 0.5), 40.0, ((0, 4), (1, 8)), jnp.float32),
        "first_norm": gaussian(key_of[14], (4, D), (0.122 * (TOKENS // 2) ** 0.5), 56.0, ((1, 8),), jnp.float32),
        "second_qkv": jnp.clip(jnp.exp(math.log(572.8671) - 1.3862944 * jax.random.uniform(key_of[15], (3, D, D), jnp.float32) ** level_of(key_of[15], (3, D, D), ((1, 8), (2, 4)), -0.2, 0.2)), 143.21678, 572.8671),
        "second_out": jnp.clip(jnp.exp(math.log(8.951049) - 1.3846957 * jax.random.uniform(key_of[16], (D, D), jnp.float32) ** level_of(key_of[16], (D, D), ((0, 4), (1, 8)), -0.2, 0.2)), 2.2413425, 8.951049),
        "second_up": jnp.clip(jnp.exp(math.log(227.9424) - 1.3857554 * jax.random.uniform(key_of[17], (D, FF), jnp.float32) ** level_of(key_of[17], (D, FF), ((0, 8), (1, 4)), -0.2, 0.2)), 57.01632, 227.9424),
        "second_down": jnp.clip(jnp.exp(math.log(768.0) - 1.3878957 * jax.random.uniform(key_of[18], (FF, D), jnp.float32) ** level_of(key_of[18], (FF, D), ((0, 4), (1, 8)), -0.2, 0.2)), 191.6928, 768.0),
        "second_norm": jnp.clip(jnp.exp(math.log(1566.72) - 1.387079 * jax.random.uniform(key_of[19], (4, D), jnp.float32) ** level_of(key_of[19], (4, D), ((1, 8),), -0.2, 0.2)), 391.3728, 1566.72),
    }


@jax.custom_vjp
def low(v):
    return lax.optimization_barrier(v.astype(jnp.bfloat16)).astype(jnp.float32)

@jax.custom_vjp
def low_back(v):
    return v

def low_keep(v):
    return (low(v), None)

def low_pass(kept, grad):
    return (grad,)

def back_keep(v):
    return (v, None)

def back_low(kept, grad):
    return (low(grad),)
low.defvjp(low_keep, low_pass)
low_back.defvjp(back_keep, back_low)
NORM_EPS = 1e-05
BETA_ONE = 0.9
BETA_TWO = 0.95
ADAM_EPS = 1e-08
DECAY_RATE = 0.01
PEAK_RATE = 0.15
WARM_STEPS = 2.0
LAST_STEP = 40.0
MASK_VALUE = -1000000000.0
HIGH = lax.Precision.HIGHEST

def layer_norm(summed, gain, shift):
    center = summed - lax.optimization_barrier(jnp.mean(summed, axis=-1, keepdims=True))
    variance = lax.optimization_barrier(jnp.mean(center * center, axis=-1, keepdims=True))
    return center * lax.rsqrt(variance + NORM_EPS) * gain + shift

def forward(tok_float, qkv_w, out_w, up_w, down_w, norm_w, length):
    raw = jnp.einsum('td,cde->cte', tok_float, qkv_w, precision=HIGH)
    projected = low_back(low(raw))
    split_heads = projected.reshape(3, L, HEADS, HD)
    queries, key_rows, value_rows = (split_heads[0], split_heads[1], split_heads[2])
    product = low_back(jnp.einsum('qhe,khe->hqk', queries, key_rows, precision=HIGH))
    scores = product * HD ** (-0.5)
    key_valid = jnp.arange(L) < length
    scores = jnp.where(key_valid[None, None, :], scores, MASK_VALUE)
    probs = jax.nn.softmax(scores, axis=-1)
    context = jnp.einsum('hqk,khe->qhe', low(probs), value_rows, precision=HIGH).reshape(L, D)
    context = low_back(low(context))
    attn = low_back(jnp.dot(context, out_w, precision=HIGH))
    hidden = layer_norm(tok_float + attn, norm_w[0], norm_w[1])
    up_value = low_back(jnp.dot(low(hidden), up_w, precision=HIGH))
    inner = low(jax.nn.gelu(up_value, approximate=False))
    ffn = low_back(jnp.dot(inner, down_w, precision=HIGH))
    return layer_norm(hidden + ffn, norm_w[2], norm_w[3])

def adamw_update(gradient, weight_low, first, second, rate, fix_one, fix_two, decay):
    weight = weight_low.astype(jnp.float32)
    first_new = BETA_ONE * first + (1.0 - BETA_ONE) * gradient
    second_new = BETA_TWO * second + (1.0 - BETA_TWO) * gradient * gradient
    direction = first_new / fix_one / (jnp.sqrt(second_new / fix_two) + ADAM_EPS)
    weight_new = weight - rate * (direction + decay * weight)
    return (weight_new, first_new, second_new, weight_new.astype(jnp.bfloat16))

def reference(tokens, grad_out, token_weight, lengths, step, qkv_weight, out_weight, up_weight, down_weight, norm_params, first_qkv, first_out, first_up, first_down, first_norm, second_qkv, second_out, second_up, second_down, second_norm):
    params = tuple((w.astype(jnp.float32) for w in (qkv_weight, out_weight, up_weight, down_weight, norm_params)))
    inputs = tokens.astype(jnp.float32).reshape(SEQS, L, D)
    cotangents = (grad_out.astype(jnp.float32) * token_weight[:, None]).reshape(SEQS, L, D)

    def per_sequence(carry, item):
        tok_float, cotangent, length = item
        valid = (jnp.arange(L) < length).astype(jnp.float32)

        def closed(inner_tokens, qkv_w, out_w, up_w, down_w, norm_w):
            return forward(inner_tokens, qkv_w, out_w, up_w, down_w, norm_w, length)
        result, pull = jax.vjp(closed, tok_float, *params)
        grads = pull(cotangent * valid[:, None])
        new_carry = tuple((total + piece for total, piece in zip(carry, grads[1:])))
        return (new_carry, (result, grads[0]))
    start = tuple((jnp.zeros(p.shape, jnp.float32) for p in params))
    totals, (results, input_grads) = lax.scan(per_sequence, start, (inputs, cotangents, lengths))
    step_float = step[0].astype(jnp.float32)
    rate = PEAK_RATE * jnp.minimum(step_float / WARM_STEPS, (LAST_STEP - step_float) / (LAST_STEP - WARM_STEPS))
    fix_one = 1.0 - BETA_ONE ** step_float
    fix_two = 1.0 - BETA_TWO ** step_float
    upd_qkv = adamw_update(totals[0], qkv_weight, first_qkv, second_qkv, rate, fix_one, fix_two, DECAY_RATE)
    upd_out = adamw_update(totals[1], out_weight, first_out, second_out, rate, fix_one, fix_two, DECAY_RATE)
    upd_up = adamw_update(totals[2], up_weight, first_up, second_up, rate, fix_one, fix_two, DECAY_RATE)
    upd_down = adamw_update(totals[3], down_weight, first_down, second_down, rate, fix_one, fix_two, DECAY_RATE)
    upd_norm = adamw_update(totals[4], norm_params, first_norm, second_norm, rate, fix_one, fix_two, 0.0)
    return (results.reshape(TOKENS, D).astype(jnp.bfloat16), input_grads.reshape(TOKENS, D), upd_qkv[0], upd_qkv[1], upd_qkv[2], upd_qkv[3], upd_out[0], upd_out[1], upd_out[2], upd_out[3], upd_up[0], upd_up[1], upd_up[2], upd_up[3], upd_down[0], upd_down[1], upd_down[2], upd_down[3], upd_norm[0], upd_norm[1], upd_norm[2], upd_norm[3])
```

```python
import jax
import jax.numpy as jnp
from jax import lax
from jax.sharding import PartitionSpec as P

HD = 64
NORM_EPS = 1e-05
BETA_ONE = 0.9
BETA_TWO = 0.95
ADAM_EPS = 1e-08
DECAY_RATE = 0.01
PEAK_RATE = 0.15
WARM_STEPS = 2.0
LAST_STEP = 40.0
MASK_VALUE = -1000000000.0
BF = jnp.bfloat16
F32 = jnp.float32
CHUNK = 256


def dot_nn(a, b):
    return lax.dot_general(a, b, (((1,), (0,)), ((), ())), preferred_element_type=F32)


def dot_nt(a, b):
    return lax.dot_general(a, b, (((1,), (1,)), ((), ())), preferred_element_type=F32)


def dot_tn(a, b):
    return lax.dot_general(a, b, (((0,), (0,)), ((), ())), preferred_element_type=F32)


def norm_stats(summed):
    center = summed - jnp.mean(summed, axis=-1, keepdims=True)
    inverse = lax.rsqrt(jnp.mean(center * center, axis=-1, keepdims=True) + NORM_EPS)
    return center * inverse, inverse


def norm_pull(upstream, normed, inverse, gain):
    scaled = upstream * gain
    return inverse * (
        scaled
        - jnp.mean(scaled, axis=-1, keepdims=True)
        - normed * jnp.mean(scaled * normed, axis=-1, keepdims=True)
    )


def adamw_update(gradient, weight_low, first, second, rate, fix_one, fix_two, decay):
    weight = weight_low.astype(F32)
    first_new = BETA_ONE * first + (1.0 - BETA_ONE) * gradient
    second_new = BETA_TWO * second + (1.0 - BETA_TWO) * gradient * gradient
    direction = first_new / fix_one / (jnp.sqrt(second_new / fix_two) + ADAM_EPS)
    weight_new = weight - rate * (direction + decay * weight)
    return (weight_new, first_new, second_new, weight_new.astype(BF))


def swap(x, axis, size, bit):
    return lax.ppermute(x, axis, [(i, i ^ bit) for i in range(size)])


def solution(mesh):
    dp_size = mesh.shape["dp"]
    t_size = mesh.shape["tensor"]

    def core_swap(x):
        return swap(x, "tensor", t_size, 1)

    def far_swap(x):
        return swap(x, "tensor", t_size, 2)

    def gather_dp(x):
        rows = x.shape[0]
        if dp_size != 8 or rows % 16:
            return lax.all_gather(x, "dp", axis=0, tiled=True)
        me = lax.axis_index("dp")
        deep = [x] + [swap(x, "dp", 8, k) for k in (2, 4, 6)]
        wide = swap(jnp.stack(deep), "dp", 8, 1)
        whole = jnp.stack([deep[0], wide[0], deep[1], wide[1], deep[2], wide[2], deep[3], wide[3]])
        order = jnp.bitwise_xor(jnp.arange(8, dtype=jnp.int32), me)
        return jnp.take(whole, order, axis=0).reshape(8 * rows, x.shape[1])

    def scatter_dp(x):
        if dp_size != 8 or (x.shape[0] // 8) % 16:
            return lax.psum_scatter(x, "dp", scatter_dimension=0, tiled=True)
        me = lax.axis_index("dp")
        blocks = x.reshape(4, 2, x.shape[0] // 8, x.shape[1])
        side, level = me % 2, me // 2
        there = lax.dynamic_index_in_dim(blocks, 1 - side, 1, keepdims=False).astype(BF)
        here = lax.dynamic_index_in_dim(blocks, side, 1, keepdims=False)
        here = here + swap(there, "dp", 8, 1).astype(F32)
        total = lax.dynamic_index_in_dim(here, level, 0, keepdims=False)
        for k in (1, 2, 3):
            piece = lax.dynamic_index_in_dim(here, jnp.bitwise_xor(level, k), 0, keepdims=False)
            total = total + swap(piece.astype(BF), "dp", 8, 2 * k).astype(F32)
        return total

    def on_device(
        tokens, grad_out, token_weight, lengths, step, qkv_weight, out_weight, up_weight, down_weight,
        norm_params, first_qkv, first_out, first_up, first_down, first_norm, second_qkv, second_out,
        second_up, second_down, second_norm,
    ):
        t_index = lax.axis_index("tensor")
        low, high = t_index % 2, t_index // 2
        seq_count = lengths.shape[0]
        tok_count, width = tokens.shape
        seq_len = tok_count // seq_count
        half = seq_len // 2
        rows_d = qkv_weight.shape[1]
        local = qkv_weight.shape[2]
        heads = local // HD
        score_scale = HD ** (-0.5)

        pack_q = jnp.concatenate(
            [qkv_weight[0], qkv_weight[1], qkv_weight[2], norm_params.T, jnp.zeros((rows_d, 60), BF)], axis=1
        )
        pack_u = jnp.concatenate([up_weight, out_weight.T], axis=1)
        q_mine = gather_dp(pack_q)
        u_mine = gather_dp(pack_u)
        d_mine = gather_dp(down_weight.T)
        norm_float = q_mine[:, 3 * local : 3 * local + 4].T.astype(F32)
        q_w = [q_mine, core_swap(q_mine)]
        u_w = [u_mine, core_swap(u_mine)]
        d_w = [d_mine, core_swap(d_mine)]
        o_here = jnp.concatenate([w[:, up_weight.shape[1] :] for w in u_w], axis=1)
        o_there = far_swap(o_here)
        o_low = jnp.where(high == 0, o_here, o_there)
        o_high = jnp.where(high == 0, o_there, o_here)
        u_w = [w[:, : up_weight.shape[1]] for w in u_w]

        def pick(x):
            whole = lax.dynamic_slice_in_dim(x, low * seq_len, seq_len, 0)
            part = lax.dynamic_slice_in_dim(x, 2 * seq_len + low * half, half, 0)
            return whole, part

        tok_a, tok_c = pick(tokens)
        tok_kv = tokens[2 * seq_len :]
        len_a = lax.dynamic_index_in_dim(lengths, low, 0, keepdims=False)
        len_c = lengths[2]
        mask_a = (jnp.arange(seq_len, dtype=jnp.int32) < len_a)[None, None, :]
        mask_c = (jnp.arange(seq_len, dtype=jnp.int32) < len_c)[None, None, :]
        valid_a = mask_a[0, 0].astype(F32)
        valid_c = lax.dynamic_slice_in_dim(mask_c[0, 0].astype(F32), low * half, half, 0)

        def attend(xq, xkv, mask):
            saved, outs = [], []
            for w in q_w:
                q = dot_nn(xq, w[:, :local]).astype(BF).reshape(-1, heads, HD)
                k = dot_nn(xkv, w[:, local : 2 * local]).astype(BF).reshape(-1, heads, HD)
                v = dot_nn(xkv, w[:, 2 * local : 3 * local]).astype(BF).reshape(-1, heads, HD)
                s = jnp.einsum("qhe,khe->hqk", q, k, preferred_element_type=F32) * score_scale
                s = jnp.where(mask, s, MASK_VALUE)
                lse = jax.nn.logsumexp(s, axis=-1, keepdims=True)
                p = jnp.exp(s - lse)
                ctx = jnp.einsum("hqk,khe->qhe", p.astype(BF), v, preferred_element_type=F32)
                outs.append(ctx.astype(BF).reshape(-1, local))
                saved.append((q, k, v, lse))
            return jnp.concatenate(outs, axis=1), saved

        ctx_a, saved_a = attend(tok_a, tok_a, mask_a)
        ctx_c, saved_c = attend(tok_c, tok_kv, mask_c)
        chunks = [(tok_a[:half], ctx_a[:half]), (tok_a[half:], ctx_a[half:]), (tok_c, ctx_c)]

        def forward(tok, ctx):
            ctx_there = far_swap(ctx)
            ctx_low = jnp.where(high == 0, ctx, ctx_there)
            ctx_high = jnp.where(high == 0, ctx_there, ctx)
            attn = dot_nt(ctx_low, o_low) + dot_nt(ctx_high, o_high)
            normed, inverse = norm_stats(tok.astype(F32) + attn)
            hidden = normed * norm_float[0] + norm_float[1]
            hidden_low = hidden.astype(BF)
            inner, slope, part = [], [], 0.0
            for u, d in zip(u_w, d_w):
                upv = dot_nn(hidden_low, u)
                cdf = 0.5 * (1.0 + lax.erf(upv * (0.5**0.5)))
                pdf = jnp.exp(-0.5 * upv * upv) * 0.3989422804014327
                inner.append((upv * cdf).astype(BF))
                slope.append(cdf + upv * pdf)
                part = part + dot_nt(inner[-1], d)
            return normed, inverse, hidden, hidden_low, inner, slope, part.astype(BF)

        fwd = [forward(*c) for c in chunks]
        go_a, go_c = pick(grad_out)
        tw_a, tw_c = pick(token_weight)
        scale = jnp.concatenate([tw_a * valid_a, tw_c * valid_c])
        go = jnp.concatenate([go_a, go_c])

        def middle(i, f):
            normed, inverse, hidden, hidden_low, inner, slope, part = f
            ffn = part.astype(F32) + far_swap(part).astype(F32)
            normed2, inverse2 = norm_stats(hidden + ffn)
            out = (normed2 * norm_float[2] + norm_float[3]).astype(BF)
            up = go[i * half : (i + 1) * half].astype(F32) * scale[i * half : (i + 1) * half, None]
            grad_two = norm_pull(up, normed2, inverse2, norm_float[2])
            sums = jnp.stack([jnp.sum(up * normed2, axis=0), jnp.sum(up, axis=0)])
            ffn_low = grad_two.astype(BF)
            up_low, back = [], 0.0
            for u, d, s in zip(u_w, d_w, slope):
                up_low.append((dot_nn(ffn_low, d) * s).astype(BF))
                back = back + dot_nt(up_low[-1], u)
            return out, grad_two, ffn_low, up_low, back.astype(BF), sums

        mid = [middle(i, f) for i, f in enumerate(fwd)]
        out_mine = jnp.concatenate([m[0] for m in mid])

        def whole_rows(mine, there):
            first = [mine[:seq_len], there[:seq_len], mine[seq_len:], there[seq_len:]]
            second = [there[:seq_len], mine[:seq_len], there[seq_len:], mine[seq_len:]]
            return jnp.where(low == 0, jnp.concatenate(first), jnp.concatenate(second))

        result = whole_rows(out_mine, core_swap(out_mine))

        hidden_low = jnp.concatenate([f[3] for f in fwd])
        ffn_low = jnp.concatenate([m[2] for m in mid])
        grads_u, grads_d = [], []
        for t in range(2):
            grads_u.append(dot_tn(hidden_low, jnp.concatenate([m[3][t] for m in mid])))
            grads_d.append(dot_tn(ffn_low, jnp.concatenate([f[4][t] for f in fwd])))

        def reduce_all(mine, there):
            return scatter_dp(mine + core_swap(there.astype(BF)).astype(F32))

        shard_up = reduce_all(grads_u[0], grads_u[1])
        shard_down = reduce_all(grads_d[0], grads_d[1]).T

        def first_norm_back(f, m):
            hidden_grad = m[1] + (m[4].astype(F32) + far_swap(m[4]).astype(F32))
            grad_one = norm_pull(hidden_grad, f[0], f[1], norm_float[0])
            sums = jnp.stack([jnp.sum(hidden_grad * f[0], axis=0), jnp.sum(hidden_grad, axis=0)])
            return grad_one, grad_one.astype(BF), sums

        back = [first_norm_back(f, m) for f, m in zip(fwd, mid)]

        def attend_back(attn_low, saved, mask):
            grads = []
            for t, (q, k, v, lse) in enumerate(saved):
                ctx_grad = dot_nn(attn_low, o_here[:, t * local : (t + 1) * local]).astype(BF).reshape(-1, heads, HD)
                s = jnp.einsum("qhe,khe->hqk", q, k, preferred_element_type=F32) * score_scale
                p = jnp.exp(jnp.where(mask, s, MASK_VALUE) - lse)
                dp = jnp.einsum("qhe,khe->hqk", ctx_grad, v, preferred_element_type=F32)
                dv = jnp.einsum("hqk,qhe->khe", p.astype(BF), ctx_grad, preferred_element_type=F32)
                ds = (p * (dp - jnp.sum(dp * p, axis=-1, keepdims=True)) * score_scale).astype(BF)
                dq = jnp.einsum("hqk,khe->qhe", ds, k, preferred_element_type=F32)
                dk = jnp.einsum("hqk,qhe->khe", ds, q, preferred_element_type=F32)
                grads.append(tuple(g.reshape(-1, local) for g in (dq, dk, dv)))
            return grads

        low_a = jnp.concatenate([back[0][1], back[1][1]])
        pg_a = [jnp.concatenate(g, axis=1).astype(BF) for g in attend_back(low_a, saved_a, mask_a)]
        pg_c = []
        for (dq, dk, dv) in attend_back(back[2][1], saved_c, mask_c):
            kv = jnp.concatenate([dk, dv], axis=1)
            mine = lax.dynamic_slice_in_dim(kv, low * half, half, 0)
            there = lax.dynamic_slice_in_dim(kv, (1 - low) * half, half, 0).astype(BF)
            pg_c.append((dq, mine, there))
        got = [core_swap(pg_c[1 - t][2]) for t in range(2)]
        pg_c = [jnp.concatenate([pg_c[t][0], pg_c[t][1] + got[t].astype(F32)], axis=1).astype(BF) for t in range(2)]
        pgs = [[pg_a[t][:half] for t in range(2)], [pg_a[t][half:] for t in range(2)], pg_c]
        gi = []
        for i in range(3):
            part = sum(dot_nt(pgs[i][t], q_w[t][:, : 3 * local]) for t in range(2)).astype(BF)
            gi.append(back[i][0] + (part.astype(F32) + far_swap(part).astype(F32)))
        gi = jnp.concatenate(gi)
        input_grad = whole_rows(gi, core_swap(gi))

        tok_mine = jnp.concatenate([tok_a, tok_c])
        low_mine = jnp.concatenate([b[1] for b in back])
        ctx_mine = jnp.concatenate([ctx_a, ctx_c])
        sum_one = back[0][2] + back[1][2] + back[2][2]
        sum_two = mid[0][5] + mid[1][5] + mid[2][5]
        norm_cols = jnp.concatenate([sum_one, sum_two]).astype(BF).astype(F32).T
        packs = []
        for t in range(2):
            gq = dot_tn(tok_mine, jnp.concatenate([pgs[0][t], pgs[1][t], pgs[2][t]]))
            go_t = dot_tn(low_mine, ctx_mine[:, t * local : (t + 1) * local])
            packs.append(jnp.concatenate([gq, go_t, norm_cols], axis=1))
        shard = reduce_all(packs[0], packs[1])
        shard_qkv = jnp.stack([shard[:, c * local : (c + 1) * local] for c in range(3)])
        shard_out = shard[:, 3 * local : 4 * local].T
        shard_norm = shard[:, 4 * local : 4 * local + 4].T

        step_float = step[0].astype(F32)
        rate = PEAK_RATE * jnp.minimum(step_float / WARM_STEPS, (LAST_STEP - step_float) / (LAST_STEP - WARM_STEPS))
        fix_one = 1.0 - BETA_ONE**step_float
        fix_two = 1.0 - BETA_TWO**step_float
        res = (result, input_grad)
        for g, w, m, v, decay in (
            (shard_qkv, qkv_weight, first_qkv, second_qkv, DECAY_RATE),
            (shard_out, out_weight, first_out, second_out, DECAY_RATE),
            (shard_up, up_weight, first_up, second_up, DECAY_RATE),
            (shard_down, down_weight, first_down, second_down, DECAY_RATE),
            (shard_norm, norm_params, first_norm, second_norm, 0.0),
        ):
            res = res + adamw_update(g, w, m, v, rate, fix_one, fix_two, decay)
        return res

    rows = P("dp", None)
    qkv, col, row, norm = P(None, "dp", "tensor"), P("tensor", "dp"), P("dp", "tensor"), P(None, "dp")
    params = (qkv, col, row, col, norm)
    return jax.shard_map(
        on_device,
        mesh=mesh,
        in_specs=(rows, rows, P("dp"), P("dp"), P()) + params * 3,
        out_specs=(rows, rows) + (qkv,) * 4 + (col,) * 4 + (row,) * 4 + (col,) * 4 + (norm,) * 4,
        check_vma=False,
    )
```

```python
import jax
import jax.numpy as jnp
from jax import lax
from jax.experimental import pallas as pl
from jax.experimental.pallas import tpu as pltpu
from jax.sharding import PartitionSpec as P

HD = 64
NORM_EPS = 1e-05
MASK_VALUE = -1000000000.0
BETA_ONE = 0.9
BETA_TWO = 0.95
ADAM_EPS = 1e-08
DECAY_RATE = 0.01
PEAK_RATE = 0.15
WARM_STEPS = 2.0
LAST_STEP = 40.0
BF = jnp.bfloat16
F32 = jnp.float32
VM = pltpu.VMEM
CHUNK = 256


def dot_nn(a, b):
    return lax.dot_general(a, b, (((1,), (0,)), ((), ())), preferred_element_type=F32)


def dot_nt(a, b):
    return lax.dot_general(a, b, (((1,), (1,)), ((), ())), preferred_element_type=F32)


def dot_tn(a, b):
    return lax.dot_general(a, b, (((0,), (0,)), ((), ())), preferred_element_type=F32)


def sds(shape, dtype=BF):
    return jax.ShapeDtypeStruct(shape, dtype)


class Order:
    def __init__(self):
        self.last = None

    def call(self, body, outs, ins, info, flops, name, scratch=(), limit=20, any_out=False):
        ins = list(ins)
        specs = [pl.BlockSpec(memory_space=pltpu.SMEM)] + [pl.BlockSpec(memory_space=VM)] * len(ins)
        run = body
        if self.last is not None:
            ins.append(self.last)
            specs.append(pl.BlockSpec(memory_space=pl.ANY))
            n = len(ins)

            def run(*refs):
                body(*refs[:n], *refs[n + 1 :])

        single = not isinstance(outs, (list, tuple))
        shapes = outs if single else list(outs)
        spec = pl.BlockSpec(memory_space=pl.ANY if any_out else VM)
        res = pl.pallas_call(
            run,
            out_shape=shapes,
            in_specs=specs,
            out_specs=spec if single else [spec] * len(shapes),
            scratch_shapes=list(scratch),
            compiler_params=pltpu.CompilerParams(vmem_limit_bytes=limit * 1024 * 1024),
            cost_estimate=pl.CostEstimate(flops=1, bytes_accessed=1, transcendentals=0),
            name=name,
        )(info, *ins)
        self.last = res if single else res[-1]
        return res


def low_of(info):
    return lax.rem(info[0], 2)


def first_row(info, chunk):
    low = low_of(info)
    row = (2 * low + chunk) * CHUNK if chunk < 2 else (4 + low) * CHUNK
    return pl.multiple_of(row, CHUNK)


def norm_stats(summed):
    center = summed - jnp.mean(summed, axis=-1, keepdims=True)
    inverse = lax.rsqrt(jnp.mean(center * center, axis=-1, keepdims=True) + NORM_EPS)
    return center * inverse, inverse


def norm_pull(upstream, normed, inverse, gain):
    scaled = upstream * gain
    return inverse * (
        scaled
        - jnp.mean(scaled, axis=-1, keepdims=True)
        - normed * jnp.mean(scaled * normed, axis=-1, keepdims=True)
    )


def gelu_parts(u):
    cdf = 0.5 * (1.0 + lax.erf(u * (0.5**0.5)))
    pdf = jnp.exp(-0.5 * u * u) * 0.3989422804014327
    return u * cdf, cdf + u * pdf


def adamw_update(gradient, weight_low, first, second, rate, fix_one, fix_two, decay):
    weight = weight_low.astype(F32)
    first_new = BETA_ONE * first + (1.0 - BETA_ONE) * gradient
    second_new = BETA_TWO * second + (1.0 - BETA_TWO) * gradient * gradient
    direction = first_new / fix_one / (jnp.sqrt(second_new / fix_two) + ADAM_EPS)
    weight_new = weight - rate * (direction + decay * weight)
    return (weight_new, first_new, second_new, weight_new.astype(BF))


def pack(order, info, qkv, norm, up, out, token_weight):
    rows, local = qkv.shape[1], qkv.shape[2]
    units = up.shape[1]

    def body(sc, q, n, u, o, t, t_out, pq, pu):
        t_out[...] = t[...]
        for c in range(3):
            pq[:, c * local : (c + 1) * local] = q[c]
        pq[:, 3 * local :] = jnp.transpose(o[...].astype(F32)).astype(BF)
        pu[:, :units] = u[...]
        cols = jnp.concatenate([n[...].astype(F32), jnp.zeros((124, rows), F32)], axis=0)
        pu[:, units:] = jnp.transpose(cols).astype(BF)

    outs = [sds(token_weight.shape, F32), sds((rows, 4 * local)), sds((rows, units + 128))]
    return order.call(body, outs, [qkv, norm, up, out, token_weight], info, 0, "pack")


def place(order, info, blocks, marks, shift, name, tail=0):
    height, width = blocks[0].shape
    count = len(blocks)

    def body(sc, *refs):
        out = refs[count]
        base = lax.shift_right_logical(sc[1], shift)
        for k in range(count):
            at = pl.ds(pl.multiple_of(jnp.bitwise_xor(base, marks[k]) * height, 16), height)
            out[at, :] = refs[k][...]
            if tail:
                refs[count + 1][at, :] = refs[k][:, width - tail :]

    outs = sds((count * height, width))
    if tail:
        outs = [outs, sds((count * height, tail))]
    return order.call(body, outs, blocks, info, 0, name)


def weave(order, info, mine, there, name):
    height, width = mine.shape[0] // 4, mine.shape[1]

    def body(sc, a, b, out):
        side = lax.rem(sc[1], 2)
        for z in range(4):
            rows = slice(z * height, (z + 1) * height)
            out[pl.ds(pl.multiple_of((2 * z + side) * height, 16), height), :] = a[rows, :]
            out[pl.ds(pl.multiple_of((2 * z + 1 - side) * height, 16), height), :] = b[rows, :]

    return order.call(body, sds((8 * height, width)), [mine, there], info, 0, name)


def settle(order, info, w_up, q_own, q_oth, far_own, far_oth, units, local):
    width = w_up.shape[0]

    def body(sc, u, a, b, c, d, norms, here, low, high):
        norms[...] = jnp.transpose(u[:, units:].astype(F32))[:8, :]
        first = sc[0] < 2
        for k, (x, y) in enumerate(((a, c), (b, d))):
            lanes = slice(k * local, (k + 1) * local)
            x, y = x[:, 3 * local :], y[...]
            here[:, lanes] = x
            low[:, lanes] = jnp.where(first, x, y)
            high[:, lanes] = jnp.where(first, y, x)

    outs = [sds((8, width), F32)] + [sds((width, 2 * local))] * 3
    return order.call(body, outs, [w_up, q_own, q_oth, far_own, far_oth], info, 0, "settle")


def attend(order, info, tokens, w_own, w_oth, shared, local, name):
    heads = local // HD
    both = 2 * local
    kv_rows = 2 * CHUNK
    rows = CHUNK if shared else kv_rows
    count = rows // CHUNK

    def body(sc, x_ref, w0, w1, *refs):
        ctx_refs, (q_ref, k_ref, v_ref, lse_ref) = refs[:count], refs[count:]
        low = low_of(sc)
        length = sc[4] if shared else sc[2 + low]
        keys = lax.broadcasted_iota(jnp.int32, (1, kv_rows), 1)
        bias = jnp.where(keys < length, 0.0, MASK_VALUE)
        for t, w in enumerate((w0, w1)):
            lanes = slice(t * local, (t + 1) * local)
            if shared:
                q_ref[:, lanes] = (dot_nn(x_ref[pl.ds(first_row(sc, 2), rows), :], w[:, :local]) * 0.125).astype(BF)
                p = dot_nn(x_ref[2 * kv_rows :, :], w[:, local : 3 * local])
                k_ref[:, lanes] = p[:, :local].astype(BF)
                v_ref[:, lanes] = p[:, local:].astype(BF)
            else:
                p = dot_nn(x_ref[pl.ds(first_row(sc, 0), rows), :], w[:, : 3 * local])
                q_ref[:, lanes] = (p[:, :local] * 0.125).astype(BF)
                k_ref[:, lanes] = p[:, local : 2 * local].astype(BF)
                v_ref[:, lanes] = p[:, 2 * local :].astype(BF)
        for h in range(2 * heads):
            lanes = slice(h * HD, (h + 1) * HD)
            k, v = k_ref[:, lanes], v_ref[:, lanes]
            for r in range(count):
                at = slice(r * CHUNK, (r + 1) * CHUNK)
                s = dot_nt(q_ref[at, lanes], k) + bias
                top = jnp.max(s, axis=-1, keepdims=True)
                e = jnp.exp(s - top)
                total = jnp.sum(e, axis=-1, keepdims=True)
                ctx = dot_nn((e * (1.0 / total)).astype(BF), v)
                ctx_refs[r][:, lanes] = ctx.astype(BF)
                lse_ref[at, h : h + 1] = top + jnp.log(total)

    outs = [sds((CHUNK, both))] * count + [sds((rows, both)), sds((kv_rows, both)), sds((kv_rows, both)), sds((rows, 128), F32)]
    return order.call(body, outs, [tokens, w_own, w_oth], info, 4e9, name)


def lift(order, info, chunk, tokens, ctx, there, o_low, o_high, u0, u1, norms, units, name):
    rows, width = CHUNK, tokens.shape[1]
    both = 2 * units

    def body(sc, tok, c0, c1, ol, oh, u0, u1, nr, normed_ref, inv_ref, hl_ref, slope_ref, inner_ref):
        first = sc[0] < 2
        a, b = c0[...], c1[...]
        attn = dot_nt(jnp.where(first, a, b), ol[...]) + dot_nt(jnp.where(first, b, a), oh[...])
        normed, inverse = norm_stats(tok[pl.ds(first_row(sc, chunk), rows), :].astype(F32) + attn)
        normed_ref[...] = normed
        inv_ref[...] = jnp.broadcast_to(inverse, (rows, 128))
        hl_ref[...] = (normed * nr[0:1, :] + nr[1:2, :]).astype(BF)
        for t, u in enumerate((u0, u1)):
            for c in range(0, units, 256):
                lanes = slice(t * units + c, t * units + c + 256)
                g, s = gelu_parts(dot_nn(hl_ref[...], u[:, c : c + 256]))
                slope_ref[:, lanes] = s
                inner_ref[:, lanes] = g.astype(BF)

    outs = [sds((rows, width), F32), sds((rows, 128), F32), sds((rows, width)), sds((rows, both), F32), sds((rows, both))]
    return order.call(body, outs, [tokens, ctx, there, o_low, o_high, u0, u1, norms], info, 4e9, name)


def drop(order, info, inner, d0, d1, name):
    rows, units, width = inner.shape[0], d0.shape[1], d0.shape[0]

    def body(sc, i_ref, d0, d1, part_ref):
        part_ref[...] = (dot_nt(i_ref[:, :units], d0[...]) + dot_nt(i_ref[:, units:], d1[...])).astype(BF)

    return order.call(body, sds((rows, width)), [inner, d0, d1], info, 3e9, name)


def row_scale(sc, weights, chunk):
    low = low_of(sc)
    length = sc[2 + low] if chunk < 2 else sc[4]
    first = chunk * CHUNK if chunk < 2 else low * CHUNK
    top = lax.div(first_row(sc, chunk), 128)
    slot = lax.broadcasted_iota(jnp.int32, (128, 128), 0)
    lane = lax.broadcasted_iota(jnp.int32, (128, 128), 1)
    cols = []
    for k in range(CHUNK // 128):
        keep = (slot == lane) & (slot + (first + k * 128) < length)
        cols.append(jnp.sum(jnp.where(keep, weights[pl.ds(top + k, 1), :], 0.0), axis=-1, keepdims=True))
    return jnp.concatenate(cols, axis=0)


def turn(order, info, chunk, normed, part, there, go, scale, norms, u0, u1, d0, d1, slope, name):
    rows, width = part.shape
    units = d0.shape[1]
    both = 2 * units

    def body(sc, nm, p0, p1, g, sw, nr, u0, u1, d0, d1, sl, out_ref, two_ref, fl_ref, ul_ref, sums_ref, part_ref):
        at = pl.ds(first_row(sc, chunk), rows)
        ffn = p0[...].astype(F32) + p1[...].astype(F32)
        n2, inv2 = norm_stats((nm[...] * nr[0:1, :] + nr[1:2, :]) + ffn)
        out_ref[...] = (n2 * nr[2:3, :] + nr[3:4, :]).astype(BF)
        up = g[at, :].astype(F32) * row_scale(sc, sw, chunk)
        two = norm_pull(up, n2, inv2, nr[2:3, :])
        sums_ref[0:1, :] = jnp.sum(up * n2, axis=0, keepdims=True)
        sums_ref[1:2, :] = jnp.sum(up, axis=0, keepdims=True)
        two_ref[...] = two
        fl_ref[...] = two.astype(BF)
        acc = None
        for t, (u, d) in enumerate(((u0, d0), (u1, d1))):
            for c in range(0, units, 256):
                lanes = slice(t * units + c, t * units + c + 256)
                ul_ref[:, lanes] = (dot_nn(fl_ref[...], d[:, c : c + 256]) * sl[:, lanes]).astype(BF)
                piece = dot_nt(ul_ref[:, lanes], u[:, c : c + 256])
                acc = piece if acc is None else acc + piece
        part_ref[...] = acc.astype(BF)

    outs = [sds((rows, width)), sds((rows, width), F32), sds((rows, width)), sds((rows, both)), sds((8, width), F32), sds((rows, width))]
    return order.call(body, outs, [normed, part, there, go, scale, norms, u0, u1, d0, d1, slope], info, 6e9, name)


def grads(order, info, lefts, rights, name):
    n = len(lefts)
    width, units = lefts[0].shape[1], rights[0].shape[1] // 2

    def body(sc, *refs):
        ls, rs = refs[:n], refs[n : 2 * n]
        for t, o in ((1, refs[2 * n + 1]), (0, refs[2 * n])):
            for r in range(0, width, 256):
                acc = None
                for x, y in zip(ls, rs):
                    piece = dot_tn(x[:, r : r + 256], y[:, t * units : (t + 1) * units])
                    acc = piece if acc is None else acc + piece
                o[r : r + 256, :] = acc.astype(BF)

    return order.call(body, [sds((width, units))] * 2, list(lefts) + list(rights), info, 4e9, name)


def attend_back(order, info, chunks, norms, o_here, q, k, v, lse, weights, local, name):
    heads = local // HD
    n = len(chunks)
    rows, kv_rows = q.shape[0], k.shape[0]
    width = norms.shape[1]
    both = 2 * local
    whole = weights is not None

    def body(sc, *refs):
        ins = refs[: 5 * n]
        nr, o_ref, q_ref, k_ref, v_ref, lse_ref = refs[5 * n : 5 * n + 6]
        at = 5 * n + 6
        if whole:
            w_refs = refs[at : at + 2]
            at += 2
        one_refs, low_refs = refs[at : at + n], refs[at + n : at + 2 * n]
        at += 2 * n
        if whole:
            pg_ref, sums_ref = refs[at : at + 2]
            part_refs = refs[at + 2 : at + 2 + n]
            cg_ref = refs[at + 2 + n]
        else:
            sums_ref, dq_ref, mine_ref, there_ref, cg_ref, kv_ref = refs[at:]
        low = low_of(sc)
        gain = shift = None
        for i in range(n):
            two, p0, p1, nm, inv = ins[5 * i : 5 * i + 5]
            normed = nm[...]
            grad = two[...] + (p0[...].astype(F32) + p1[...].astype(F32))
            s0 = jnp.sum(grad * normed, axis=0, keepdims=True)
            s1 = jnp.sum(grad, axis=0, keepdims=True)
            gain, shift = (s0, s1) if i == 0 else (gain + s0, shift + s1)
            one = norm_pull(grad, normed, inv[:, :1], nr[0:1, :])
            one_refs[i][...] = one
            low_refs[i][...] = one.astype(BF)
            cg_ref[i * CHUNK : (i + 1) * CHUNK, :] = dot_nn(low_refs[i][...], o_ref[...]).astype(BF)
        sums_ref[0:1, :] = gain
        sums_ref[1:2, :] = shift
        keys = lax.broadcasted_iota(jnp.int32, (kv_rows, 1), 0)
        length = sc[2 + low] if whole else sc[4]
        bias = jnp.where(keys < length, 0.0, MASK_VALUE)
        lse_t = jnp.transpose(lse_ref[...])
        for h in range(2 * heads):
            lanes = slice(h * HD, (h + 1) * HD)
            t, j = divmod(h, heads)
            qh, kh, vh, cg = q_ref[:, lanes], k_ref[:, lanes], v_ref[:, lanes], cg_ref[:, lanes]
            p = jnp.exp(dot_nt(kh, qh) + bias - lse_t[h : h + 1, :])
            dp = dot_nt(vh, cg)
            ds = (p * (dp - jnp.sum(dp * p, axis=0, keepdims=True))).astype(BF)
            dv = dot_nn(p.astype(BF), cg)
            dk = dot_nn(ds, qh)
            dq = dot_tn(ds, kh) * 0.125
            if whole:
                base = t * 3 * local + j * HD
                pg_ref[:, base : base + HD] = dq.astype(BF)
                pg_ref[:, base + local : base + local + HD] = dk.astype(BF)
                pg_ref[:, base + 2 * local : base + 2 * local + HD] = dv.astype(BF)
            else:
                base = t * 2 * local + j * HD
                dq_ref[:, lanes] = dq.astype(BF)
                kv_ref[:, base : base + HD] = dk
                kv_ref[:, base + local : base + local + HD] = dv
        if whole:
            for i in range(n):
                r = slice(i * CHUNK, (i + 1) * CHUNK)
                acc = dot_nt(pg_ref[r, : 3 * local], w_refs[0][:, : 3 * local])
                acc = acc + dot_nt(pg_ref[r, 3 * local :], w_refs[1][:, : 3 * local])
                part_refs[i][...] = acc.astype(BF)
        else:
            mine_ref[...] = kv_ref[pl.ds(pl.multiple_of(low * CHUNK, CHUNK), CHUNK), :]
            there_ref[...] = kv_ref[pl.ds(pl.multiple_of((1 - low) * CHUNK, CHUNK), CHUNK), :].astype(BF)

    outs = [sds((CHUNK, width), F32)] * n + [sds((CHUNK, width))] * n
    scratch = [VM((rows, both), BF)]
    if whole:
        outs += [sds((rows, 6 * local)), sds((8, width), F32)] + [sds((CHUNK, width))] * n
    else:
        outs += [sds((8, width), F32), sds((rows, both)), sds((CHUNK, 2 * both), F32), sds((CHUNK, 2 * both))]
        scratch += [VM((kv_rows, 2 * both), F32)]
    ins = [x for c in chunks for x in c] + [norms, o_here, q, k, v, lse] + (list(weights) if whole else [])
    return order.call(body, outs, ins, info, 8e9, name, scratch=scratch)


def project_back(order, info, dq, mine, there, w_own, w_oth, local, name):
    rows, width = dq.shape[0], w_own.shape[0]

    def body(sc, dq_ref, a, b, w0, w1, pg_ref, part_ref):
        acc = None
        for t, w in enumerate((w0, w1)):
            base = t * 3 * local
            pg_ref[:, base : base + local] = dq_ref[:, t * local : (t + 1) * local]
            here = a[:, t * 2 * local : (t + 1) * 2 * local]
            got = b[:, (1 - t) * 2 * local : (2 - t) * 2 * local]
            pg_ref[:, base + local : base + 3 * local] = (here + got.astype(F32)).astype(BF)
            piece = dot_nt(pg_ref[:, base : base + 3 * local], w[:, : 3 * local])
            acc = piece if acc is None else acc + piece
        part_ref[...] = acc.astype(BF)

    return order.call(body, [sds((rows, 6 * local)), sds((rows, width))], [dq, mine, there, w_own, w_oth], info, 1e9, name)


def grads_attn(order, info, tokens, pg_a, pg_c, lows, ctxs, sums_one, sums_two, local):
    width = tokens.shape[1]
    n, s1, s2 = len(lows), len(sums_one), len(sums_two)

    def body(sc, *refs):
        tok, pa, pc = refs[:3]
        ls, cs = refs[3 : 3 + n], refs[3 + n : 3 + 2 * n]
        ones = refs[3 + 2 * n : 3 + 2 * n + s1]
        twos = refs[3 + 2 * n + s1 : 3 + 2 * n + s1 + s2]
        first_own, first_oth, second_own, second_oth = refs[3 + 2 * n + s1 + s2 :]
        one = sum(x[0:2, :] for x in ones)
        two = sum(x[0:2, :] for x in twos)
        stack = jnp.concatenate([one, two, jnp.zeros((124, width), F32)], axis=0)
        cols = jnp.transpose(stack).astype(BF)
        at_a, at_c = pl.ds(first_row(sc, 0), 2 * CHUNK), pl.ds(first_row(sc, 2), CHUNK)

        def outer(rr, lanes):
            return dot_tn(tok[at_a, rr], pa[:, lanes]) + dot_tn(tok[at_c, rr], pc[:, lanes])

        for t, o in ((1, first_oth), (0, first_own)):
            for r in range(0, width, 256):
                rr = slice(r, r + 256)
                o[rr, :] = outer(rr, slice(t * 3 * local, (t * 3 + 2) * local)).astype(BF)
        for t, o in ((1, second_oth), (0, second_own)):
            for r in range(0, width, 256):
                rr = slice(r, r + 256)
                o[rr, :local] = outer(rr, slice((t * 3 + 2) * local, (t * 3 + 3) * local)).astype(BF)
                acc = None
                for x, y in zip(ls, cs):
                    piece = dot_tn(x[:, rr], y[:, t * local : (t + 1) * local])
                    acc = piece if acc is None else acc + piece
                o[rr, local : 2 * local] = acc.astype(BF)
                o[rr, 2 * local :] = cols[rr, :]

    ins = [tokens, pg_a, pg_c] + list(lows) + list(ctxs) + list(sums_one) + list(sums_two)
    outs = [sds((width, 2 * local))] * 2 + [sds((width, 2 * local + 128))] * 2
    return order.call(body, outs, ins, info, 5e9, "grads_attn")


def fold_side(order, info, mine, there, name):
    height, width = mine.shape[0] // 8, mine.shape[1]

    def body(sc, a, b, away, here):
        side = lax.rem(sc[1], 2)
        for z in range(4):
            rows = slice(z * height, (z + 1) * height)
            for out, s in ((away, 1 - side), (here, side)):
                at = pl.ds(pl.multiple_of((2 * z + s) * height, 16), height)
                out[rows, :] = (a[at, :].astype(F32) + b[at, :].astype(F32)).astype(BF)

    return order.call(body, [sds((4 * height, width))] * 2, [mine, there], info, 0, name)


def fold_level(order, info, mine, there, name):
    height, width = mine.shape[0] // 4, mine.shape[1]

    def body(sc, a, b, *outs):
        level = lax.shift_right_logical(sc[1], 1)
        for k in range(4):
            at = pl.ds(pl.multiple_of(jnp.bitwise_xor(level, k) * height, 16), height)
            outs[k][...] = (a[at, :].astype(F32) + b[at, :].astype(F32)).astype(outs[k].dtype)

    shapes = [sds((height, width), F32)] + [sds((height, width))] * 3
    return order.call(body, shapes, [mine, there], info, 0, name)


def add_rows(order, info, one, part, there, name):
    def body(sc, a, b, c, o):
        o[...] = a[...] + (b[...].astype(F32) + c[...].astype(F32))

    return order.call(body, sds(one.shape, F32), [one, part, there], info, 0, name)


def lay_rows(order, info, mine, there, name):
    n = len(mine)
    step, width = mine[0].shape

    def body(sc, *refs):
        out, sems = refs[2 * n], refs[2 * n + 1]
        copies = []
        for g in range(2):
            half = low_of(sc) if g == 0 else 1 - low_of(sc)
            for i in range(n):
                row = (2 * half + i) * step if i < 2 else (4 + half) * step
                at = pl.ds(pl.multiple_of(row, step), step)
                copies.append(pltpu.make_async_copy(refs[g * n + i], out.at[at, :], sems.at[g * n + i]))
                copies[-1].start()
        for c in copies:
            c.wait()

    outs = sds((2 * n * step, width), mine[0].dtype)
    return order.call(body, outs, list(mine) + list(there), info, 0, name, scratch=[pltpu.SemaphoreType.DMA((2 * n,))], any_out=True)


def update(order, rates, groups, items, name):
    arrays = [x for it in items for x in it[:3]]
    shapes = [sds(it[0].shape, d) for it in items for d in (F32, F32, F32, BF)]
    pieces = [p for g in groups for p in g]

    def body(sc, *refs):
        ins = refs[len(pieces) : len(pieces) + len(arrays)]
        outs = refs[len(pieces) + len(arrays) :]
        rate, fix_one, fix_two = sc[0], sc[1], sc[2]
        for n, it in enumerate(items):
            w, m, v = ins[3 * n : 3 * n + 3]
            for index, group, first, count, turned in it[4]:
                a, b, c, d = (r.at[:, first : first + count] for r in refs[4 * group : 4 * group + 4])
                g = (a[...] + b[...].astype(F32)) + (c[...].astype(F32) + d[...].astype(F32))
                if turned:
                    g = jnp.transpose(g)[: w.shape[0], :]
                res = adamw_update(g, w[index], m[index], v[index], rate, fix_one, fix_two, it[3])
                for r, o in zip(res, outs[4 * n : 4 * n + 4]):
                    o[index] = r

    return order.call(body, shapes, pieces + arrays, rates, 0, name)


def swap(x, axis, size, bit):
    return lax.ppermute(x, axis, [(i, i ^ bit) for i in range(size)])


def after(x, *others):
    return lax.optimization_barrier((x,) + others)[0]


def solution(mesh):
    dp_size = mesh.shape["dp"]
    t_size = mesh.shape["tensor"]

    def core_swap(x):
        return swap(x, "tensor", t_size, 1)

    def far_swap(x):
        return swap(x, "tensor", t_size, 2)

    def on_device(
        tokens, grad_out, token_weight, lengths, step, qkv_weight, out_weight, up_weight, down_weight,
        norm_params, first_qkv, first_out, first_up, first_down, first_norm, second_qkv, second_out,
        second_up, second_down, second_norm,
    ):
        order = Order()
        rows_d, local = qkv_weight.shape[1], qkv_weight.shape[2]
        units = up_weight.shape[1]
        tok_count = tokens.shape[0]
        direct = dp_size == 8 and rows_d % 16 == 0
        places = jnp.stack([lax.axis_index("tensor"), lax.axis_index("dp")]).astype(jnp.int32)
        info = jnp.concatenate([places, lengths])
        scale = token_weight.reshape(tok_count // 128, 128)
        step_float = step[0].astype(F32)
        rate = PEAK_RATE * jnp.minimum(step_float / WARM_STEPS, (LAST_STEP - step_float) / (LAST_STEP - WARM_STEPS))
        fix_one = 1.0 - BETA_ONE**step_float
        fix_two = 1.0 - BETA_TWO**step_float
        rates = jnp.stack([rate, fix_one, fix_two])
        down_t = down_weight.T

        if direct:
            scale, pack_q, pack_u = pack(order, info, qkv_weight, norm_params, up_weight, out_weight, scale)
            near = [pack_q] + [swap(pack_q, "dp", 8, k) for k in (2, 4, 6)]
            far = [swap(x, "dp", 8, 1) for x in near]
            pack_u = after(pack_u, near[1])
            z_u = [pack_u] + [swap(pack_u, "dp", 8, 2 * k) for k in (1, 2, 3)]
            q_own, o_own = place(order, info, near + far, (0, 2, 4, 6, 1, 3, 5, 7), 0, "place_q", tail=local)
            q_oth, o_far = core_swap(q_own), far_swap(o_own)
            down_t_late = after(down_t, near[2])
            z_d = [down_t_late] + [swap(down_t_late, "dp", 8, 2 * k) for k in (1, 2, 3)]
        else:
            pad = jnp.zeros((rows_d, 124), BF)
            pack_q = jnp.concatenate([qkv_weight[0], qkv_weight[1], qkv_weight[2], out_weight.T], axis=1)
            pack_u = jnp.concatenate([up_weight, norm_params.T, pad], axis=1)
            q_own, u_own, d_own = (lax.all_gather(x, "dp", axis=0, tiled=True) for x in (pack_q, pack_u, down_t))
            o_own = q_own[:, 3 * local :]
            q_oth, o_far = core_swap(q_own), far_swap(o_own)

        ctx_c, q_c, k_c, v_c, lse_c = attend(order, info, tokens, q_own, q_oth, True, local, "attend_c")
        if direct:
            zs_u = place(order, info, z_u, (0, 1, 2, 3), 1, "place_u")
        *ctx_a, q_a, k_a, v_a, lse_a = attend(order, info, tokens, q_own, q_oth, False, local, "attend_a")
        ctxs = ctx_a + [ctx_c]
        theres = [far_swap(c) for c in ctxs]
        if direct:
            zs_d = place(order, info, z_d, (0, 1, 2, 3), 1, "place_d")
            x_d = swap(zs_d, "dp", 8, 1)
            u_own = weave(order, info, zs_u, swap(zs_u, "dp", 8, 1), "weave_u")
        u_oth = core_swap(u_own)
        norms, o_here, o_low, o_high = settle(order, info, u_own, q_own, q_oth, o_far, core_swap(o_far), units, local)
        normed, inverse, hidden, slope, inner = zip(*[
            lift(order, info, i, tokens, ctxs[i], theres[i], o_low, o_high, u_own, u_oth, norms, units, f"lift_{i}") for i in range(3)
        ])
        if direct:
            d_own = weave(order, info, zs_d, x_d, "weave_d")
        d_oth = core_swap(d_own)
        parts = [drop(order, info, inner[i], d_own, d_oth, f"drop_{i}") for i in range(3)]
        results, twos, ffn, up, sums_two, backs = zip(*[
            turn(order, info, i, normed[i], parts[i], far_swap(parts[i]), grad_out, scale, norms, u_own, u_oth, d_own, d_oth,
                 slope[i], f"turn_{i}")
            for i in range(3)
        ])
        res_there = [core_swap(x) for x in results]
        theres = [far_swap(b) for b in backs]
        down_own, down_oth = grads(order, info, ffn, inner, "grads_d")
        down_got = core_swap(down_oth)
        up_own, up_oth = grads(order, info, hidden, up, "grads_u")
        up_got = core_swap(up_oth)
        if direct:
            away_d, here_d = fold_side(order, info, down_own, down_got, "side_d")
            got_d = swap(away_d, "dp", 8, 1)
        pieces = [(twos[i], backs[i], theres[i], normed[i], inverse[i]) for i in range(3)]
        ones0, ones1, low0, low1, pg_a, sums_a, in0, in1 = attend_back(
            order, info, pieces[:2], norms, o_here, q_a, k_a, v_a, lse_a, (q_own, q_oth), local, "back_a")
        in_there = [far_swap(in0), far_swap(in1)]
        if direct:
            away_u, here_u = fold_side(order, info, up_own, up_got, "side_u")
            got_u = swap(away_u, "dp", 8, 1)
        ones2, low2, sums_c, dq_c, kv_mine, kv_there = attend_back(
            order, info, pieces[2:], norms, o_here, q_c, k_c, v_c, lse_c, None, local, "back_c")
        kv_got = core_swap(kv_there)

        def spread(own, *sent):
            return [own] + [swap(p, "dp", 8, 2 * k) for k, p in zip((1, 2, 3), sent)]

        if direct:
            sum_d = spread(*fold_level(order, info, here_d, got_d, "level_d"))
        pg_c, in2 = project_back(order, info, dq_c, kv_mine, kv_got, q_own, q_oth, local, "project_c")
        in_there.append(far_swap(in2))
        qk_own, qk_oth, vo_own, vo_oth = grads_attn(
            order, info, tokens, pg_a, pg_c, (low0, low1, low2), ctxs, (sums_a, sums_c), sums_two, local)
        qk_got, vo_got = core_swap(qk_oth), core_swap(vo_oth)
        if direct:
            away_1, here_1 = fold_side(order, info, qk_own, qk_got, "side_qk")
            got_1 = swap(away_1, "dp", 8, 1)
            away_2, here_2 = fold_side(order, info, vo_own, vo_got, "side_vo")
            got_2 = swap(away_2, "dp", 8, 1)
            sum_u = spread(*fold_level(order, info, here_u, got_u, "level_u"))
        gi = [add_rows(order, info, o, p, t, f"add_{i}") for i, (o, p, t) in enumerate(zip((ones0, ones1, ones2), (in0, in1, in2), in_there))]
        if direct:
            sum_1 = spread(*fold_level(order, info, here_1, got_1, "level_qk"))
        result = lay_rows(order, info, results, res_there, "lay_out")
        everything = slice(None)
        if direct:
            n_down = update(order, rates, [sum_d], [
                (down_t, first_down.T, second_down.T, DECAY_RATE, [(everything, 0, 0, units, False)])], "update_d")
            sum_2 = spread(*fold_level(order, info, here_2, got_2, "level_vo"))
        input_grad = lay_rows(order, info, gi, [core_swap(x) for x in gi], "lay_grad")
        if direct:
            n_up = update(order, rates, [sum_u], [
                (up_weight, first_up, second_up, DECAY_RATE, [(everything, 0, 0, units, False)])], "update_u")
            res = update(order, rates, [sum_1, sum_2], [
                (qkv_weight, first_qkv, second_qkv, DECAY_RATE,
                 [(0, 0, 0, local, False), (1, 0, local, local, False), (2, 1, 0, local, False)]),
                (out_weight, first_out, second_out, DECAY_RATE, [(everything, 1, local, local, True)]),
                (norm_params, first_norm, second_norm, 0.0, [(everything, 1, 2 * local, 128, True)]),
            ], "update_a")
            n_down = [x.T for x in n_down]
            n_qkv, n_out, n_norm = res[:4], res[4:8], res[8:]
        else:
            def total(mine, got):
                return lax.psum_scatter(mine.astype(F32) + got.astype(F32), "dp", scatter_dimension=0, tiled=True)

            su, sd, s1, s2 = total(up_own, up_got), total(down_own, down_got), total(qk_own, qk_got), total(vo_own, vo_got)
            rest = (rate, fix_one, fix_two)
            n_up = adamw_update(su, up_weight, first_up, second_up, *rest, DECAY_RATE)
            n_down = adamw_update(sd.T, down_weight, first_down, second_down, *rest, DECAY_RATE)
            sq = jnp.stack([s1[:, :local], s1[:, local:], s2[:, :local]])
            n_qkv = adamw_update(sq, qkv_weight, first_qkv, second_qkv, *rest, DECAY_RATE)
            n_out = adamw_update(s2[:, local : 2 * local].T, out_weight, first_out, second_out, *rest, DECAY_RATE)
            n_norm = adamw_update(s2[:, 2 * local : 2 * local + 4].T, norm_params, first_norm, second_norm, *rest, 0.0)
        return (result, input_grad, *n_qkv, *n_out, *n_up, *n_down, *n_norm)

    rows = P("dp", None)
    qkv, col, row, norm = P(None, "dp", "tensor"), P("tensor", "dp"), P("dp", "tensor"), P(None, "dp")
    weights = (qkv, col, row, col, norm)
    return jax.shard_map(
        on_device,
        mesh=mesh,
        in_specs=(rows, rows, P("dp"), P("dp"), P()) + weights * 3,
        out_specs=(rows, rows) + (qkv,) * 4 + (col,) * 4 + (row,) * 4 + (col,) * 4 + (norm,) * 4,
        check_vma=False,
    )
```

```python
import jax
import jax.numpy as jnp
from jax import lax
from jax.experimental import pallas as pl
from jax.experimental.pallas import tpu as pltpu
from jax.sharding import PartitionSpec as P

HD = 64
NORM_EPS = 1e-05
MASK_VALUE = -1000000000.0
BETA_ONE = 0.9
BETA_TWO = 0.95
ADAM_EPS = 1e-08
DECAY_RATE = 0.01
PEAK_RATE = 0.15
WARM_STEPS = 2.0
LAST_STEP = 40.0
BF = jnp.bfloat16
F32 = jnp.float32
VM = pltpu.VMEM
CHUNK = 256


def dot_nn(a, b):
    return lax.dot_general(a, b, (((1,), (0,)), ((), ())), preferred_element_type=F32)


def dot_nt(a, b):
    return lax.dot_general(a, b, (((1,), (1,)), ((), ())), preferred_element_type=F32)


def dot_tn(a, b):
    return lax.dot_general(a, b, (((0,), (0,)), ((), ())), preferred_element_type=F32)


def sds(shape, dtype=BF):
    return jax.ShapeDtypeStruct(shape, dtype)


class Order:
    def __init__(self):
        self.last = None

    def call(self, body, outs, ins, info, name, scratch=(), limit=20, raw_in=False, raw_out=False, deps=(), warm=(), free=False):
        ins = list(ins)
        n = len(ins) + 1
        specs = [pl.BlockSpec(memory_space=pltpu.SMEM)]
        specs += [pl.BlockSpec(memory_space=pltpu.HBM if raw_in else VM)] * len(ins)
        extra = list(warm) + list(deps) + ([] if self.last is None or free else [self.last])
        specs += [pl.BlockSpec(memory_space=VM)] * len(warm)
        specs += [pl.BlockSpec(memory_space=pl.ANY)] * (len(extra) - len(warm))

        def run(*refs):
            body(*refs[:n], *refs[n + len(extra) :])

        single = not isinstance(outs, (list, tuple))
        shapes = outs if single else list(outs)
        spec = pl.BlockSpec(memory_space=pltpu.HBM if raw_out else VM)
        res = pl.pallas_call(
            run,
            out_shape=shapes,
            in_specs=specs,
            out_specs=spec if single else [spec] * len(shapes),
            scratch_shapes=list(scratch),
            compiler_params=pltpu.CompilerParams(vmem_limit_bytes=limit * 1024 * 1024),
            cost_estimate=pl.CostEstimate(flops=1, bytes_accessed=1, transcendentals=0),
            name=name,
        )(info, *ins, *extra)
        if not free:
            self.last = res if single else res[-1]
        return res


def low_of(info):
    return lax.rem(info[0], 2)


def rows_of(kind):
    return 2 * CHUNK if kind == "a" else CHUNK


def first_row(info, kind, other=False):
    low = 1 - low_of(info) if other else low_of(info)
    return pl.multiple_of(2 * low * CHUNK if kind == "a" else (4 + low) * CHUNK, CHUNK)


def used_of(info, kind):
    return info[2 + low_of(info)] if kind == "a" else info[4]


def by_chunk(rows, step):
    if rows == CHUNK:
        step(0)
    else:

        @pl.loop(0, rows // CHUNK)
        def _(r):
            step(pl.multiple_of(r * CHUNK, CHUNK))


def norm_stats(summed):
    center = summed - jnp.mean(summed, axis=-1, keepdims=True)
    inverse = lax.rsqrt(jnp.mean(center * center, axis=-1, keepdims=True) + NORM_EPS)
    return center * inverse, inverse


def norm_pull(upstream, normed, inverse, gain):
    scaled = upstream * gain
    return inverse * (
        scaled
        - jnp.mean(scaled, axis=-1, keepdims=True)
        - normed * jnp.mean(scaled * normed, axis=-1, keepdims=True)
    )


def gelu_parts(u):
    cdf = 0.5 * (1.0 + lax.erf(u * (0.5**0.5)))
    pdf = jnp.exp(-0.5 * u * u) * 0.3989422804014327
    return u * cdf, cdf + u * pdf


def adamw_update(gradient, weight_low, first, second, rate, fix_one, fix_two, decay):
    weight = weight_low.astype(F32)
    first_new = BETA_ONE * first + (1.0 - BETA_ONE) * gradient
    second_new = BETA_TWO * second + (1.0 - BETA_TWO) * gradient * gradient
    direction = first_new / fix_one / (jnp.sqrt(second_new / fix_two) + ADAM_EPS)
    weight_new = weight - rate * (direction + decay * weight)
    return (weight_new, first_new, second_new, weight_new.astype(BF))


def pack(order, info, qkv, out):
    rows, local = qkv.shape[1], qkv.shape[2]

    def body(sc, *refs):
        given, (pq, po), (q, o, sems) = refs[:2], refs[2:4], refs[4:]
        copies = [pltpu.make_async_copy(a, b, sems.at[k]) for k, (a, b) in enumerate(zip(given, (q, o)))]
        for c in copies:
            c.start()
        for c in copies:
            c.wait()
        for c in range(3):
            pq[:, c * local : (c + 1) * local] = q[c]
        turned = jnp.transpose(o[...].astype(F32)).astype(BF)
        pq[:, 3 * local :] = turned
        po[...] = turned

    ins = [qkv, out]
    scratch = [VM(x.shape, x.dtype) for x in ins] + [pltpu.SemaphoreType.DMA((2,))]
    return order.call(body, [sds((rows, 4 * local)), sds((rows, local))], ins, info, "pack", scratch=scratch, raw_in=True)


def pack_more(order, info, up, out_there, norm, **kw):
    rows, units, local = up.shape[0], up.shape[1], out_there.shape[1]
    pad = -(units + local) % 128

    def body(sc, u, o, n, p):
        p[:, :units] = u[...]
        p[:, units : units + local] = o[...]
        cols = jnp.concatenate([n[...].astype(F32), jnp.zeros((124, rows), F32)], axis=0)
        p[:, units + local :] = jnp.transpose(cols)[:, :pad].astype(BF)

    return order.call(body, sds((rows, units + local + pad)), [up, out_there, norm], info, "pack_more", **kw)


def stack(order, info, blocks, name, **kw):
    height, width = blocks[0].shape
    count = len(blocks)

    def body(sc, *refs):
        for k in range(count):
            refs[count][k * height : (k + 1) * height, :] = refs[k][...]

    return order.call(body, sds((count * height, width)), blocks, info, name, **kw)


def place(order, info, blocks, marks, name, **kw):
    count = len(marks)
    height, width = sum(b.shape[0] for b in blocks) // count, blocks[0].shape[1]
    n = len(blocks)

    def body(sc, *refs):
        k = 0
        for ref in refs[:n]:
            for r in range(0, ref.shape[0], height):
                at = pl.ds(pl.multiple_of(jnp.bitwise_xor(sc[1], marks[k]) * height, 16), height)
                refs[n][at, :] = ref[r : r + height, :]
                k += 1

    return order.call(body, sds((count * height, width)), blocks, info, name, **kw)


def settle(order, info, u_own, u_oth, q_own, q_oth, units, local, **kw):
    width = u_own.shape[0]
    top = (units + local) // 128 * 128
    row = units + local - top

    def body(sc, a, b, c, d, norms, here, low, high):
        norms[...] = jnp.transpose(a[:, top:].astype(F32))[row : row + 8, :]
        first = sc[0] < 2
        for k, (x, y) in enumerate(((c, a), (d, b))):
            lanes = slice(k * local, (k + 1) * local)
            x, y = x[:, 3 * local :], y[:, units : units + local]
            here[:, lanes] = x
            low[:, lanes] = jnp.where(first, x, y)
            high[:, lanes] = jnp.where(first, y, x)

    outs = [sds((8, width), F32)] + [sds((width, 2 * local))] * 3
    return order.call(body, outs, [u_own, u_oth, q_own, q_oth], info, "settle", **kw)


def attend(order, info, kind, tokens, w_own, w_oth, local, name, **kw):
    heads = local // HD
    both = 2 * local
    kv_rows = 2 * CHUNK
    rows = rows_of(kind)

    def body(sc, x_ref, w0, w1, q_ref, k_ref, v_ref, lse_ref, ctx_ref, part_ref):
        keys = lax.broadcasted_iota(jnp.int32, (1, kv_rows), 1)
        bias = jnp.where(keys < used_of(sc, kind), 0.0, MASK_VALUE)
        for t, w in enumerate((w0, w1)):
            if kind == "c":
                q_ref[t] = (dot_nn(x_ref[pl.ds(first_row(sc, kind), rows), :], w[:, :local]) * 0.125).astype(BF)
                p = dot_nn(x_ref[2 * kv_rows :, :], w[:, local : 3 * local])
                k_ref[t] = p[:, :local].astype(BF)
                v_ref[t] = p[:, local:].astype(BF)
            else:
                p = dot_nn(x_ref[pl.ds(first_row(sc, kind), rows), :], w[:, : 3 * local])
                q_ref[t] = (p[:, :local] * 0.125).astype(BF)
                k_ref[t] = p[:, local : 2 * local].astype(BF)
                v_ref[t] = p[:, 2 * local :].astype(BF)

        @pl.loop(0, 2 * (rows // CHUNK))
        def _(i):
            t = lax.rem(i, 2)
            at = pl.ds(pl.multiple_of(lax.div(i, 2) * CHUNK, CHUNK), CHUNK)
            for h in range(heads):
                lanes = slice(h * HD, (h + 1) * HD)
                s = dot_nt(q_ref[t, at, lanes], k_ref[t, :, lanes]) + bias
                top = jnp.max(s, axis=-1, keepdims=True)
                e = jnp.exp(s - top)
                total = jnp.sum(e, axis=-1, keepdims=True)
                part_ref[t, at, lanes] = dot_nn((e * (1.0 / total)).astype(BF), v_ref[t, :, lanes]).astype(BF)
                lse_ref[t, at, h : h + 1] = top + jnp.log(total)

        for t in range(2):
            ctx_ref[:, t * local : (t + 1) * local] = part_ref[t]

    outs = [sds((2, n, local)) for n in (rows, kv_rows, kv_rows)] + [sds((2, rows, 128), F32), sds((rows, both))]
    return order.call(body, outs, [tokens, w_own, w_oth], info, name, scratch=[VM((2, rows, local), BF)], **kw)


def lift(order, info, kind, tokens, ctx, there, o_low, o_high, u0, u1, norms, units, name, **kw):
    rows, width = rows_of(kind), tokens.shape[1]
    both = 2 * units

    def body(sc, tok, c0, c1, ol, oh, u0, u1, nr, normed_ref, inv_ref, slope_ref, own_ref, send_ref):
        first = sc[0] < 2
        top = first_row(sc, kind)

        def step(r):
            at = pl.ds(r, CHUNK)
            a, b = c0[at, :], c1[at, :]
            attn = dot_nt(jnp.where(first, a, b), ol[...]) + dot_nt(jnp.where(first, b, a), oh[...])
            normed, inverse = norm_stats(tok[pl.ds(pl.multiple_of(top + r, CHUNK), CHUNK), :].astype(F32) + attn)
            normed_ref[at, :] = normed
            inv_ref[at, :] = jnp.broadcast_to(inverse, (CHUNK, 128))
            send_ref[at, :width] = (normed * nr[0:1, :] + nr[1:2, :]).astype(BF)
            for t, u in enumerate((u0, u1)):
                for c in range(0, units, 256):
                    g, s = gelu_parts(dot_nn(send_ref[at, :width], u[:, c : c + 256]))
                    slope_ref[at, t * units + c : t * units + c + 256] = s
                    if t == 0:
                        own_ref[at, c : c + 256] = g.astype(BF)
                    else:
                        send_ref[at, width + c : width + c + 256] = g.astype(BF)

        by_chunk(rows, step)

    outs = [sds((rows, width), F32), sds((rows, 128), F32), sds((rows, both), F32), sds((rows, units)), sds((rows, width + units))]
    return order.call(body, outs, [tokens, ctx, there, o_low, o_high, u0, u1, norms], info, name, **kw)


def drop(order, info, own, sent, d0, d1, name, **kw):
    rows, width = own.shape[0], d0.shape[0]

    def body(sc, own_ref, sent_ref, d0, d1, *parts):
        for k, part_ref in enumerate(parts):
            at = slice(k * CHUNK, (k + 1) * CHUNK)
            part_ref[...] = (dot_nt(own_ref[at, :], d0[...]) + dot_nt(sent_ref[at, width:], d1[...])).astype(BF)

    return order.call(body, [sds((CHUNK, width))] * (rows // CHUNK), [own, sent, d0, d1], info, name, **kw)


def row_scale(info, weights, kind, r):
    length = used_of(info, kind)
    first = r if kind == "a" else low_of(info) * CHUNK
    top = lax.div(first_row(info, kind) + r, 128)
    slot = lax.broadcasted_iota(jnp.int32, (128, 128), 0)
    lane = lax.broadcasted_iota(jnp.int32, (128, 128), 1)
    cols = []
    for k in range(CHUNK // 128):
        keep = (slot == lane) & (slot + (first + k * 128) < length)
        cols.append(jnp.sum(jnp.where(keep, weights[pl.ds(top + k, 1), :], 0.0), axis=-1, keepdims=True))
    return jnp.concatenate(cols, axis=0)


def turn(order, info, kind, normed, part, there, go, weights, norms, u0, u1, d0, d1, slope, name, below=None, **kw):
    rows, width = normed.shape
    n = len(part)
    skip = 0 if below is None else below.shape[0]
    units = d0.shape[1]
    both = 2 * units

    def body(sc, nm, g, sw, nr, u0, u1, d0, d1, sl, *refs):
        parts, refs = refs[: 2 * n], refs[2 * n :]
        if n > 1:
            p0, p1 = refs[-2:]
            refs = refs[:-2]
            for k in range(n):
                p0[k * CHUNK : (k + 1) * CHUNK, :] = parts[k][...]
                p1[k * CHUNK : (k + 1) * CHUNK, :] = parts[n + k][...]
        else:
            p0, p1 = parts
        out_ref, two_ref, own_ref, send_ref, sums_ref, part_ref = refs[-6:]
        if skip:
            out_ref[rows:, :] = refs[0][...]
        sums_ref[...] = jnp.zeros((8, width), F32)
        top = first_row(sc, kind)

        def step(r):
            at = pl.ds(r, CHUNK)
            ffn = p0[at, :].astype(F32) + p1[at, :].astype(F32)
            n2, inv2 = norm_stats((nm[at, :] * nr[0:1, :] + nr[1:2, :]) + ffn)
            out_ref[at, :] = (n2 * nr[2:3, :] + nr[3:4, :]).astype(BF)
            up = g[pl.ds(pl.multiple_of(top + r, CHUNK), CHUNK), :].astype(F32) * row_scale(sc, sw, kind, r)
            two = norm_pull(up, n2, inv2, nr[2:3, :])
            sums_ref[0:1, :] += jnp.sum(up * n2, axis=0, keepdims=True)
            sums_ref[1:2, :] += jnp.sum(up, axis=0, keepdims=True)
            two_ref[at, :] = two
            send_ref[at, :width] = two.astype(BF)
            acc = None
            for t, (u, d) in enumerate(((u0, d0), (u1, d1))):
                to = (own_ref, send_ref)[t]
                for c in range(0, units, 256):
                    lanes = slice(t * width + c, t * width + c + 256)
                    slope = sl[at, t * units + c : t * units + c + 256]
                    to[at, lanes] = (dot_nn(send_ref[at, :width], d[:, c : c + 256]) * slope).astype(BF)
                    piece = dot_nt(to[at, lanes], u[:, c : c + 256])
                    acc = piece if acc is None else acc + piece
            part_ref[at, :] = acc.astype(BF)

        by_chunk(rows, step)

    outs = [sds((rows + skip, width)), sds((rows, width), F32), sds((rows, units)), sds((rows, width + units))]
    outs += [sds((8, width), F32), sds((rows, width))]
    ins = [normed, go, weights, norms, u0, u1, d0, d1, slope, *part, *there] + ([] if below is None else [below])
    scratch = [VM((rows, width), BF)] * (2 if n > 1 else 0)
    return order.call(body, outs, ins, info, name, scratch=scratch, **kw)


def split_sides(info, whole, away, here):
    side = lax.rem(info[1], 2)
    height = whole.shape[0] // 8
    for z in range(4):
        rows = slice(z * height, (z + 1) * height)
        for out, s in ((away, 1 - side), (here, side)):
            out[rows, :] = whole[pl.ds(pl.multiple_of((2 * z + s) * height, 16), height), :].astype(out.dtype)


def grads(order, info, pairs, width, units, name, split=True, **kw):
    flat = [x for p in pairs for x in (p[0], p[2])]

    def body(sc, *refs):
        ins, outs = refs[: len(flat)], refs[len(flat) :]
        whole = outs[-1]

        @pl.loop(0, width // 256)
        def _(i):
            acc = None
            for k, (_, first, _, column) in enumerate(pairs):
                left = ins[2 * k][:, pl.ds(pl.multiple_of(first + i * 256, 256), 256)]
                piece = dot_tn(left, ins[2 * k + 1][:, column : column + units])
                acc = piece if acc is None else acc + piece
            whole[pl.ds(pl.multiple_of(i * 256, 256), 256), :] = acc

        if split:
            split_sides(sc, whole, outs[1], outs[0])

    if split:
        outs, scratch = [sds((width // 2, units), d) for d in (F32, BF)], [VM((width, units), F32)]
    else:
        outs, scratch = sds((width, units), F32), []
    return order.call(body, outs, flat, info, name, scratch=scratch, **kw)


def attend_back(order, info, kind, two, part, there, normed, inverse, norms, o_here, q, k, v, lse, weights, local, name, **kw):
    heads = local // HD
    rows, kv_rows = q.shape[1], k.shape[1]
    width = norms.shape[1]
    whole = kind == "a"

    def body(sc, two_ref, p0, p1, nm, inv, nr, o_ref, q_ref, k_ref, v_ref, lse_ref, *refs):
        if whole:
            w0, w1, one_ref, low_ref, pg0, pg1, sums_ref, part_ref, cg_ref, kv_ref, lt_ref, dq_ref = refs
        else:
            one_ref, low_ref, sums_ref, dq_ref, mine_ref, there_ref, cg_ref, kv_ref, lt_ref = refs
        low = low_of(sc)
        sums_ref[...] = jnp.zeros((8, width), F32)
        keys = lax.broadcasted_iota(jnp.int32, (kv_rows, 1), 0)
        bias = jnp.where(keys < used_of(sc, kind), 0.0, MASK_VALUE)
        if whole:
            kv_ref[...] = jnp.zeros((2, kv_rows, 2 * local), F32)

        def step(r):
            at = pl.ds(r, CHUNK)
            nrm = nm[at, :]
            grad = two_ref[at, :] + (p0[at, :].astype(F32) + p1[at, :].astype(F32))
            sums_ref[0:1, :] += jnp.sum(grad * nrm, axis=0, keepdims=True)
            sums_ref[1:2, :] += jnp.sum(grad, axis=0, keepdims=True)
            one = norm_pull(grad, nrm, inv[at, :1], nr[0:1, :])
            one_ref[at, :] = one
            low_ref[at, :] = one.astype(BF)
            for t in range(2):
                cg_ref[t] = dot_nn(low_ref[at, :], o_ref[:, t * local : (t + 1) * local]).astype(BF)
                lt_ref[t] = jnp.transpose(lse_ref[t, at, :])[:8, :]

            @pl.loop(0, 2)
            def _(t):
                for h in range(heads):
                    lanes = slice(h * HD, (h + 1) * HD)
                    qh, kh, cg = q_ref[t, at, lanes], k_ref[t, :, lanes], cg_ref[t, :, lanes]
                    p = jnp.exp(dot_nt(kh, qh) + bias - lt_ref[t, h : h + 1, :])
                    dp = dot_nt(v_ref[t, :, lanes], cg)
                    ds = (p * (dp - jnp.sum(dp * p, axis=0, keepdims=True))).astype(BF)
                    dv = dot_nn(p.astype(BF), cg)
                    dk = dot_nn(ds, qh)
                    dq_ref[t, at, lanes] = (dot_tn(ds, kh) * 0.125).astype(BF)
                    late = slice(local + h * HD, local + (h + 1) * HD)
                    if whole:
                        kv_ref[t, :, lanes] += dk
                        kv_ref[t, :, late] += dv
                    else:
                        kv_ref[t, :, lanes] = dk
                        kv_ref[t, :, late] = dv

        by_chunk(rows, step)
        if whole:
            for t, pg in enumerate((pg0, pg1)):
                pg[:, :local] = dq_ref[t]
                pg[:, local : 3 * local] = kv_ref[t].astype(BF)
            pg1[:, 3 * local :] = jnp.zeros((rows, -(3 * local) % 128), BF)

            def last(r):
                at = pl.ds(r, CHUNK)
                acc = dot_nt(pg0[at, :], w0[:, : 3 * local]) + dot_nt(pg1[at, : 3 * local], w1[:, : 3 * local])
                part_ref[at, :] = acc.astype(BF)

            by_chunk(rows, last)
        else:
            for t in range(2):
                mine_ref[t] = kv_ref[t, pl.ds(pl.multiple_of(low * CHUNK, CHUNK), CHUNK), :]
                there_ref[t] = kv_ref[t, pl.ds(pl.multiple_of((1 - low) * CHUNK, CHUNK), CHUNK), :].astype(BF)

    outs = [sds((rows, width), F32), sds((rows, width))]
    scratch = [VM((2, CHUNK, local), BF), VM((2, kv_rows, 2 * local), F32), VM((2, 8, CHUNK), F32)]
    if whole:
        outs += [sds((rows, 3 * local)), sds((rows, 3 * local + -(3 * local) % 128)), sds((8, width), F32), sds((rows, width))]
        scratch += [VM((2, rows, local), BF)]
    else:
        outs += [sds((8, width), F32), sds((2, rows, local)), sds((2, CHUNK, 2 * local), F32), sds((2, CHUNK, 2 * local))]
    ins = [two, part, there, normed, inverse, norms, o_here, q, k, v, lse] + (list(weights) if whole else [])
    return order.call(body, outs, ins, info, name, scratch=scratch, **kw)


def project_back(order, info, dq, mine, there, w_own, w_oth, out_oth, local, name, **kw):
    rows, width = dq.shape[1], w_own.shape[0]

    def body(sc, dq_ref, a, b, w0, w1, o, pg0, send_ref, part_ref, pg1):
        acc = None
        send_ref[:, local:] = o[...]
        for t, (w, pg) in enumerate(((w0, pg0), (w1, pg1))):
            pg[:, :local] = dq_ref[t]
            pg[:, local:] = (a[t] + b[1 - t].astype(F32)).astype(BF)
            piece = dot_nt(pg[...], w[:, : 3 * local])
            acc = piece if acc is None else acc + piece
        part_ref[...] = acc.astype(BF)
        for c in range(3):
            send_ref[c * rows : (c + 1) * rows, :local] = pg1[:, c * local : (c + 1) * local]

    outs = [sds((rows, 3 * local)), sds((3 * rows, local + out_oth.shape[1])), sds((rows, width))]
    scratch = [VM((rows, 3 * local), BF)]
    return order.call(body, outs, [dq, mine, there, w_own, w_oth, out_oth], info, name, scratch=scratch, **kw)


def grads_out(order, info, lows, ctxs, sums, local, **kw):
    width = lows[0].shape[1]
    n, s1, s2 = len(lows), len(sums[0]), len(sums[1])

    def body(sc, *refs):
        ls, cs = refs[:n], refs[n : 2 * n]
        ones, twos = refs[2 * n : 2 * n + s1], refs[2 * n + s1 : 2 * n + s1 + s2]
        *outs, cols_ref = refs[2 * n + s1 + s2 :]
        one = sum(x[0:2, :] for x in ones)
        two = sum(x[0:2, :] for x in twos)
        cols = jnp.concatenate([one, two, jnp.zeros((124, width), F32)], axis=0)
        cols_ref[...] = jnp.transpose(cols).astype(BF)

        @pl.loop(0, width // 256)
        def _(i):
            rr = pl.ds(pl.multiple_of(i * 256, 256), 256)
            for t, o in enumerate(outs):
                acc = None
                for x, y in zip(ls, cs):
                    piece = dot_tn(x[:, rr], y[:, t * local : (t + 1) * local])
                    acc = piece if acc is None else acc + piece
                o[rr, :local] = acc.astype(o.dtype)
                o[rr, local:] = cols_ref[rr, :].astype(o.dtype)

    ins = list(lows) + list(ctxs) + list(sums[0]) + list(sums[1])
    outs = [sds((width, local + 128), d) for d in (F32, BF)]
    return order.call(body, outs, ins, info, "grads_out", scratch=[VM((width, 128), BF)], **kw)


def grads_attn(order, info, tokens, mine, there, out_mine, split=True, **kw):
    width, local = tokens.shape[1], mine[0].shape[1] // 3
    full, cut = 4 * local + 128, 2 * local

    def body(sc, tok, ma, mc, ta, tc, om, *outs):
        whole = outs[-1]
        at = {k: pl.ds(first_row(sc, *k), rows_of(k[0])) for k in (("a", False), ("c", False), ("a", True), ("c", True))}
        pairs = [(at["a", False], ma), (at["c", False], mc), (at["a", True], ta)]

        @pl.loop(0, width // 256)
        def _(i):
            rr = pl.ds(pl.multiple_of(i * 256, 256), 256)
            acc = sum(dot_tn(tok[rows, rr], ref[:, : 3 * local]) for rows, ref in pairs)
            last = tok[at["c", True], rr]
            for c in range(3):
                lanes = slice(c * local, (c + 1) * local)
                whole[rr, lanes] = acc[:, lanes] + dot_tn(last, tc[c * CHUNK : (c + 1) * CHUNK, :local])
            whole[rr, 3 * local :] = om[rr, :] + tc[rr, local:].astype(F32)

        if split:
            here_1, away_1, here_2, away_2 = outs[:-1]
            split_sides(sc, whole.at[:, :cut], away_1, here_1)
            split_sides(sc, whole.at[:, cut:], away_2, here_2)

    ins = [tokens, *mine, *there, out_mine]
    if split:
        outs = [sds((width // 2, w), d) for w in (cut, full - cut) for d in (F32, BF)]
        scratch = [VM((width, full), F32)]
    else:
        outs, scratch = sds((width, full), F32), []
    return order.call(body, outs, ins, info, "grads_attn", scratch=scratch, **kw)


def fold_pair(order, info, mine, there, name, **kw):
    height, width = mine.shape[0] // 4, mine.shape[1]

    def body(sc, a, b, here, away):
        level = lax.shift_right_logical(sc[1], 1)
        for out, ks in ((away, (1, 3)), (here, (0, 2))):
            for i, k in enumerate(ks):
                at = pl.ds(pl.multiple_of(jnp.bitwise_xor(level, k) * height, 16), height)
                out[i * height : (i + 1) * height, :] = (a[at, :] + b[at, :].astype(F32)).astype(out.dtype)

    return order.call(body, [sds((2 * height, width), F32), sds((2 * height, width))], [mine, there], info, name, **kw)


def fold_last(order, info, mine, there, name, **kw):
    height, width = mine.shape[0] // 2, mine.shape[1]

    def body(sc, a, b, here, away):
        away[...] = (a[height:, :] + b[height:, :].astype(F32)).astype(BF)
        here[...] = a[:height, :] + b[:height, :].astype(F32)

    return order.call(body, [sds((height, width), F32), sds((height, width))], [mine, there], info, name, **kw)


def add_rows(order, info, groups, name, **kw):
    def body(sc, *refs):
        at = 0
        for k in range(len(groups)):
            a, b, c = refs[3 * k : 3 * k + 3]
            refs[-1][at : at + a.shape[0], :] = a[...] + (b[...].astype(F32) + c[...].astype(F32))
            at += a.shape[0]

    rows = sum(g[0].shape[0] for g in groups)
    return order.call(body, sds((rows, groups[0][0].shape[1]), F32), [x for g in groups for x in g], info, name, **kw)


def lay_rows(order, info, mine, there, name, **kw):
    pieces = []
    for g, arrays in enumerate((mine, there)):
        i = 0
        for n, x in enumerate(arrays):
            for r in range(0, x.shape[0], CHUNK):
                pieces.append((g, g * len(mine) + n, r, i))
                i += 1
    count, arrays = len(pieces), list(mine) + list(there)
    width = mine[0].shape[1]

    def body(sc, *refs):
        out, sems = refs[len(arrays)], refs[len(arrays) + 1]
        copies = []
        for k, (g, n, r, i) in enumerate(pieces):
            half = low_of(sc) if g == 0 else 1 - low_of(sc)
            row = (2 * half + i) * CHUNK if i < 2 else (4 + half) * CHUNK
            at = pl.ds(pl.multiple_of(row, CHUNK), CHUNK)
            copies.append(pltpu.make_async_copy(refs[n].at[r : r + CHUNK, :], out.at[at, :], sems.at[k]))
            copies[-1].start()
        for c in copies:
            c.wait()

    outs = sds((count * CHUNK, width), mine[0].dtype)
    return order.call(body, outs, arrays, info, name, scratch=[pltpu.SemaphoreType.DMA((count,))], raw_out=True, **kw)


def update(order, rates, groups, items, name, **kw):
    arrays = [x for it in items for x in it[:3]]
    shapes = [sds(it[0].shape, d) for it in items for d in (F32, F32, F32, BF)]
    pieces = [p for g in groups for p in g]

    def body(sc, *refs):
        ins = refs[len(pieces) : len(pieces) + len(arrays)]
        outs = refs[len(pieces) + len(arrays) :]
        rate, fix_one, fix_two = sc[0], sc[1], sc[2]
        for n, it in enumerate(items):
            w, m, v = ins[3 * n : 3 * n + 3]
            for index, group, first, count, turned in it[4]:
                lanes = slice(first, first + count)
                g = refs[2 * group][:, lanes] + refs[2 * group + 1][:, lanes].astype(F32)
                if turned:
                    g = jnp.transpose(g)[: w.shape[0], :]
                res = adamw_update(g, w[index], m[index], v[index], rate, fix_one, fix_two, it[3])
                for r, o in zip(res, outs[4 * n : 4 * n + 4]):
                    o[index] = r

    return order.call(body, shapes, pieces + arrays, rates, name, **kw)


def swap(x, axis, size, bit):
    return lax.ppermute(x, axis, [(i, i ^ bit) for i in range(size)])


def solution(mesh):
    dp_size = mesh.shape["dp"]
    t_size = mesh.shape["tensor"]

    def core_swap(x):
        return swap(x, "tensor", t_size, 1)

    def far_swap(x):
        return swap(x, "tensor", t_size, 2)

    def dp_swap(x, bit):
        return swap(x, "dp", dp_size, bit)

    def on_device(
        tokens, grad_out, token_weight, lengths, step, qkv_weight, out_weight, up_weight, down_weight,
        norm_params, first_qkv, first_out, first_up, first_down, first_norm, second_qkv, second_out,
        second_up, second_down, second_norm,
    ):
        order = Order()
        rows_d, local = qkv_weight.shape[1], qkv_weight.shape[2]
        units = up_weight.shape[1]
        tok_count = tokens.shape[0]
        direct = dp_size == 8 and rows_d % 16 == 0
        places = jnp.stack([lax.axis_index("tensor"), lax.axis_index("dp")]).astype(jnp.int32)
        info = jnp.concatenate([places, lengths])
        weights = token_weight.reshape(tok_count // 128, 128)
        step_float = step[0].astype(F32)
        rate = PEAK_RATE * jnp.minimum(step_float / WARM_STEPS, (LAST_STEP - step_float) / (LAST_STEP - WARM_STEPS))
        fix_one = 1.0 - BETA_ONE**step_float
        fix_two = 1.0 - BETA_TWO**step_float
        rates = jnp.stack([rate, fix_one, fix_two])
        down_t = down_weight.T

        slots = (0, 2, 4, 6, 1, 3, 5, 7)
        if direct:
            pack_q, pack_o = pack(order, info, qkv_weight, out_weight)
            q_x = dp_swap(pack_q, 1)
            q_z = [dp_swap(pack_q, k) for k in (2, 4, 6)]
            pack_u = pack_more(order, info, up_weight, far_swap(pack_o), norm_params, warm=[tokens])
            q_near = stack(order, info, q_z, "stack_q", deps=[q_x])
            q_far = dp_swap(q_near, 1)
            u_four = stack(order, info, [pack_u] + [dp_swap(pack_u, k) for k in (2, 4, 6)], "stack_u")
            u_x = dp_swap(u_four, 1)
            q_own = place(order, info, [pack_q, q_near, q_x, q_far], slots, "place_q")
            q_oth = core_swap(q_own)
            d_one = dp_swap(down_t, 4)
        else:
            pad = jnp.zeros((rows_d, -(units + local) % 128 - 4), BF)
            pack_q = jnp.concatenate([qkv_weight[0], qkv_weight[1], qkv_weight[2], out_weight.T], axis=1)
            pack_u = jnp.concatenate([up_weight, far_swap(out_weight.T), norm_params.T, pad], axis=1)
            q_own, u_own, d_own = (lax.all_gather(x, "dp", axis=0, tiled=True) for x in (pack_q, pack_u, down_t))
            q_oth = core_swap(q_own)

        q_a, k_a, v_a, lse_a, ctx_a = attend(order, info, "a", tokens, q_own, q_oth, local, "attend_a")
        ctx_a_there = far_swap(ctx_a)
        if direct:
            d_two = stack(order, info, [down_t, d_one], "stack_d")
            d_z = dp_swap(d_two, 2)
        q_c, k_c, v_c, lse_c, ctx_c = attend(order, info, "c", tokens, q_own, q_oth, local, "attend_c")
        ctx_c_there = far_swap(ctx_c)
        if direct:
            d_four = stack(order, info, [d_two, d_z], "stack_d4")
            d_x = dp_swap(d_four, 1)
            u_own = place(order, info, [u_four, u_x], slots, "place_u", deps=[ctx_a_there])
        u_oth = core_swap(u_own)
        norms, o_here, o_low, o_high = settle(order, info, u_own, u_oth, q_own, q_oth, units, local)
        args = (o_low, o_high, u_own, u_oth, norms, units)
        normed_a, inv_a, slope_a, inner_a, sent_a = lift(order, info, "a", tokens, ctx_a, ctx_a_there, *args, "lift_a")
        if direct:
            d_own = place(order, info, [d_four, d_x], (0, 4, 2, 6, 1, 5, 3, 7), "place_d", warm=[grad_out, weights], deps=[ctx_c_there])
        d_oth = core_swap(d_own)
        normed_c, inv_c, slope_c, inner_c, sent_c = lift(order, info, "c", tokens, ctx_c, ctx_c_there, *args, "lift_c")
        part_c = drop(order, info, inner_c, sent_c, d_own, d_oth, "drop_c")
        part_c_there = [far_swap(p) for p in part_c]
        part_a = drop(order, info, inner_a, sent_a, d_own, d_oth, "drop_a")
        part_a_there = [far_swap(p) for p in part_a]
        got_hi_a, got_hi_c = core_swap(sent_a), core_swap(sent_c)
        args = (grad_out, weights, norms, u_own, u_oth, d_own, d_oth)
        res_c, two_c, up_c, fu_c, sums_c2, back_c = turn(
            order, info, "c", normed_c, part_c, part_c_there, *args, slope_c, "turn_c", deps=[got_hi_a, got_hi_c])
        result, two_a, up_a, fu_a, sums_a2, back_a = turn(
            order, info, "a", normed_a, part_a, part_a_there, *args, slope_a, "turn_a", below=res_c)
        back_a_there = far_swap(back_a)
        back_c_there = far_swap(back_c)
        got_fu_a, got_fu_c = core_swap(fu_a), core_swap(fu_c)
        width = tokens.shape[1]
        pairs = [(fu_a, 0, inner_a, 0), (fu_c, 0, inner_c, 0), (got_fu_a, 0, got_hi_a, width), (got_fu_c, 0, got_hi_c, width)]
        grad_d = grads(order, info, pairs, width, units, "grads_d", split=direct)
        pairs = [(sent_a, 0, up_a, 0), (sent_c, 0, up_c, 0), (got_hi_a, 0, got_fu_a, width), (got_hi_c, 0, got_fu_c, width)]
        grad_u = grads(order, info, pairs, width, units, "grads_u", split=direct)
        res_there = core_swap(result)

        def second_fold(parts, name, **kw):
            here, away = fold_pair(order, info, *parts, "pair_" + name, **kw)
            return here, dp_swap(away, 2)

        def third_fold(pair, name, **kw):
            here, away = fold_last(order, info, *pair, "last_" + name, **kw)
            return here, dp_swap(away, 4)

        if direct:
            fold_d, fold_u = (grad_d[0], dp_swap(grad_d[1], 1)), (grad_u[0], dp_swap(grad_u[1], 1))
        one_a, low_a, pg_a, pg_a_oth, sums_a1, in_a = attend_back(
            order, info, "a", two_a, back_a, back_a_there, normed_a, inv_a, norms, o_here, q_a, k_a, v_a, lse_a, (q_own, q_oth), local, "back_a")
        in_a_there = far_swap(in_a)
        got_a = core_swap(pg_a_oth)
        one_c, low_c, sums_c1, dq_c, kv_mine, kv_there = attend_back(
            order, info, "c", two_c, back_c, back_c_there, normed_c, inv_c, norms, o_here, q_c, k_c, v_c, lse_c, None, local, "back_c")
        kv_got = core_swap(kv_there)
        if direct:
            fold_d = second_fold(fold_d, "d")
            fold_u = second_fold(fold_u, "u")
        res_full = lay_rows(order, info, [result], [res_there], "lay_out")
        out_mine, out_oth = grads_out(
            order, info, (low_a, low_c), (ctx_a, ctx_c), ((sums_a1, sums_c1), (sums_a2, sums_c2)), local)
        pg_c, sent, in_c = project_back(order, info, dq_c, kv_mine, kv_got, q_own, q_oth, out_oth, local, "project_c")
        in_c_there = far_swap(in_c)
        got_c = core_swap(sent)
        grad_a = grads_attn(order, info, tokens, (pg_a, pg_c), (got_a, got_c), out_mine, split=direct)
        everything = slice(None)
        if direct:
            keep_1, send_1, keep_2, send_2 = grad_a
            fold_1, fold_2 = (keep_1, dp_swap(send_1, 1)), (keep_2, dp_swap(send_2, 1))
            fold_d = third_fold(fold_d, "d")
            fold_u = third_fold(fold_u, "u")
            fold_2 = second_fold(fold_2, "vo")
            n_down = update(order, rates, [fold_d], [
                (down_t, first_down.T, second_down.T, DECAY_RATE, [(everything, 0, 0, units, False)])], "update_d")
            fold_1 = second_fold(fold_1, "qk")
            n_up = update(order, rates, [fold_u], [
                (up_weight, first_up, second_up, DECAY_RATE, [(everything, 0, 0, units, False)])], "update_u")
            fold_2 = third_fold(fold_2, "vo")
            fold_1 = third_fold(fold_1, "qk")
        gi = add_rows(order, info, [(one_a, in_a, in_a_there), (one_c, in_c, in_c_there)], "add_in")
        gi_there = core_swap(gi)
        if direct:
            res = update(order, rates, [fold_1, fold_2], [
                (qkv_weight, first_qkv, second_qkv, DECAY_RATE,
                 [(0, 0, 0, local, False), (1, 0, local, local, False), (2, 1, 0, local, False)]),
                (out_weight, first_out, second_out, DECAY_RATE, [(everything, 1, local, local, True)]),
                (norm_params, first_norm, second_norm, 0.0, [(everything, 1, 2 * local, 128, True)]),
            ], "update_a")
            n_down = [x.T for x in n_down]
            n_qkv, n_out, n_norm = res[:4], res[4:8], res[8:]
        input_grad = lay_rows(order, info, [gi], [gi_there], "lay_grad")
        if not direct:
            su, sd, sa = (lax.psum_scatter(x, "dp", scatter_dimension=0, tiled=True) for x in (grad_u, grad_d, grad_a))
            rest = (rate, fix_one, fix_two)
            n_up = adamw_update(su, up_weight, first_up, second_up, *rest, DECAY_RATE)
            n_down = adamw_update(sd.T, down_weight, first_down, second_down, *rest, DECAY_RATE)
            sq = jnp.stack([sa[:, c * local : (c + 1) * local] for c in range(3)])
            n_qkv = adamw_update(sq, qkv_weight, first_qkv, second_qkv, *rest, DECAY_RATE)
            n_out = adamw_update(sa[:, 3 * local : 4 * local].T, out_weight, first_out, second_out, *rest, DECAY_RATE)
            n_norm = adamw_update(sa[:, 4 * local : 4 * local + 4].T, norm_params, first_norm, second_norm, *rest, 0.0)
        return (res_full, input_grad, *n_qkv, *n_out, *n_up, *n_down, *n_norm)

    rows = P("dp", None)
    qkv, col, row, norm = P(None, "dp", "tensor"), P("tensor", "dp"), P("dp", "tensor"), P(None, "dp")
    params = (qkv, col, row, col, norm)
    return jax.shard_map(
        on_device,
        mesh=mesh,
        in_specs=(rows, rows, P("dp"), P("dp"), P()) + params * 3,
        out_specs=(rows, rows) + (qkv,) * 4 + (col,) * 4 + (row,) * 4 + (col,) * 4 + (norm,) * 4,
        check_vma=False,
    )
```

```python
import jax
import jax.numpy as jnp
from jax import lax
from jax.experimental import pallas as pl
from jax.experimental.pallas import tpu as pltpu
from jax.sharding import PartitionSpec as P

HD = 64
NORM_EPS = 1e-05
MASK_VALUE = -1000000000.0
BETA_ONE = 0.9
BETA_TWO = 0.95
ADAM_EPS = 1e-08
DECAY_RATE = 0.01
PEAK_RATE = 0.15
WARM_STEPS = 2.0
LAST_STEP = 40.0
BF = jnp.bfloat16
F32 = jnp.float32
VM = pltpu.VMEM
CHUNK = 256


def dot_nn(a, b):
    return lax.dot_general(a, b, (((1,), (0,)), ((), ())), preferred_element_type=F32)


def dot_nt(a, b):
    return lax.dot_general(a, b, (((1,), (1,)), ((), ())), preferred_element_type=F32)


def dot_tn(a, b):
    return lax.dot_general(a, b, (((0,), (0,)), ((), ())), preferred_element_type=F32)


def sds(shape, dtype=BF):
    return jax.ShapeDtypeStruct(shape, dtype)


class Order:
    def __init__(self):
        self.last = None

    def call(self, body, outs, ins, info, name, scratch=(), limit=12, raw_in=False, raw_out=False, deps=(), warm=(), free=False):
        ins = list(ins)
        n = len(ins) + 1
        specs = [pl.BlockSpec(memory_space=pltpu.SMEM)]
        specs += [pl.BlockSpec(memory_space=pltpu.HBM if raw_in else VM)] * len(ins)
        extra = list(warm) + list(deps) + ([] if self.last is None or free else [self.last])
        specs += [pl.BlockSpec(memory_space=VM)] * len(warm)
        specs += [pl.BlockSpec(memory_space=pl.ANY)] * (len(extra) - len(warm))

        single = not isinstance(outs, (list, tuple))
        shapes = ([outs] if single else list(outs)) + [sds((8, 128), F32)]
        specs_out = [pl.BlockSpec(memory_space=pltpu.HBM if raw_out else VM)] * (len(shapes) - 1) + [pl.BlockSpec(memory_space=VM)]
        token = n + len(extra) + len(shapes) - 1

        def run(*refs):
            body(*refs[:n], *refs[n + len(extra) : token], *refs[token + 1 :])
            refs[token][...] = jnp.zeros((8, 128), F32)

        res = pl.pallas_call(
            run,
            out_shape=shapes,
            in_specs=specs,
            out_specs=specs_out,
            scratch_shapes=list(scratch),
            compiler_params=pltpu.CompilerParams(vmem_limit_bytes=limit * 1024 * 1024),
            cost_estimate=pl.CostEstimate(flops=1, bytes_accessed=1, transcendentals=0),
            name=name,
        )(info, *ins, *extra)
        if not free:
            self.last = res[-1]
        return res[0] if single else list(res[:-1])


def low_of(info):
    return lax.rem(info[0], 2)


def rows_of(kind):
    return 2 * CHUNK if kind == "a" else CHUNK


def first_row(info, kind, other=False):
    low = 1 - low_of(info) if other else low_of(info)
    return pl.multiple_of(2 * low * CHUNK if kind == "a" else (4 + low) * CHUNK, CHUNK)


def used_of(info, kind):
    return info[2 + low_of(info)] if kind == "a" else info[4]


def by_chunk(rows, step):
    if rows == CHUNK:
        step(0)
    else:

        @pl.loop(0, rows // CHUNK)
        def _(r):
            step(pl.multiple_of(r * CHUNK, CHUNK))


def norm_stats(summed):
    center = summed - jnp.mean(summed, axis=-1, keepdims=True)
    inverse = lax.rsqrt(jnp.mean(center * center, axis=-1, keepdims=True) + NORM_EPS)
    return center * inverse, inverse


def norm_pull(upstream, normed, inverse, gain):
    scaled = upstream * gain
    return inverse * (
        scaled
        - jnp.mean(scaled, axis=-1, keepdims=True)
        - normed * jnp.mean(scaled * normed, axis=-1, keepdims=True)
    )


def gelu_parts(u):
    cdf = 0.5 * (1.0 + lax.erf(u * (0.5**0.5)))
    pdf = jnp.exp(-0.5 * u * u) * 0.3989422804014327
    return u * cdf, cdf + u * pdf


def adamw_update(gradient, weight_low, first, second, rate, fix_one, fix_two, decay):
    weight = weight_low.astype(F32)
    first_new = BETA_ONE * first + (1.0 - BETA_ONE) * gradient
    second_new = BETA_TWO * second + (1.0 - BETA_TWO) * gradient * gradient
    direction = first_new / fix_one / (jnp.sqrt(second_new / fix_two) + ADAM_EPS)
    weight_new = weight - rate * (direction + decay * weight)
    return (weight_new, first_new, second_new, weight_new.astype(BF))


def pack(order, info, qkv, out):
    rows, local = qkv.shape[1], qkv.shape[2]

    def body(sc, *refs):
        given, (pq, po), (q, o, sems) = refs[:2], refs[2:4], refs[4:]
        copies = [pltpu.make_async_copy(a, b, sems.at[k]) for k, (a, b) in enumerate(zip(given, (q, o)))]
        for c in copies:
            c.start()
        for c in copies:
            c.wait()
        for c in range(3):
            pq[:, c * local : (c + 1) * local] = q[c]
        turned = jnp.transpose(o[...].astype(F32)).astype(BF)
        pq[:, 3 * local :] = turned
        po[...] = turned

    ins = [qkv, out]
    scratch = [VM(x.shape, x.dtype) for x in ins] + [pltpu.SemaphoreType.DMA((2,))]
    return order.call(body, [sds((rows, 4 * local)), sds((rows, local))], ins, info, "pack", scratch=scratch, raw_in=True)


def pack_more(order, info, up, out_there, norm, **kw):
    rows, units, local = up.shape[0], up.shape[1], out_there.shape[1]
    pad = -(units + local) % 128

    def body(sc, u, o, n, p):
        p[:, :units] = u[...]
        p[:, units : units + local] = o[...]
        cols = jnp.concatenate([n[...].astype(F32), jnp.zeros((124, rows), F32)], axis=0)
        p[:, units + local :] = jnp.transpose(cols)[:, :pad].astype(BF)

    return order.call(body, sds((rows, units + local + pad)), [up, out_there, norm], info, "pack_more", **kw)


def stack(order, info, blocks, name, **kw):
    height, width = blocks[0].shape
    count = len(blocks)

    def body(sc, *refs):
        for k in range(count):
            refs[count][k * height : (k + 1) * height, :] = refs[k][...]

    return order.call(body, sds((count * height, width)), blocks, info, name, **kw)


def place(order, info, blocks, marks, name, **kw):
    count = len(marks)
    height, width = sum(b.shape[0] for b in blocks) // count, blocks[0].shape[1]
    n = len(blocks)

    def body(sc, *refs):
        k = 0
        for ref in refs[:n]:
            for r in range(0, ref.shape[0], height):
                at = pl.ds(pl.multiple_of(jnp.bitwise_xor(sc[1], marks[k]) * height, 16), height)
                refs[n][at, :] = ref[r : r + height, :]
                k += 1

    return order.call(body, sds((count * height, width)), blocks, info, name, **kw)


def settle(order, info, u_own, u_oth, q_own, q_oth, units, local, **kw):
    width = u_own.shape[0]
    top = (units + local) // 128 * 128
    row = units + local - top

    def body(sc, a, b, c, d, norms, here, low, high):
        norms[...] = jnp.transpose(a[:, top:].astype(F32))[row : row + 8, :]
        first = sc[0] < 2
        for k, (x, y) in enumerate(((c, a), (d, b))):
            lanes = slice(k * local, (k + 1) * local)
            x, y = x[:, 3 * local :], y[:, units : units + local]
            here[:, lanes] = x
            low[:, lanes] = jnp.where(first, x, y)
            high[:, lanes] = jnp.where(first, y, x)

    outs = [sds((8, width), F32)] + [sds((width, 2 * local))] * 3
    return order.call(body, outs, [u_own, u_oth, q_own, q_oth], info, "settle", **kw)


def attend(order, info, kind, tokens, w_own, w_oth, local, name, **kw):
    heads = local // HD
    both = 2 * local
    kv_rows = 2 * CHUNK
    rows = rows_of(kind)

    def body(sc, x_ref, w0, w1, q_ref, k_ref, v_ref, lse_ref, ctx_ref, part_ref):
        keys = lax.broadcasted_iota(jnp.int32, (1, kv_rows), 1)
        bias = jnp.where(keys < used_of(sc, kind), 0.0, MASK_VALUE)
        for t, w in enumerate((w0, w1)):
            if kind == "c":
                q_ref[t] = (dot_nn(x_ref[pl.ds(first_row(sc, kind), rows), :], w[:, :local]) * 0.125).astype(BF)
                p = dot_nn(x_ref[2 * kv_rows :, :], w[:, local : 3 * local])
                k_ref[t] = p[:, :local].astype(BF)
                v_ref[t] = p[:, local:].astype(BF)
            else:
                p = dot_nn(x_ref[pl.ds(first_row(sc, kind), rows), :], w[:, : 3 * local])
                q_ref[t] = (p[:, :local] * 0.125).astype(BF)
                k_ref[t] = p[:, local : 2 * local].astype(BF)
                v_ref[t] = p[:, 2 * local :].astype(BF)

        @pl.loop(0, 2 * (rows // CHUNK))
        def _(i):
            t = lax.rem(i, 2)
            at = pl.ds(pl.multiple_of(lax.div(i, 2) * CHUNK, CHUNK), CHUNK)
            for h in range(heads):
                lanes = slice(h * HD, (h + 1) * HD)
                s = dot_nt(q_ref[t, at, lanes], k_ref[t, :, lanes]) + bias
                top = jnp.max(s, axis=-1, keepdims=True)
                e = jnp.exp(s - top)
                total = jnp.sum(e, axis=-1, keepdims=True)
                part_ref[t, at, lanes] = dot_nn((e * (1.0 / total)).astype(BF), v_ref[t, :, lanes]).astype(BF)
                lse_ref[t, at, h : h + 1] = top + jnp.log(total)

        for t in range(2):
            ctx_ref[:, t * local : (t + 1) * local] = part_ref[t]

    outs = [sds((2, n, local)) for n in (rows, kv_rows, kv_rows)] + [sds((2, rows, 128), F32), sds((rows, both))]
    return order.call(body, outs, [tokens, w_own, w_oth], info, name, scratch=[VM((2, rows, local), BF)], **kw)


def lift(order, info, kind, tokens, ctx, there, o_low, o_high, u0, u1, norms, units, name, **kw):
    rows, width = rows_of(kind), tokens.shape[1]
    both = 2 * units

    def body(sc, tok, c0, c1, ol, oh, u0, u1, nr, normed_ref, inv_ref, slope_ref, own_ref, send_ref):
        first = sc[0] < 2
        top = first_row(sc, kind)

        def step(r):
            at = pl.ds(r, CHUNK)
            a, b = c0[at, :], c1[at, :]
            attn = dot_nt(jnp.where(first, a, b), ol[...]) + dot_nt(jnp.where(first, b, a), oh[...])
            normed, inverse = norm_stats(tok[pl.ds(pl.multiple_of(top + r, CHUNK), CHUNK), :].astype(F32) + attn)
            normed_ref[at, :] = normed
            inv_ref[at, :] = jnp.broadcast_to(inverse, (CHUNK, 128))
            send_ref[at, :width] = (normed * nr[0:1, :] + nr[1:2, :]).astype(BF)
            for t, u in enumerate((u0, u1)):
                for c in range(0, units, 256):
                    g, s = gelu_parts(dot_nn(send_ref[at, :width], u[:, c : c + 256]))
                    slope_ref[at, t * units + c : t * units + c + 256] = s
                    if t == 0:
                        own_ref[at, c : c + 256] = g.astype(BF)
                    else:
                        send_ref[at, width + c : width + c + 256] = g.astype(BF)

        by_chunk(rows, step)

    outs = [sds((rows, width), F32), sds((rows, 128), F32), sds((rows, both), F32), sds((rows, units)), sds((rows, width + units))]
    return order.call(body, outs, [tokens, ctx, there, o_low, o_high, u0, u1, norms], info, name, **kw)


def drop(order, info, own, sent, d0, d1, name, **kw):
    rows, width = own.shape[0], d0.shape[0]

    def body(sc, own_ref, sent_ref, d0, d1, *parts):
        for k, part_ref in enumerate(parts):
            at = slice(k * CHUNK, (k + 1) * CHUNK)
            part_ref[...] = (dot_nt(own_ref[at, :], d0[...]) + dot_nt(sent_ref[at, width:], d1[...])).astype(BF)

    return order.call(body, [sds((CHUNK, width))] * (rows // CHUNK), [own, sent, d0, d1], info, name, **kw)


def row_scale(info, weights, kind, r):
    length = used_of(info, kind)
    first = r if kind == "a" else low_of(info) * CHUNK
    top = lax.div(first_row(info, kind) + r, 128)
    slot = lax.broadcasted_iota(jnp.int32, (128, 128), 0)
    lane = lax.broadcasted_iota(jnp.int32, (128, 128), 1)
    cols = []
    for k in range(CHUNK // 128):
        keep = (slot == lane) & (slot + (first + k * 128) < length)
        cols.append(jnp.sum(jnp.where(keep, weights[pl.ds(top + k, 1), :], 0.0), axis=-1, keepdims=True))
    return jnp.concatenate(cols, axis=0)


def turn(order, info, kind, row, normed, part, there, go, weights, norms, u0, u1, d0, d1, slope, name, around=(), before=None, **kw):
    width = normed.shape[1]
    units = d0.shape[1]
    skip = around[0].shape[0] if around else 0
    total = skip + CHUNK + (around[1].shape[0] if around else 0)

    def body(sc, nm, g, sw, nr, u0, u1, d0, d1, sl, p0, p1, *refs):
        out_ref, two_ref, own_ref, send_ref, sums_ref, part_ref = refs[-6:]
        if around:
            out_ref[:skip, :] = refs[0][...]
            out_ref[skip + CHUNK :, :] = refs[1][...]
        at = slice(row, row + CHUNK)
        ffn = p0[...].astype(F32) + p1[...].astype(F32)
        n2, inv2 = norm_stats((nm[at, :] * nr[0:1, :] + nr[1:2, :]) + ffn)
        out_ref[skip : skip + CHUNK, :] = (n2 * nr[2:3, :] + nr[3:4, :]).astype(BF)
        up = g[pl.ds(pl.multiple_of(first_row(sc, kind) + row, CHUNK), CHUNK), :].astype(F32) * row_scale(sc, sw, kind, row)
        two = norm_pull(up, n2, inv2, nr[2:3, :])
        sums_ref[0:1, :] = jnp.sum(up * n2, axis=0, keepdims=True)
        sums_ref[1:2, :] = jnp.sum(up, axis=0, keepdims=True)
        two_ref[...] = two
        send_ref[:, :width] = two.astype(BF)
        acc = None
        for t, (u, d) in enumerate(((u0, d0), (u1, d1))):
            to, base = ((own_ref, 0), (send_ref, width))[t]
            for c in range(0, units, 256):
                lanes = slice(base + c, base + c + 256)
                steep = sl[at, t * units + c : t * units + c + 256]
                to[:, lanes] = (dot_nn(send_ref[:, :width], d[:, c : c + 256]) * steep).astype(BF)
                piece = dot_nt(to[:, lanes], u[:, c : c + 256])
                acc = piece if acc is None else acc + piece
        if before is None:
            part_ref[...] = acc.astype(BF)
        else:
            part_ref[:CHUNK, :] = refs[-7][...]
            part_ref[CHUNK:, :] = acc.astype(BF)

    outs = [sds((total, width)), sds((CHUNK, width), F32), sds((CHUNK, units)), sds((CHUNK, width + units))]
    outs += [sds((8, width), F32), sds((CHUNK if before is None else 2 * CHUNK, width))]
    ins = [normed, go, weights, norms, u0, u1, d0, d1, slope, part, there, *around] + ([] if before is None else [before])
    return order.call(body, outs, ins, info, name, **kw)


def split_sides(info, whole, away, here):
    side = lax.rem(info[1], 2)
    height = whole.shape[0] // 8
    for z in range(4):
        rows = slice(z * height, (z + 1) * height)
        for out, s in ((away, 1 - side), (here, side)):
            out[rows, :] = whole[pl.ds(pl.multiple_of((2 * z + s) * height, 16), height), :].astype(out.dtype)


def grads(order, info, pairs, width, units, name, split=True, **kw):
    flat = []
    for p in pairs:
        flat += [x for x in (p[0], p[3]) if not any(x is y for y in flat)]

    def place_of(x):
        return next(k for k, y in enumerate(flat) if x is y)


    def body(sc, *refs):
        ins, outs = refs[: len(flat)], refs[len(flat) :]
        whole = outs[-1]

        @pl.loop(0, width // 256)
        def _(i):
            acc = None
            for x, top, first, y, row, column in pairs:
                left = ins[place_of(x)][top : top + CHUNK, pl.ds(pl.multiple_of(first + i * 256, 256), 256)]
                piece = dot_tn(left, ins[place_of(y)][row : row + CHUNK, column : column + units])
                acc = piece if acc is None else acc + piece
            whole[pl.ds(pl.multiple_of(i * 256, 256), 256), :] = acc

        if split:
            split_sides(sc, whole, outs[1], outs[0])

    if split:
        outs, scratch = [sds((width // 2, units), d) for d in (F32, BF)], [VM((width, units), F32)]
    else:
        outs, scratch = sds((width, units), F32), []
    return order.call(body, outs, flat, info, name, scratch=scratch, **kw)


def attend_back(order, info, kind, two, part, there, normed, inverse, norms, o_here, q, k, v, lse, weights, local, name, **kw):
    heads = local // HD
    rows, kv_rows = q.shape[1], k.shape[1]
    width = norms.shape[1]
    whole = kind == "a"

    n = rows // CHUNK

    def body(sc, *refs):
        twos, p0, p1, refs = refs[:n], refs[n], refs[n + 1], refs[n + 2 :]
        nm, inv, nr, o_ref, q_ref, k_ref, v_ref, lse_ref, *refs = refs
        if whole:
            w0, w1, one_ref, low_ref, pg0, pg1, sums_ref, part_ref, cg_ref, kv_ref, lt_ref, dq_ref = refs
        else:
            one_ref, low_ref, sums_ref, dq_ref, mine_ref, send_ref, cg_ref, kv_ref, lt_ref = refs
        low = low_of(sc)
        sums_ref[...] = jnp.zeros((8, width), F32)
        keys = lax.broadcasted_iota(jnp.int32, (kv_rows, 1), 0)
        bias = jnp.where(keys < used_of(sc, kind), 0.0, MASK_VALUE)
        if whole:
            kv_ref[...] = jnp.zeros((2, kv_rows, 2 * local), F32)

        def step(r):
            at, i = slice(r, r + CHUNK), r // CHUNK
            nrm = nm[at, :]
            grad = twos[i][...] + (p0[at, :].astype(F32) + p1[at, :].astype(F32))
            sums_ref[0:1, :] += jnp.sum(grad * nrm, axis=0, keepdims=True)
            sums_ref[1:2, :] += jnp.sum(grad, axis=0, keepdims=True)
            one = norm_pull(grad, nrm, inv[at, :1], nr[0:1, :])
            one_ref[at, :] = one
            low_ref[at, :] = one.astype(BF)
            for t in range(2):
                cg_ref[t, at, :] = dot_nn(low_ref[at, :], o_ref[:, t * local : (t + 1) * local]).astype(BF)
                lt_ref[t, i] = jnp.transpose(lse_ref[t, at, :])[:8, :]

        for r in range(0, rows, CHUNK):
            step(r)

        def heads_of(r):
            at, i = pl.ds(r, CHUNK), lax.div(r, CHUNK)

            @pl.loop(0, 2)
            def _(t):
                for h in range(heads):
                    lanes = slice(h * HD, (h + 1) * HD)
                    qh, kh, cg = q_ref[t, at, lanes], k_ref[t, :, lanes], cg_ref[t, at, lanes]
                    p = jnp.exp(dot_nt(kh, qh) + bias - lt_ref[t, i, h : h + 1, :])
                    dp = dot_nt(v_ref[t, :, lanes], cg)
                    ds = (p * (dp - jnp.sum(dp * p, axis=0, keepdims=True))).astype(BF)
                    dv = dot_nn(p.astype(BF), cg)
                    dk = dot_nn(ds, qh)
                    dq_ref[t, at, lanes] = (dot_tn(ds, kh) * 0.125).astype(BF)
                    late = slice(local + h * HD, local + (h + 1) * HD)
                    if whole:
                        kv_ref[t, :, lanes] += dk
                        kv_ref[t, :, late] += dv
                    else:
                        kv_ref[t, :, lanes] = dk
                        kv_ref[t, :, late] = dv

        by_chunk(rows, heads_of)
        if whole:
            for t, pg in enumerate((pg0, pg1)):
                pg[:, :local] = dq_ref[t]
                pg[:, local : 3 * local] = kv_ref[t].astype(BF)
            pg1[:, 3 * local :] = jnp.zeros((rows, -(3 * local) % 128), BF)

            def last(r):
                at = pl.ds(r, CHUNK)
                acc = dot_nt(pg0[at, :], w0[:, : 3 * local]) + dot_nt(pg1[at, : 3 * local], w1[:, : 3 * local])
                part_ref[at, :] = acc.astype(BF)

            by_chunk(rows, last)
        else:
            own = pl.ds(pl.multiple_of(low * CHUNK, CHUNK), CHUNK)
            other = pl.ds(pl.multiple_of((1 - low) * CHUNK, CHUNK), CHUNK)
            for t in range(2):
                mine_ref[t] = kv_ref[t, own, :]
            for k, (t, at) in enumerate(((1, own), (1, other), (0, other))):
                send_ref[k * CHUNK : (k + 1) * CHUNK, :] = kv_ref[t, at, :].astype(BF)
            for k in range(2):
                send_ref[3 * CHUNK :, k * local : (k + 1) * local] = dq_ref[1, k * 128 : (k + 1) * 128, :]

    outs = [sds((rows, width), F32), sds((rows, width))]
    scratch = [VM((2, rows, local), BF), VM((2, kv_rows, 2 * local), F32), VM((2, n, 8, CHUNK), F32)]
    if whole:
        outs += [sds((rows, 3 * local)), sds((rows, 3 * local + -(3 * local) % 128)), sds((8, width), F32), sds((rows, width))]
        scratch += [VM((2, rows, local), BF)]
    else:
        outs += [sds((8, width), F32), sds((2, rows, local)), sds((2, CHUNK, 2 * local), F32), sds((3 * CHUNK + 128, 2 * local))]
    ins = [*two, part, there, normed, inverse, norms, o_here, q, k, v, lse] + (list(weights) if whole else [])
    return order.call(body, outs, ins, info, name, scratch=scratch, **kw)


def project_back(order, info, dq, mine, got, w_own, w_oth, local, name, **kw):
    rows, width = dq.shape[1], w_own.shape[0]

    def body(sc, dq_ref, a, g, w0, w1, part_ref, pg):
        acc = None
        for t, w in enumerate((w0, w1)):
            pg[:, :local] = dq_ref[t]
            pg[:, local:] = (a[t] + g[(t + 1) * CHUNK : (t + 2) * CHUNK, :].astype(F32)).astype(BF)
            piece = dot_nt(pg[...], w[:, : 3 * local])
            acc = piece if acc is None else acc + piece
        part_ref[...] = acc.astype(BF)

    scratch = [VM((rows, 3 * local), BF)]
    return order.call(body, sds((rows, width)), [dq, mine, got, w_own, w_oth], info, name, scratch=scratch, **kw)


def grads_out(order, info, lows, ctxs, sums, local, **kw):
    width = lows[0].shape[1]
    n, s1, s2 = len(lows), len(sums[0]), len(sums[1])

    def body(sc, *refs):
        ls, cs = refs[:n], refs[n : 2 * n]
        ones, twos = refs[2 * n : 2 * n + s1], refs[2 * n + s1 : 2 * n + s1 + s2]
        *outs, cols_ref = refs[2 * n + s1 + s2 :]
        one = sum(x[0:2, :] for x in ones)
        two = sum(x[0:2, :] for x in twos)
        cols = jnp.concatenate([one, two, jnp.zeros((124, width), F32)], axis=0)
        cols_ref[...] = jnp.transpose(cols).astype(BF)

        @pl.loop(0, width // 256)
        def _(i):
            rr = pl.ds(pl.multiple_of(i * 256, 256), 256)
            for t, o in enumerate(outs):
                acc = None
                for x, y in zip(ls, cs):
                    piece = dot_tn(x[:, rr], y[:, t * local : (t + 1) * local])
                    acc = piece if acc is None else acc + piece
                o[rr, :local] = acc.astype(o.dtype)
                o[rr, local : local + 128] = cols_ref[rr, :].astype(o.dtype)
                o[rr, local + 128 :] = jnp.zeros((256, 64), o.dtype)

    ins = list(lows) + list(ctxs) + list(sums[0]) + list(sums[1])
    outs = [sds((width, local + 192), d) for d in (F32, BF)]
    return order.call(body, outs, ins, info, "grads_out", scratch=[VM((width, 128), BF)], **kw)


def grads_attn(order, info, tokens, pg_a, got_a, dq, mine, sent, got, split=True, **kw):
    width, local = tokens.shape[1], pg_a.shape[1] // 3
    full = 3 * local + -(3 * local) % 128

    def body(sc, tok, ma, ta, q, m, s, g, *outs):
        *outs, whole, here, there = outs
        here[:, :local] = q[0]
        here[:, local:] = (m[0] + g[CHUNK : 2 * CHUNK, :].astype(F32)).astype(BF)
        for k in range(2):
            there[k * 128 : (k + 1) * 128, :local] = g[3 * CHUNK :, k * local : (k + 1) * local]
        there[:, local:] = (s[2 * CHUNK : 3 * CHUNK, :].astype(F32) + g[:CHUNK, :].astype(F32)).astype(BF)
        at = {k: pl.ds(first_row(sc, *k), rows_of(k[0])) for k in (("a", False), ("c", False), ("a", True), ("c", True))}
        pairs = [(at["a", False], ma), (at["c", False], here), (at["a", True], ta), (at["c", True], there)]

        @pl.loop(0, width // 256)
        def _(i):
            rr = pl.ds(pl.multiple_of(i * 256, 256), 256)
            whole[rr, : 3 * local] = sum(dot_tn(tok[rows, rr], ref[:, : 3 * local]) for rows, ref in pairs)
            whole[rr, 3 * local :] = jnp.zeros((256, full - 3 * local), F32)

        if split:
            split_sides(sc, whole, outs[1], outs[0])
        else:
            outs[0][...] = whole[...]

    outs = [sds((width // 2, full), d) for d in (F32, BF)] if split else sds((width, full), F32)
    scratch = [VM((width, full), F32), VM((CHUNK, 3 * local), BF), VM((CHUNK, 3 * local), BF)]
    return order.call(body, outs, [tokens, pg_a, got_a, dq, mine, sent, got], info, "grads_attn", scratch=scratch, **kw)


def fold_both(order, info, mine, there, name, **kw):
    def body(sc, a, b, here, away, whole):
        whole[...] = a[...] + b[...].astype(F32)
        split_sides(sc, whole, away, here)

    rows, width = mine.shape
    outs = [sds((rows // 2, width), d) for d in (F32, BF)]
    return order.call(body, outs, [mine, there], info, name, scratch=[VM((rows, width), F32)], **kw)


def fold_pair(order, info, mine, there, name, **kw):
    height, width = mine.shape[0] // 4, mine.shape[1]

    def body(sc, a, b, here, away):
        level = lax.shift_right_logical(sc[1], 1)
        for out, ks in ((away, (1, 3)), (here, (0, 2))):
            for i, k in enumerate(ks):
                at = pl.ds(pl.multiple_of(jnp.bitwise_xor(level, k) * height, 16), height)
                out[i * height : (i + 1) * height, :] = (a[at, :] + b[at, :].astype(F32)).astype(out.dtype)

    return order.call(body, [sds((2 * height, width), F32), sds((2 * height, width))], [mine, there], info, name, **kw)


def fold_last(order, info, mine, there, name, **kw):
    height, width = mine.shape[0] // 2, mine.shape[1]

    def body(sc, a, b, here, away):
        away[...] = (a[height:, :] + b[height:, :].astype(F32)).astype(BF)
        here[...] = a[:height, :] + b[:height, :].astype(F32)

    return order.call(body, [sds((height, width), F32), sds((height, width))], [mine, there], info, name, **kw)


def add_rows(order, info, groups, name, **kw):
    def body(sc, *refs):
        at = 0
        for k in range(len(groups)):
            a, b, c = refs[3 * k : 3 * k + 3]
            refs[-1][at : at + a.shape[0], :] = a[...] + (b[...].astype(F32) + c[...].astype(F32))
            at += a.shape[0]

    rows = sum(g[0].shape[0] for g in groups)
    return order.call(body, sds((rows, groups[0][0].shape[1]), F32), [x for g in groups for x in g], info, name, **kw)


def lay_rows(order, info, mine, there, name, **kw):
    pieces = []
    for g, arrays in enumerate((mine, there)):
        i = 0
        for n, x in enumerate(arrays):
            for r in range(0, x.shape[0], CHUNK):
                pieces.append((g, g * len(mine) + n, r, i))
                i += 1
    count, arrays = len(pieces), list(mine) + list(there)
    width = mine[0].shape[1]

    def body(sc, *refs):
        out, sems = refs[len(arrays)], refs[len(arrays) + 1]
        copies = []
        for k, (g, n, r, i) in enumerate(pieces):
            half = low_of(sc) if g == 0 else 1 - low_of(sc)
            row = (2 * half + i) * CHUNK if i < 2 else (4 + half) * CHUNK
            at = pl.ds(pl.multiple_of(row, CHUNK), CHUNK)
            copies.append(pltpu.make_async_copy(refs[n].at[r : r + CHUNK, :], out.at[at, :], sems.at[k]))
            copies[-1].start()
        for c in copies:
            c.wait()

    outs = sds((count * CHUNK, width), mine[0].dtype)
    return order.call(body, outs, arrays, info, name, scratch=[pltpu.SemaphoreType.DMA((count,))], raw_out=True, **kw)


def update(order, rates, groups, items, name, **kw):
    arrays = [x for it in items for x in it[:3]]
    shapes = [sds(it[0].shape, d) for it in items for d in (F32, F32, F32, BF)]
    pieces = [p for g in groups for p in g]

    def body(sc, *refs):
        ins = refs[len(pieces) : len(pieces) + len(arrays)]
        outs = refs[len(pieces) + len(arrays) :]
        rate, fix_one, fix_two = sc[0], sc[1], sc[2]
        for n, it in enumerate(items):
            w, m, v = ins[3 * n : 3 * n + 3]
            for index, group, first, count, turned in it[4]:
                lanes = slice(first, first + count)
                g = refs[2 * group][:, lanes] + refs[2 * group + 1][:, lanes].astype(F32)
                if turned:
                    g = jnp.transpose(g)[: w.shape[0], :]
                res = adamw_update(g, w[index], m[index], v[index], rate, fix_one, fix_two, it[3])
                for r, o in zip(res, outs[4 * n : 4 * n + 4]):
                    o[index] = r

    return order.call(body, shapes, pieces + arrays, rates, name, **kw)


def swap(x, axis, size, bit):
    return lax.ppermute(x, axis, [(i, i ^ bit) for i in range(size)])


def solution(mesh):
    dp_size = mesh.shape["dp"]
    t_size = mesh.shape["tensor"]

    def core_swap(x):
        return swap(x, "tensor", t_size, 1)

    def far_swap(x):
        return swap(x, "tensor", t_size, 2)

    def dp_swap(x, bit):
        return swap(x, "dp", dp_size, bit)

    def on_device(
        tokens, grad_out, token_weight, lengths, step, qkv_weight, out_weight, up_weight, down_weight,
        norm_params, first_qkv, first_out, first_up, first_down, first_norm, second_qkv, second_out,
        second_up, second_down, second_norm,
    ):
        order = Order()
        rows_d, local = qkv_weight.shape[1], qkv_weight.shape[2]
        units = up_weight.shape[1]
        tok_count = tokens.shape[0]
        direct = dp_size == 8 and rows_d % 16 == 0
        places = jnp.stack([lax.axis_index("tensor"), lax.axis_index("dp")]).astype(jnp.int32)
        info = jnp.concatenate([places, lengths])
        weights = token_weight.reshape(tok_count // 128, 128)
        step_float = step[0].astype(F32)
        rate = PEAK_RATE * jnp.minimum(step_float / WARM_STEPS, (LAST_STEP - step_float) / (LAST_STEP - WARM_STEPS))
        fix_one = 1.0 - BETA_ONE**step_float
        fix_two = 1.0 - BETA_TWO**step_float
        rates = jnp.stack([rate, fix_one, fix_two])
        down_t = down_weight.T

        slots = (0, 2, 4, 6, 1, 3, 5, 7)
        if direct:
            pack_q, pack_o = pack(order, info, qkv_weight, out_weight)
            q_x = dp_swap(pack_q, 1)
            q_z = [dp_swap(pack_q, k) for k in (2, 4, 6)]
            pack_u = pack_more(order, info, up_weight, far_swap(pack_o), norm_params, warm=[tokens])
            q_near = stack(order, info, q_z, "stack_q", deps=[q_x])
            q_far = dp_swap(q_near, 1)
            u_four = stack(order, info, [pack_u] + [dp_swap(pack_u, k) for k in (2, 4, 6)], "stack_u")
            u_x = dp_swap(u_four, 1)
            q_own = place(order, info, [pack_q, q_near, q_x, q_far], slots, "place_q")
            q_oth = core_swap(q_own)
            d_one = dp_swap(down_t, 4)
        else:
            pad = jnp.zeros((rows_d, -(units + local) % 128 - 4), BF)
            pack_q = jnp.concatenate([qkv_weight[0], qkv_weight[1], qkv_weight[2], out_weight.T], axis=1)
            pack_u = jnp.concatenate([up_weight, far_swap(out_weight.T), norm_params.T, pad], axis=1)
            q_own, u_own, d_own = (lax.all_gather(x, "dp", axis=0, tiled=True) for x in (pack_q, pack_u, down_t))
            q_oth = core_swap(q_own)

        q_a, k_a, v_a, lse_a, ctx_a = attend(order, info, "a", tokens, q_own, q_oth, local, "attend_a")
        ctx_a_there = far_swap(ctx_a)
        if direct:
            d_two = stack(order, info, [down_t, d_one], "stack_d")
            d_z = dp_swap(d_two, 2)
        q_c, k_c, v_c, lse_c, ctx_c = attend(order, info, "c", tokens, q_own, q_oth, local, "attend_c")
        ctx_c_there = far_swap(ctx_c)
        if direct:
            d_four = stack(order, info, [d_two, d_z], "stack_d4")
            d_x = dp_swap(d_four, 1)
            u_own = place(order, info, [u_four, u_x], slots, "place_u", deps=[ctx_a_there])
        u_oth = core_swap(u_own)
        norms, o_here, o_low, o_high = settle(order, info, u_own, u_oth, q_own, q_oth, units, local)
        args = (o_low, o_high, u_own, u_oth, norms, units)
        normed_a, inv_a, slope_a, inner_a, sent_a = lift(order, info, "a", tokens, ctx_a, ctx_a_there, *args, "lift_a")
        if direct:
            d_own = place(order, info, [d_four, d_x], (0, 4, 2, 6, 1, 5, 3, 7), "place_d", warm=[grad_out, weights], deps=[ctx_c_there])
        d_oth = core_swap(d_own)
        normed_c, inv_c, slope_c, inner_c, sent_c = lift(order, info, "c", tokens, ctx_c, ctx_c_there, *args, "lift_c")
        part_c = drop(order, info, inner_c, sent_c, d_own, d_oth, "drop_c")
        part_c_there = [far_swap(p) for p in part_c]
        part_a = drop(order, info, inner_a, sent_a, d_own, d_oth, "drop_a")
        part_a_there = [far_swap(p) for p in part_a]
        got_hi_a, got_hi_c = core_swap(sent_a), core_swap(sent_c)
        args = (grad_out, weights, norms, u_own, u_oth, d_own, d_oth)
        res_c, two_c, up_c, fu_c, sums_c2, back_c = turn(
            order, info, "c", 0, normed_c, part_c[0], part_c_there[0], *args, slope_c, "turn_c", deps=[got_hi_a, got_hi_c])
        res_0, two_0, up_0, fu_0, sums_02, back_0 = turn(
            order, info, "a", 0, normed_a, part_a[0], part_a_there[0], *args, slope_a, "turn_0")
        result, two_1, up_1, fu_1, sums_12, back_a = turn(
            order, info, "a", CHUNK, normed_a, part_a[1], part_a_there[1], *args, slope_a, "turn_1", around=(res_0, res_c), before=back_0)
        back_a_there, back_c_there = far_swap(back_a), far_swap(back_c)
        fus = (fu_0, fu_1, fu_c)
        got_fus = [core_swap(x) for x in fus]
        width = tokens.shape[1]
        inners, sents = ((inner_a, 0), (inner_a, CHUNK), (inner_c, 0)), ((sent_a, 0), (sent_a, CHUNK), (sent_c, 0))
        gots = ((got_hi_a, 0), (got_hi_a, CHUNK), (got_hi_c, 0))
        pairs = [(f, 0, 0, x, r, 0) for f, (x, r) in zip(fus, inners)] + [(f, 0, 0, x, r, width) for f, (x, r) in zip(got_fus, gots)]
        grad_d = grads(order, info, pairs, width, units, "grads_d", split=direct)
        ups = (up_0, up_1, up_c)
        pairs = [(x, r, 0, u, 0, 0) for (x, r), u in zip(sents, ups)] + [(x, r, 0, f, 0, width) for (x, r), f in zip(gots, got_fus)]
        grad_u = grads(order, info, pairs, width, units, "grads_u", split=direct)
        res_there = core_swap(result)

        def second_fold(parts, name, **kw):
            here, away = fold_pair(order, info, *parts, "pair_" + name, **kw)
            return here, dp_swap(away, 2)

        def third_fold(pair, name, **kw):
            here, away = fold_last(order, info, *pair, "last_" + name, **kw)
            return here, dp_swap(away, 4)

        if direct:
            fold_d, fold_u = (grad_d[0], dp_swap(grad_d[1], 1)), (grad_u[0], dp_swap(grad_u[1], 1))
        if direct:
            fold_d = second_fold(fold_d, "d", deps=[back_a_there])
        one_a, low_a, pg_a, pg_a_oth, sums_a1, in_a = attend_back(
            order, info, "a", (two_0, two_1), back_a, back_a_there, normed_a, inv_a, norms, o_here, q_a, k_a, v_a, lse_a, (q_own, q_oth), local, "back_a")
        in_a_there = far_swap(in_a)
        got_a = core_swap(pg_a_oth)
        if direct:
            fold_d = third_fold(fold_d, "d")
        one_c, low_c, sums_c1, dq_c, kv_mine, sent = attend_back(
            order, info, "c", (two_c,), back_c, back_c_there, normed_c, inv_c, norms, o_here, q_c, k_c, v_c, lse_c, None, local, "back_c")
        got_c = core_swap(sent)
        if direct:
            fold_u = second_fold(fold_u, "u")
        out_mine, out_oth = grads_out(
            order, info, (low_a, low_c), (ctx_a, ctx_c), ((sums_a1, sums_c1), (sums_02, sums_12, sums_c2)), local)
        out_got = core_swap(out_oth)
        grad_a = grads_attn(order, info, tokens, pg_a, got_a, dq_c, kv_mine, sent, got_c, split=direct)
        everything = slice(None)
        if direct:
            fold_1 = grad_a[0], dp_swap(grad_a[1], 1)
            keep, send = fold_both(order, info, out_mine, out_got, "side_o")
            fold_2 = keep, dp_swap(send, 1)
        in_c = project_back(order, info, dq_c, kv_mine, got_c, q_own, q_oth, local, "project_c")
        in_c_there = far_swap(in_c)
        if direct:
            fold_u = third_fold(fold_u, "u")
            fold_1 = second_fold(fold_1, "qkv", deps=[fold_d[1]])
            fold_2 = second_fold(fold_2, "o", deps=[fold_u[1]])
            n_down = update(order, rates, [fold_d], [
                (down_t, first_down.T, second_down.T, DECAY_RATE, [(everything, 0, 0, units, False)])], "update_d")
            fold_1 = third_fold(fold_1, "qkv")
            n_up = update(order, rates, [fold_u], [
                (up_weight, first_up, second_up, DECAY_RATE, [(everything, 0, 0, units, False)])], "update_u")
            fold_2 = third_fold(fold_2, "o")
        gi = add_rows(order, info, [(one_a, in_a, in_a_there), (one_c, in_c, in_c_there)], "add_in")
        gi_there = core_swap(gi)
        res_full = lay_rows(order, info, [result], [res_there], "lay_out")
        input_grad = lay_rows(order, info, [gi], [gi_there], "lay_grad")
        if direct:
            res = update(order, rates, [fold_1, fold_2], [
                (qkv_weight, first_qkv, second_qkv, DECAY_RATE,
                 [(c, 0, c * local, local, False) for c in range(3)]),
                (out_weight, first_out, second_out, DECAY_RATE, [(everything, 1, 0, local, True)]),
                (norm_params, first_norm, second_norm, 0.0, [(everything, 1, local, 128, True)]),
            ], "update_a")
            n_down = [x.T for x in n_down]
            n_qkv, n_out, n_norm = res[:4], res[4:8], res[8:]
        if not direct:
            grad_o = out_mine + out_got.astype(F32)
            su, sd, sa, so = (
                lax.psum_scatter(x, "dp", scatter_dimension=0, tiled=True) for x in (grad_u, grad_d, grad_a, grad_o))
            rest = (rate, fix_one, fix_two)
            n_up = adamw_update(su, up_weight, first_up, second_up, *rest, DECAY_RATE)
            n_down = adamw_update(sd.T, down_weight, first_down, second_down, *rest, DECAY_RATE)
            sq = jnp.stack([sa[:, c * local : (c + 1) * local] for c in range(3)])
            n_qkv = adamw_update(sq, qkv_weight, first_qkv, second_qkv, *rest, DECAY_RATE)
            n_out = adamw_update(so[:, :local].T, out_weight, first_out, second_out, *rest, DECAY_RATE)
            n_norm = adamw_update(so[:, local : local + 4].T, norm_params, first_norm, second_norm, *rest, 0.0)
        return (res_full, input_grad, *n_qkv, *n_out, *n_up, *n_down, *n_norm)

    rows = P("dp", None)
    qkv, col, row, norm = P(None, "dp", "tensor"), P("tensor", "dp"), P("dp", "tensor"), P(None, "dp")
    params = (qkv, col, row, col, norm)
    return jax.shard_map(
        on_device,
        mesh=mesh,
        in_specs=(rows, rows, P("dp"), P("dp"), P()) + params * 3,
        out_specs=(rows, rows) + (qkv,) * 4 + (col,) * 4 + (row,) * 4 + (col,) * 4 + (norm,) * 4,
        check_vma=False,
    )
```

```python
import jax
import jax.numpy as jnp
from jax import lax
from jax.experimental import pallas as pl
from jax.experimental.pallas import tpu as pltpu
from jax.sharding import PartitionSpec as P

HD = 64
NORM_EPS = 1e-05
MASK_VALUE = -1000000000.0
BETA_ONE = 0.9
BETA_TWO = 0.95
ADAM_EPS = 1e-08
DECAY_RATE = 0.01
PEAK_RATE = 0.15
WARM_STEPS = 2.0
LAST_STEP = 40.0
BF = jnp.bfloat16
F32 = jnp.float32
VM = pltpu.VMEM
CHUNK = 256


def dot_nn(a, b):
    return lax.dot_general(a, b, (((1,), (0,)), ((), ())), preferred_element_type=F32)


def dot_nt(a, b):
    return lax.dot_general(a, b, (((1,), (1,)), ((), ())), preferred_element_type=F32)


def dot_tn(a, b):
    return lax.dot_general(a, b, (((0,), (0,)), ((), ())), preferred_element_type=F32)


def sds(shape, dtype=BF):
    return jax.ShapeDtypeStruct(shape, dtype)


class Order:
    def __init__(self):
        self.last = None

    def call(self, body, outs, ins, info, name, scratch=(), limit=12, raw_in=False, raw_out=False, deps=(), warm=(), free=False):
        ins = list(ins)
        n = len(ins) + 1
        specs = [pl.BlockSpec(memory_space=pltpu.SMEM)]
        specs += [pl.BlockSpec(memory_space=pltpu.HBM if raw_in else VM)] * len(ins)
        extra = list(warm) + list(deps) + ([] if self.last is None or free else [self.last])
        specs += [pl.BlockSpec(memory_space=VM)] * len(warm)
        specs += [pl.BlockSpec(memory_space=pl.ANY)] * (len(extra) - len(warm))

        single = not isinstance(outs, (list, tuple))
        shapes = ([outs] if single else list(outs)) + [sds((8, 128), F32)]
        specs_out = [pl.BlockSpec(memory_space=pltpu.HBM if raw_out else VM)] * (len(shapes) - 1) + [pl.BlockSpec(memory_space=VM)]
        token = n + len(extra) + len(shapes) - 1

        def run(*refs):
            body(*refs[:n], *refs[n + len(extra) : token], *refs[token + 1 :])
            refs[token][...] = jnp.zeros((8, 128), F32)

        res = pl.pallas_call(
            run,
            out_shape=shapes,
            in_specs=specs,
            out_specs=specs_out,
            scratch_shapes=list(scratch),
            compiler_params=pltpu.CompilerParams(vmem_limit_bytes=limit * 1024 * 1024),
            cost_estimate=pl.CostEstimate(flops=1, bytes_accessed=1, transcendentals=0),
            name=name,
        )(info, *ins, *extra)
        if not free:
            self.last = res[-1]
        return res[0] if single else list(res[:-1])


def low_of(info):
    return lax.rem(info[0], 2)


def rows_of(kind):
    return 2 * CHUNK if kind == "a" else CHUNK


def first_row(info, kind, other=False):
    low = 1 - low_of(info) if other else low_of(info)
    return pl.multiple_of(2 * low * CHUNK if kind == "a" else (4 + low) * CHUNK, CHUNK)


def used_of(info, kind):
    return info[2 + low_of(info)] if kind == "a" else info[4]


def by_chunk(rows, step):
    if rows == CHUNK:
        step(0)
    else:

        @pl.loop(0, rows // CHUNK)
        def _(r):
            step(pl.multiple_of(r * CHUNK, CHUNK))


def norm_stats(summed):
    center = summed - jnp.mean(summed, axis=-1, keepdims=True)
    inverse = lax.rsqrt(jnp.mean(center * center, axis=-1, keepdims=True) + NORM_EPS)
    return center * inverse, inverse


def norm_pull(upstream, normed, inverse, gain):
    scaled = upstream * gain
    return inverse * (
        scaled
        - jnp.mean(scaled, axis=-1, keepdims=True)
        - normed * jnp.mean(scaled * normed, axis=-1, keepdims=True)
    )


def gelu_parts(u):
    cdf = 0.5 * (1.0 + lax.erf(u * (0.5**0.5)))
    pdf = jnp.exp(-0.5 * u * u) * 0.3989422804014327
    return u * cdf, cdf + u * pdf


def adamw_update(gradient, weight_low, first, second, rate, fix_one, fix_two, decay):
    weight = weight_low.astype(F32)
    first_new = BETA_ONE * first + (1.0 - BETA_ONE) * gradient
    second_new = BETA_TWO * second + (1.0 - BETA_TWO) * gradient * gradient
    direction = first_new / fix_one / (jnp.sqrt(second_new / fix_two) + ADAM_EPS)
    weight_new = weight - rate * (direction + decay * weight)
    return (weight_new, first_new, second_new, weight_new.astype(BF))


def pack(order, info, qkv, out):
    rows, local = qkv.shape[1], qkv.shape[2]

    def body(sc, *refs):
        given, (pq, po), (q, o, sems) = refs[:2], refs[2:4], refs[4:]
        copies = [pltpu.make_async_copy(a, b, sems.at[k]) for k, (a, b) in enumerate(zip(given, (q, o)))]
        for c in copies:
            c.start()
        for c in copies:
            c.wait()
        for c in range(3):
            pq[:, c * local : (c + 1) * local] = q[c]
        turned = jnp.transpose(o[...].astype(F32)).astype(BF)
        pq[:, 3 * local :] = turned
        po[...] = turned

    ins = [qkv, out]
    scratch = [VM(x.shape, x.dtype) for x in ins] + [pltpu.SemaphoreType.DMA((2,))]
    return order.call(body, [sds((rows, 4 * local)), sds((rows, local))], ins, info, "pack", scratch=scratch, raw_in=True)


def pack_more(order, info, up, out_there, norm, **kw):
    rows, units, local = up.shape[0], up.shape[1], out_there.shape[1]
    pad = -(units + local) % 128

    def body(sc, u, o, n, p):
        p[:, :units] = u[...]
        p[:, units : units + local] = o[...]
        cols = jnp.concatenate([n[...].astype(F32), jnp.zeros((124, rows), F32)], axis=0)
        p[:, units + local :] = jnp.transpose(cols)[:, :pad].astype(BF)

    return order.call(body, sds((rows, units + local + pad)), [up, out_there, norm], info, "pack_more", **kw)


def stack(order, info, blocks, name, **kw):
    height, width = blocks[0].shape
    count = len(blocks)

    def body(sc, *refs):
        for k in range(count):
            refs[count][k * height : (k + 1) * height, :] = refs[k][...]

    return order.call(body, sds((count * height, width)), blocks, info, name, **kw)


def place(order, info, blocks, marks, name, **kw):
    count = len(marks)
    height, width = sum(b.shape[0] for b in blocks) // count, blocks[0].shape[1]
    n = len(blocks)

    def body(sc, *refs):
        k = 0
        for ref in refs[:n]:
            for r in range(0, ref.shape[0], height):
                at = pl.ds(pl.multiple_of(jnp.bitwise_xor(sc[1], marks[k]) * height, 16), height)
                refs[n][at, :] = ref[r : r + height, :]
                k += 1

    return order.call(body, sds((count * height, width)), blocks, info, name, **kw)


def settle(order, info, u_own, u_oth, q_own, q_oth, units, local, **kw):
    width = u_own.shape[0]
    top = (units + local) // 128 * 128
    row = units + local - top

    def body(sc, a, b, c, d, norms, here, low, high):
        norms[...] = jnp.transpose(a[:, top:].astype(F32))[row : row + 8, :]
        first = sc[0] < 2
        for k, (x, y) in enumerate(((c, a), (d, b))):
            lanes = slice(k * local, (k + 1) * local)
            x, y = x[:, 3 * local :], y[:, units : units + local]
            here[:, lanes] = x
            low[:, lanes] = jnp.where(first, x, y)
            high[:, lanes] = jnp.where(first, y, x)

    outs = [sds((8, width), F32)] + [sds((width, 2 * local))] * 3
    return order.call(body, outs, [u_own, u_oth, q_own, q_oth], info, "settle", **kw)


def attend(order, info, kind, tokens, w_own, w_oth, local, name, **kw):
    heads = local // HD
    both = 2 * local
    kv_rows = 2 * CHUNK
    rows = rows_of(kind)

    def body(sc, x_ref, w0, w1, q_ref, k_ref, v_ref, lse_ref, ctx_ref, part_ref):
        keys = lax.broadcasted_iota(jnp.int32, (1, kv_rows), 1)
        bias = jnp.where(keys < used_of(sc, kind), 0.0, MASK_VALUE)
        for t, w in enumerate((w0, w1)):
            if kind == "c":
                q_ref[t] = (dot_nn(x_ref[pl.ds(first_row(sc, kind), rows), :], w[:, :local]) * 0.125).astype(BF)
                p = dot_nn(x_ref[2 * kv_rows :, :], w[:, local : 3 * local])
                k_ref[t] = p[:, :local].astype(BF)
                v_ref[t] = p[:, local:].astype(BF)
            else:
                p = dot_nn(x_ref[pl.ds(first_row(sc, kind), rows), :], w[:, : 3 * local])
                q_ref[t] = (p[:, :local] * 0.125).astype(BF)
                k_ref[t] = p[:, local : 2 * local].astype(BF)
                v_ref[t] = p[:, 2 * local :].astype(BF)

        @pl.loop(0, 2 * (rows // CHUNK))
        def _(i):
            t = lax.rem(i, 2)
            at = pl.ds(pl.multiple_of(lax.div(i, 2) * CHUNK, CHUNK), CHUNK)
            for h in range(heads):
                lanes = slice(h * HD, (h + 1) * HD)
                s = dot_nt(q_ref[t, at, lanes], k_ref[t, :, lanes]) + bias
                top = jnp.max(s, axis=-1, keepdims=True)
                e = jnp.exp(s - top)
                total = jnp.sum(e, axis=-1, keepdims=True)
                part_ref[t, at, lanes] = dot_nn((e * (1.0 / total)).astype(BF), v_ref[t, :, lanes]).astype(BF)
                lse_ref[t, at, h : h + 1] = top + jnp.log(total)

        for t in range(2):
            ctx_ref[:, t * local : (t + 1) * local] = part_ref[t]

    outs = [sds((2, n, local)) for n in (rows, kv_rows, kv_rows)] + [sds((2, rows, 128), F32), sds((rows, both))]
    return order.call(body, outs, [tokens, w_own, w_oth], info, name, scratch=[VM((2, rows, local), BF)], **kw)


def lift(order, info, kind, tokens, ctx, there, o_low, o_high, u0, u1, norms, units, name, **kw):
    rows, width = rows_of(kind), tokens.shape[1]
    both = 2 * units

    def body(sc, tok, c0, c1, ol, oh, u0, u1, nr, normed_ref, inv_ref, slope_ref, own_ref, send_ref):
        first = sc[0] < 2
        top = first_row(sc, kind)

        def step(r):
            at = pl.ds(r, CHUNK)
            a, b = c0[at, :], c1[at, :]
            attn = dot_nt(jnp.where(first, a, b), ol[...]) + dot_nt(jnp.where(first, b, a), oh[...])
            normed, inverse = norm_stats(tok[pl.ds(pl.multiple_of(top + r, CHUNK), CHUNK), :].astype(F32) + attn)
            normed_ref[at, :] = normed
            inv_ref[at, :] = jnp.broadcast_to(inverse, (CHUNK, 128))
            send_ref[at, :width] = (normed * nr[0:1, :] + nr[1:2, :]).astype(BF)
            for t, u in enumerate((u0, u1)):
                for c in range(0, units, 256):
                    g, s = gelu_parts(dot_nn(send_ref[at, :width], u[:, c : c + 256]))
                    slope_ref[at, t * units + c : t * units + c + 256] = s
                    if t == 0:
                        own_ref[at, c : c + 256] = g.astype(BF)
                    else:
                        send_ref[at, width + c : width + c + 256] = g.astype(BF)

        by_chunk(rows, step)

    outs = [sds((rows, width), F32), sds((rows, 128), F32), sds((rows, both), F32), sds((rows, units)), sds((rows, width + units))]
    return order.call(body, outs, [tokens, ctx, there, o_low, o_high, u0, u1, norms], info, name, **kw)


def drop(order, info, own, sent, d0, d1, name, **kw):
    rows, width = own.shape[0], d0.shape[0]

    def body(sc, own_ref, sent_ref, d0, d1, *parts):
        for k, part_ref in enumerate(parts):
            at = slice(k * CHUNK, (k + 1) * CHUNK)
            part_ref[...] = (dot_nt(own_ref[at, :], d0[...]) + dot_nt(sent_ref[at, width:], d1[...])).astype(BF)

    return order.call(body, [sds((CHUNK, width))] * (rows // CHUNK), [own, sent, d0, d1], info, name, **kw)


def row_scale(info, weights, kind, r):
    length = used_of(info, kind)
    first = r if kind == "a" else low_of(info) * CHUNK
    top = lax.div(first_row(info, kind) + r, 128)
    slot = lax.broadcasted_iota(jnp.int32, (128, 128), 0)
    lane = lax.broadcasted_iota(jnp.int32, (128, 128), 1)
    cols = []
    for k in range(CHUNK // 128):
        keep = (slot == lane) & (slot + (first + k * 128) < length)
        cols.append(jnp.sum(jnp.where(keep, weights[pl.ds(top + k, 1), :], 0.0), axis=-1, keepdims=True))
    return jnp.concatenate(cols, axis=0)


def turn(order, info, kind, row, normed, part, there, go, weights, norms, u0, u1, d0, d1, slope, name, around=(), before=None, **kw):
    width = normed.shape[1]
    units = d0.shape[1]
    skip = around[0].shape[0] if around else 0
    total = skip + CHUNK + (around[1].shape[0] if around else 0)

    def body(sc, nm, g, sw, nr, u0, u1, d0, d1, sl, p0, p1, *refs):
        out_ref, two_ref, own_ref, send_ref, sums_ref, part_ref = refs[-6:]
        if around:
            out_ref[:skip, :] = refs[0][...]
            out_ref[skip + CHUNK :, :] = refs[1][...]
        at = slice(row, row + CHUNK)
        ffn = p0[...].astype(F32) + p1[...].astype(F32)
        n2, inv2 = norm_stats((nm[at, :] * nr[0:1, :] + nr[1:2, :]) + ffn)
        out_ref[skip : skip + CHUNK, :] = (n2 * nr[2:3, :] + nr[3:4, :]).astype(BF)
        up = g[pl.ds(pl.multiple_of(first_row(sc, kind) + row, CHUNK), CHUNK), :].astype(F32) * row_scale(sc, sw, kind, row)
        two = norm_pull(up, n2, inv2, nr[2:3, :])
        sums_ref[0:1, :] = jnp.sum(up * n2, axis=0, keepdims=True)
        sums_ref[1:2, :] = jnp.sum(up, axis=0, keepdims=True)
        two_ref[...] = two
        send_ref[:, :width] = two.astype(BF)
        acc = None
        for t, (u, d) in enumerate(((u0, d0), (u1, d1))):
            to, base = ((own_ref, 0), (send_ref, width))[t]
            for c in range(0, units, 256):
                lanes = slice(base + c, base + c + 256)
                steep = sl[at, t * units + c : t * units + c + 256]
                to[:, lanes] = (dot_nn(send_ref[:, :width], d[:, c : c + 256]) * steep).astype(BF)
                piece = dot_nt(to[:, lanes], u[:, c : c + 256])
                acc = piece if acc is None else acc + piece
        if before is None:
            part_ref[...] = acc.astype(BF)
        else:
            part_ref[:CHUNK, :] = refs[-7][...]
            part_ref[CHUNK:, :] = acc.astype(BF)

    outs = [sds((total, width)), sds((CHUNK, width), F32), sds((CHUNK, units)), sds((CHUNK, width + units))]
    outs += [sds((8, width), F32), sds((CHUNK if before is None else 2 * CHUNK, width))]
    ins = [normed, go, weights, norms, u0, u1, d0, d1, slope, part, there, *around] + ([] if before is None else [before])
    return order.call(body, outs, ins, info, name, **kw)


def split_sides(info, whole, away, here):
    side = lax.rem(info[1], 2)
    height = whole.shape[0] // 8
    for z in range(4):
        rows = slice(z * height, (z + 1) * height)
        for out, s in ((away, 1 - side), (here, side)):
            out[rows, :] = whole[pl.ds(pl.multiple_of((2 * z + s) * height, 16), height), :].astype(out.dtype)


def grads(order, info, pairs, width, units, name, split=True, **kw):
    flat = []
    for p in pairs:
        flat += [x for x in (p[0], p[3]) if not any(x is y for y in flat)]

    def place_of(x):
        return next(k for k, y in enumerate(flat) if x is y)


    def body(sc, *refs):
        ins, outs = refs[: len(flat)], refs[len(flat) :]
        whole = outs[-1]

        @pl.loop(0, width // 256)
        def _(i):
            acc = None
            for x, top, first, y, row, column in pairs:
                left = ins[place_of(x)][top : top + CHUNK, pl.ds(pl.multiple_of(first + i * 256, 256), 256)]
                piece = dot_tn(left, ins[place_of(y)][row : row + CHUNK, column : column + units])
                acc = piece if acc is None else acc + piece
            whole[pl.ds(pl.multiple_of(i * 256, 256), 256), :] = acc

        if split:
            split_sides(sc, whole, outs[1], outs[0])

    if split:
        outs, scratch = [sds((width // 2, units), d) for d in (F32, BF)], [VM((width, units), F32)]
    else:
        outs, scratch = sds((width, units), F32), []
    return order.call(body, outs, flat, info, name, scratch=scratch, **kw)


def attend_back(order, info, kind, two, part, there, normed, inverse, norms, o_here, q, k, v, lse, weights, local, name, **kw):
    heads = local // HD
    rows, kv_rows = q.shape[1], k.shape[1]
    width = norms.shape[1]
    whole = kind == "a"

    n = rows // CHUNK

    def body(sc, *refs):
        twos, p0, p1, refs = refs[:n], refs[n], refs[n + 1], refs[n + 2 :]
        nm, inv, nr, o_ref, q_ref, k_ref, v_ref, lse_ref, *refs = refs
        if whole:
            w0, w1, one_ref, low_ref, pg0, pg1, sums_ref, part_ref, cg_ref, kv_ref, lt_ref, dq_ref = refs
        else:
            one_ref, low_ref, sums_ref, dq_ref, mine_ref, send_ref, cg_ref, kv_ref, lt_ref = refs
        low = low_of(sc)
        sums_ref[...] = jnp.zeros((8, width), F32)
        keys = lax.broadcasted_iota(jnp.int32, (kv_rows, 1), 0)
        bias = jnp.where(keys < used_of(sc, kind), 0.0, MASK_VALUE)
        if whole:
            kv_ref[...] = jnp.zeros((2, kv_rows, 2 * local), F32)

        def step(r):
            at, i = slice(r, r + CHUNK), r // CHUNK
            nrm = nm[at, :]
            grad = twos[i][...] + (p0[at, :].astype(F32) + p1[at, :].astype(F32))
            sums_ref[0:1, :] += jnp.sum(grad * nrm, axis=0, keepdims=True)
            sums_ref[1:2, :] += jnp.sum(grad, axis=0, keepdims=True)
            one = norm_pull(grad, nrm, inv[at, :1], nr[0:1, :])
            one_ref[at, :] = one
            low_ref[at, :] = one.astype(BF)
            for t in range(2):
                cg_ref[t, at, :] = dot_nn(low_ref[at, :], o_ref[:, t * local : (t + 1) * local]).astype(BF)
                lt_ref[t, i] = jnp.transpose(lse_ref[t, at, :])[:8, :]

        for r in range(0, rows, CHUNK):
            step(r)

        def heads_of(r):
            at, i = pl.ds(r, CHUNK), lax.div(r, CHUNK)

            @pl.loop(0, 2)
            def _(t):
                for h in range(heads):
                    lanes = slice(h * HD, (h + 1) * HD)
                    qh, kh, cg = q_ref[t, at, lanes], k_ref[t, :, lanes], cg_ref[t, at, lanes]
                    p = jnp.exp(dot_nt(kh, qh) + bias - lt_ref[t, i, h : h + 1, :])
                    dp = dot_nt(v_ref[t, :, lanes], cg)
                    ds = (p * (dp - jnp.sum(dp * p, axis=0, keepdims=True))).astype(BF)
                    dv = dot_nn(p.astype(BF), cg)
                    dk = dot_nn(ds, qh)
                    dq_ref[t, at, lanes] = (dot_tn(ds, kh) * 0.125).astype(BF)
                    late = slice(local + h * HD, local + (h + 1) * HD)
                    if whole:
                        kv_ref[t, :, lanes] += dk
                        kv_ref[t, :, late] += dv
                    else:
                        kv_ref[t, :, lanes] = dk
                        kv_ref[t, :, late] = dv

        by_chunk(rows, heads_of)
        if whole:
            for t, pg in enumerate((pg0, pg1)):
                pg[:, :local] = dq_ref[t]
                pg[:, local : 3 * local] = kv_ref[t].astype(BF)
            pg1[:, 3 * local :] = jnp.zeros((rows, -(3 * local) % 128), BF)

            def last(r):
                at = pl.ds(r, CHUNK)
                acc = dot_nt(pg0[at, :], w0[:, : 3 * local]) + dot_nt(pg1[at, : 3 * local], w1[:, : 3 * local])
                part_ref[at, :] = acc.astype(BF)

            by_chunk(rows, last)
        else:
            own = pl.ds(pl.multiple_of(low * CHUNK, CHUNK), CHUNK)
            other = pl.ds(pl.multiple_of((1 - low) * CHUNK, CHUNK), CHUNK)
            for t in range(2):
                mine_ref[t] = kv_ref[t, own, :]
            for k, (t, at) in enumerate(((1, own), (1, other), (0, other))):
                send_ref[k * CHUNK : (k + 1) * CHUNK, :] = kv_ref[t, at, :].astype(BF)
            for k in range(2):
                send_ref[3 * CHUNK :, k * local : (k + 1) * local] = dq_ref[1, k * 128 : (k + 1) * 128, :]

    outs = [sds((rows, width), F32), sds((rows, width))]
    scratch = [VM((2, rows, local), BF), VM((2, kv_rows, 2 * local), F32), VM((2, n, 8, CHUNK), F32)]
    if whole:
        outs += [sds((rows, 3 * local)), sds((rows, 3 * local + -(3 * local) % 128)), sds((8, width), F32), sds((rows, width))]
        scratch += [VM((2, rows, local), BF)]
    else:
        outs += [sds((8, width), F32), sds((2, rows, local)), sds((2, CHUNK, 2 * local), F32), sds((3 * CHUNK + 128, 2 * local))]
    ins = [*two, part, there, normed, inverse, norms, o_here, q, k, v, lse] + (list(weights) if whole else [])
    return order.call(body, outs, ins, info, name, scratch=scratch, **kw)


def project_back(order, info, dq, mine, got, w_own, w_oth, local, name, **kw):
    rows, width = dq.shape[1], w_own.shape[0]

    def body(sc, dq_ref, a, g, w0, w1, part_ref, pg):
        acc = None
        for t, w in enumerate((w0, w1)):
            pg[:, :local] = dq_ref[t]
            pg[:, local:] = (a[t] + g[(t + 1) * CHUNK : (t + 2) * CHUNK, :].astype(F32)).astype(BF)
            piece = dot_nt(pg[...], w[:, : 3 * local])
            acc = piece if acc is None else acc + piece
        part_ref[...] = acc.astype(BF)

    scratch = [VM((rows, 3 * local), BF)]
    return order.call(body, sds((rows, width)), [dq, mine, got, w_own, w_oth], info, name, scratch=scratch, **kw)


def grads_out(order, info, lows, ctxs, sums, local, **kw):
    width = lows[0].shape[1]
    n, s1, s2 = len(lows), len(sums[0]), len(sums[1])

    def body(sc, *refs):
        ls, cs = refs[:n], refs[n : 2 * n]
        ones, twos = refs[2 * n : 2 * n + s1], refs[2 * n + s1 : 2 * n + s1 + s2]
        *outs, cols_ref = refs[2 * n + s1 + s2 :]
        one = sum(x[0:2, :] for x in ones)
        two = sum(x[0:2, :] for x in twos)
        cols = jnp.concatenate([one, two, jnp.zeros((124, width), F32)], axis=0)
        cols_ref[...] = jnp.transpose(cols).astype(BF)

        @pl.loop(0, width // 256)
        def _(i):
            rr = pl.ds(pl.multiple_of(i * 256, 256), 256)
            for t, o in enumerate(outs):
                acc = None
                for x, y in zip(ls, cs):
                    piece = dot_tn(x[:, rr], y[:, t * local : (t + 1) * local])
                    acc = piece if acc is None else acc + piece
                o[rr, :local] = acc.astype(o.dtype)
                o[rr, local : local + 128] = cols_ref[rr, :].astype(o.dtype)
                o[rr, local + 128 :] = jnp.zeros((256, 64), o.dtype)

    ins = list(lows) + list(ctxs) + list(sums[0]) + list(sums[1])
    outs = [sds((width, local + 192), d) for d in (F32, BF)]
    return order.call(body, outs, ins, info, "grads_out", scratch=[VM((width, 128), BF)], **kw)


def grads_attn(order, info, tokens, pg_a, got_a, dq, mine, sent, got, split=True, **kw):
    width, local = tokens.shape[1], pg_a.shape[1] // 3
    full = 3 * local + -(3 * local) % 128

    def body(sc, tok, ma, ta, q, m, s, g, *outs):
        *outs, whole, here, there = outs
        here[:, :local] = q[0]
        here[:, local:] = (m[0] + g[CHUNK : 2 * CHUNK, :].astype(F32)).astype(BF)
        for k in range(2):
            there[k * 128 : (k + 1) * 128, :local] = g[3 * CHUNK :, k * local : (k + 1) * local]
        there[:, local:] = (s[2 * CHUNK : 3 * CHUNK, :].astype(F32) + g[:CHUNK, :].astype(F32)).astype(BF)
        at = {k: pl.ds(first_row(sc, *k), rows_of(k[0])) for k in (("a", False), ("c", False), ("a", True), ("c", True))}
        pairs = [(at["a", False], ma), (at["c", False], here), (at["a", True], ta), (at["c", True], there)]

        @pl.loop(0, width // 256)
        def _(i):
            rr = pl.ds(pl.multiple_of(i * 256, 256), 256)
            whole[rr, : 3 * local] = sum(dot_tn(tok[rows, rr], ref[:, : 3 * local]) for rows, ref in pairs)
            whole[rr, 3 * local :] = jnp.zeros((256, full - 3 * local), F32)

        if split:
            split_sides(sc, whole, outs[1], outs[0])
        else:
            outs[0][...] = whole[...]

    outs = [sds((width // 2, full), d) for d in (F32, BF)] if split else sds((width, full), F32)
    scratch = [VM((width, full), F32), VM((CHUNK, 3 * local), BF), VM((CHUNK, 3 * local), BF)]
    return order.call(body, outs, [tokens, pg_a, got_a, dq, mine, sent, got], info, "grads_attn", scratch=scratch, **kw)


def fold_both(order, info, mine, there, name, **kw):
    def body(sc, a, b, here, away, whole):
        whole[...] = a[...] + b[...].astype(F32)
        split_sides(sc, whole, away, here)

    rows, width = mine.shape
    outs = [sds((rows // 2, width), d) for d in (F32, BF)]
    return order.call(body, outs, [mine, there], info, name, scratch=[VM((rows, width), F32)], **kw)


def fold_pair(order, info, mine, there, name, **kw):
    height, width = mine.shape[0] // 4, mine.shape[1]

    def body(sc, a, b, here, away):
        level = lax.shift_right_logical(sc[1], 1)
        for out, ks in ((away, (1, 3)), (here, (0, 2))):
            for i, k in enumerate(ks):
                at = pl.ds(pl.multiple_of(jnp.bitwise_xor(level, k) * height, 16), height)
                out[i * height : (i + 1) * height, :] = (a[at, :] + b[at, :].astype(F32)).astype(out.dtype)

    return order.call(body, [sds((2 * height, width), F32), sds((2 * height, width))], [mine, there], info, name, **kw)


def fold_last(order, info, mine, there, name, **kw):
    height, width = mine.shape[0] // 2, mine.shape[1]

    def body(sc, a, b, here, away):
        away[...] = (a[height:, :] + b[height:, :].astype(F32)).astype(BF)
        here[...] = a[:height, :] + b[:height, :].astype(F32)

    return order.call(body, [sds((height, width), F32), sds((height, width))], [mine, there], info, name, **kw)


def add_rows(order, info, groups, name, **kw):
    def body(sc, *refs):
        at = 0
        for k in range(len(groups)):
            a, b, c = refs[3 * k : 3 * k + 3]
            refs[-1][at : at + a.shape[0], :] = a[...] + (b[...].astype(F32) + c[...].astype(F32))
            at += a.shape[0]

    rows = sum(g[0].shape[0] for g in groups)
    return order.call(body, sds((rows, groups[0][0].shape[1]), F32), [x for g in groups for x in g], info, name, **kw)


def lay_rows(order, info, mine, there, name, **kw):
    pieces = []
    for g, arrays in enumerate((mine, there)):
        i = 0
        for n, x in enumerate(arrays):
            for r in range(0, x.shape[0], CHUNK):
                pieces.append((g, g * len(mine) + n, r, i))
                i += 1
    count, arrays = len(pieces), list(mine) + list(there)
    width = mine[0].shape[1]

    def body(sc, *refs):
        out, sems = refs[len(arrays)], refs[len(arrays) + 1]
        copies = []
        for k, (g, n, r, i) in enumerate(pieces):
            half = low_of(sc) if g == 0 else 1 - low_of(sc)
            row = (2 * half + i) * CHUNK if i < 2 else (4 + half) * CHUNK
            at = pl.ds(pl.multiple_of(row, CHUNK), CHUNK)
            copies.append(pltpu.make_async_copy(refs[n].at[r : r + CHUNK, :], out.at[at, :], sems.at[k]))
            copies[-1].start()
        for c in copies:
            c.wait()

    outs = sds((count * CHUNK, width), mine[0].dtype)
    return order.call(body, outs, arrays, info, name, scratch=[pltpu.SemaphoreType.DMA((count,))], raw_out=True, **kw)


def update(order, rates, groups, items, name, **kw):
    arrays = [x for it in items for x in it[:3]]
    shapes = [sds(it[0].shape, d) for it in items for d in (F32, F32, F32, BF)]
    pieces = [p for g in groups for p in g]

    def body(sc, *refs):
        ins = refs[len(pieces) : len(pieces) + len(arrays)]
        outs = refs[len(pieces) + len(arrays) :]
        rate, fix_one, fix_two = sc[0], sc[1], sc[2]
        for n, it in enumerate(items):
            w, m, v = ins[3 * n : 3 * n + 3]
            for index, group, first, count, turned in it[4]:
                lanes = slice(first, first + count)
                g = refs[2 * group][:, lanes] + refs[2 * group + 1][:, lanes].astype(F32)
                if turned:
                    g = jnp.transpose(g)[: w.shape[0], :]
                res = adamw_update(g, w[index], m[index], v[index], rate, fix_one, fix_two, it[3])
                for r, o in zip(res, outs[4 * n : 4 * n + 4]):
                    o[index] = r

    return order.call(body, shapes, pieces + arrays, rates, name, **kw)


def swap(x, axis, size, bit):
    return lax.ppermute(x, axis, [(i, i ^ bit) for i in range(size)])


def solution(mesh):
    dp_size = mesh.shape["dp"]
    t_size = mesh.shape["tensor"]

    def core_swap(x):
        return swap(x, "tensor", t_size, 1)

    def far_swap(x):
        return swap(x, "tensor", t_size, 2)

    def dp_swap(x, bit):
        return swap(x, "dp", dp_size, bit)

    def on_device(
        tokens, grad_out, token_weight, lengths, step, qkv_weight, out_weight, up_weight, down_weight,
        norm_params, first_qkv, first_out, first_up, first_down, first_norm, second_qkv, second_out,
        second_up, second_down, second_norm,
    ):
        order = Order()
        rows_d, local = qkv_weight.shape[1], qkv_weight.shape[2]
        units = up_weight.shape[1]
        tok_count = tokens.shape[0]
        direct = dp_size == 8 and rows_d % 16 == 0
        places = jnp.stack([lax.axis_index("tensor"), lax.axis_index("dp")]).astype(jnp.int32)
        info = jnp.concatenate([places, lengths])
        weights = token_weight.reshape(tok_count // 128, 128)
        step_float = step[0].astype(F32)
        rate = PEAK_RATE * jnp.minimum(step_float / WARM_STEPS, (LAST_STEP - step_float) / (LAST_STEP - WARM_STEPS))
        fix_one = 1.0 - BETA_ONE**step_float
        fix_two = 1.0 - BETA_TWO**step_float
        rates = jnp.stack([rate, fix_one, fix_two])
        down_t = down_weight.T

        slots = (0, 2, 4, 6, 1, 3, 5, 7)
        if direct:
            pack_q, pack_o = pack(order, info, qkv_weight, out_weight)
            q_x = dp_swap(pack_q, 1)
            q_z = [dp_swap(pack_q, k) for k in (2, 4, 6)]
            pack_u = pack_more(order, info, up_weight, far_swap(pack_o), norm_params, warm=[tokens])
            q_near = stack(order, info, q_z, "stack_q", deps=[q_x])
            q_far = dp_swap(q_near, 1)
            u_four = stack(order, info, [pack_u] + [dp_swap(pack_u, k) for k in (2, 4, 6)], "stack_u")
            u_x = dp_swap(u_four, 1)
            q_own = place(order, info, [pack_q, q_near, q_x, q_far], slots, "place_q")
            q_oth = core_swap(q_own)
            d_one = dp_swap(down_t, 4)
        else:
            pad = jnp.zeros((rows_d, -(units + local) % 128 - 4), BF)
            pack_q = jnp.concatenate([qkv_weight[0], qkv_weight[1], qkv_weight[2], out_weight.T], axis=1)
            pack_u = jnp.concatenate([up_weight, far_swap(out_weight.T), norm_params.T, pad], axis=1)
            q_own, u_own, d_own = (lax.all_gather(x, "dp", axis=0, tiled=True) for x in (pack_q, pack_u, down_t))
            q_oth = core_swap(q_own)

        q_a, k_a, v_a, lse_a, ctx_a = attend(order, info, "a", tokens, q_own, q_oth, local, "attend_a")
        ctx_a_there = far_swap(ctx_a)
        if direct:
            d_two = stack(order, info, [down_t, d_one], "stack_d")
            d_z = dp_swap(d_two, 2)
        q_c, k_c, v_c, lse_c, ctx_c = attend(order, info, "c", tokens, q_own, q_oth, local, "attend_c")
        ctx_c_there = far_swap(ctx_c)
        if direct:
            d_four = stack(order, info, [d_two, d_z], "stack_d4")
            d_x = dp_swap(d_four, 1)
            u_own = place(order, info, [u_four, u_x], slots, "place_u", deps=[ctx_a_there])
        u_oth = core_swap(u_own)
        norms, o_here, o_low, o_high = settle(order, info, u_own, u_oth, q_own, q_oth, units, local)
        args = (o_low, o_high, u_own, u_oth, norms, units)
        normed_a, inv_a, slope_a, inner_a, sent_a = lift(order, info, "a", tokens, ctx_a, ctx_a_there, *args, "lift_a")
        if direct:
            d_own = place(order, info, [d_four, d_x], (0, 4, 2, 6, 1, 5, 3, 7), "place_d", warm=[grad_out, weights], deps=[ctx_c_there])
        d_oth = core_swap(d_own)
        normed_c, inv_c, slope_c, inner_c, sent_c = lift(order, info, "c", tokens, ctx_c, ctx_c_there, *args, "lift_c")
        part_c = drop(order, info, inner_c, sent_c, d_own, d_oth, "drop_c")
        part_c_there = [far_swap(p) for p in part_c]
        part_a = drop(order, info, inner_a, sent_a, d_own, d_oth, "drop_a")
        part_a_there = [far_swap(p) for p in part_a]
        got_hi_a, got_hi_c = core_swap(sent_a), core_swap(sent_c)
        args = (grad_out, weights, norms, u_own, u_oth, d_own, d_oth)
        res_c, two_c, up_c, fu_c, sums_c2, back_c = turn(
            order, info, "c", 0, normed_c, part_c[0], part_c_there[0], *args, slope_c, "turn_c", deps=[got_hi_a, got_hi_c])
        res_0, two_0, up_0, fu_0, sums_02, back_0 = turn(
            order, info, "a", 0, normed_a, part_a[0], part_a_there[0], *args, slope_a, "turn_0")
        result, two_1, up_1, fu_1, sums_12, back_a = turn(
            order, info, "a", CHUNK, normed_a, part_a[1], part_a_there[1], *args, slope_a, "turn_1", around=(res_0, res_c), before=back_0)
        back_a_there, back_c_there = far_swap(back_a), far_swap(back_c)
        fus = (fu_0, fu_1, fu_c)
        got_fus = [core_swap(x) for x in fus]
        width = tokens.shape[1]
        inners, sents = ((inner_a, 0), (inner_a, CHUNK), (inner_c, 0)), ((sent_a, 0), (sent_a, CHUNK), (sent_c, 0))
        gots = ((got_hi_a, 0), (got_hi_a, CHUNK), (got_hi_c, 0))
        pairs = [(f, 0, 0, x, r, 0) for f, (x, r) in zip(fus, inners)] + [(f, 0, 0, x, r, width) for f, (x, r) in zip(got_fus, gots)]
        grad_d = grads(order, info, pairs, width, units, "grads_d", split=direct)
        ups = (up_0, up_1, up_c)
        pairs = [(x, r, 0, u, 0, 0) for (x, r), u in zip(sents, ups)] + [(x, r, 0, f, 0, width) for (x, r), f in zip(gots, got_fus)]
        grad_u = grads(order, info, pairs, width, units, "grads_u", split=direct)
        res_there = core_swap(result)

        def second_fold(parts, name, **kw):
            here, away = fold_pair(order, info, *parts, "pair_" + name, **kw)
            return here, dp_swap(away, 2)

        def third_fold(pair, name, **kw):
            here, away = fold_last(order, info, *pair, "last_" + name, **kw)
            return here, dp_swap(away, 4)

        if direct:
            fold_d, fold_u = (grad_d[0], dp_swap(grad_d[1], 1)), (grad_u[0], dp_swap(grad_u[1], 1))
        if direct:
            fold_d = second_fold(fold_d, "d", deps=[back_a_there])
        one_a, low_a, pg_a, pg_a_oth, sums_a1, in_a = attend_back(
            order, info, "a", (two_0, two_1), back_a, back_a_there, normed_a, inv_a, norms, o_here, q_a, k_a, v_a, lse_a, (q_own, q_oth), local, "back_a")
        in_a_there = far_swap(in_a)
        got_a = core_swap(pg_a_oth)
        if direct:
            fold_d = third_fold(fold_d, "d")
        one_c, low_c, sums_c1, dq_c, kv_mine, sent = attend_back(
            order, info, "c", (two_c,), back_c, back_c_there, normed_c, inv_c, norms, o_here, q_c, k_c, v_c, lse_c, None, local, "back_c")
        got_c = core_swap(sent)
        if direct:
            fold_u = second_fold(fold_u, "u")
        out_mine, out_oth = grads_out(
            order, info, (low_a, low_c), (ctx_a, ctx_c), ((sums_a1, sums_c1), (sums_02, sums_12, sums_c2)), local)
        out_got = core_swap(out_oth)
        grad_a = grads_attn(order, info, tokens, pg_a, got_a, dq_c, kv_mine, sent, got_c, split=direct)
        everything = slice(None)
        if direct:
            fold_1 = grad_a[0], dp_swap(grad_a[1], 1)
            keep, send = fold_both(order, info, out_mine, out_got, "side_o")
            fold_2 = keep, dp_swap(send, 1)
        in_c = project_back(order, info, dq_c, kv_mine, got_c, q_own, q_oth, local, "project_c")
        in_c_there = far_swap(in_c)
        if direct:
            fold_u = third_fold(fold_u, "u")
            fold_1 = second_fold(fold_1, "qkv", deps=[fold_d[1]])
            fold_2 = second_fold(fold_2, "o")
            n_down = update(order, rates, [fold_d], [
                (down_t, first_down.T, second_down.T, DECAY_RATE, [(everything, 0, 0, units, False)])], "update_d")
            fold_1 = third_fold(fold_1, "qkv", deps=[fold_u[1]])
            fold_2 = third_fold(fold_2, "o")
        gi = add_rows(order, info, [(one_a, in_a, in_a_there), (one_c, in_c, in_c_there)], "add_in")
        gi_there = core_swap(gi)
        if direct:
            n_up = update(order, rates, [fold_u], [
                (up_weight, first_up, second_up, DECAY_RATE, [(everything, 0, 0, units, False)])], "update_u")
        res_full = lay_rows(order, info, [result], [res_there], "lay_out")
        input_grad = lay_rows(order, info, [gi], [gi_there], "lay_grad")
        if direct:
            res = update(order, rates, [fold_1, fold_2], [
                (qkv_weight, first_qkv, second_qkv, DECAY_RATE,
                 [(c, 0, c * local, local, False) for c in range(3)]),
                (out_weight, first_out, second_out, DECAY_RATE, [(everything, 1, 0, local, True)]),
                (norm_params, first_norm, second_norm, 0.0, [(everything, 1, local, 128, True)]),
            ], "update_a")
            n_down = [x.T for x in n_down]
            n_qkv, n_out, n_norm = res[:4], res[4:8], res[8:]
        if not direct:
            grad_o = out_mine + out_got.astype(F32)
            su, sd, sa, so = (
                lax.psum_scatter(x, "dp", scatter_dimension=0, tiled=True) for x in (grad_u, grad_d, grad_a, grad_o))
            rest = (rate, fix_one, fix_two)
            n_up = adamw_update(su, up_weight, first_up, second_up, *rest, DECAY_RATE)
            n_down = adamw_update(sd.T, down_weight, first_down, second_down, *rest, DECAY_RATE)
            sq = jnp.stack([sa[:, c * local : (c + 1) * local] for c in range(3)])
            n_qkv = adamw_update(sq, qkv_weight, first_qkv, second_qkv, *rest, DECAY_RATE)
            n_out = adamw_update(so[:, :local].T, out_weight, first_out, second_out, *rest, DECAY_RATE)
            n_norm = adamw_update(so[:, local : local + 4].T, norm_params, first_norm, second_norm, *rest, 0.0)
        return (res_full, input_grad, *n_qkv, *n_out, *n_up, *n_down, *n_norm)

    rows = P("dp", None)
    qkv, col, row, norm = P(None, "dp", "tensor"), P("tensor", "dp"), P("dp", "tensor"), P(None, "dp")
    params = (qkv, col, row, col, norm)
    return jax.shard_map(
        on_device,
        mesh=mesh,
        in_specs=(rows, rows, P("dp"), P("dp"), P()) + params * 3,
        out_specs=(rows, rows) + (qkv,) * 4 + (col,) * 4 + (row,) * 4 + (col,) * 4 + (norm,) * 4,
        check_vma=False,
    )
```

```python
import jax
import jax.numpy as jnp
from jax import lax
from jax.experimental import pallas as pl
from jax.experimental.pallas import tpu as pltpu
from jax.sharding import PartitionSpec as P

HD = 64
NORM_EPS = 1e-05
MASK_VALUE = -1000000000.0
BETA_ONE = 0.9
BETA_TWO = 0.95
ADAM_EPS = 1e-08
DECAY_RATE = 0.01
PEAK_RATE = 0.15
WARM_STEPS = 2.0
LAST_STEP = 40.0
BF = jnp.bfloat16
F32 = jnp.float32
VM = pltpu.VMEM
CHUNK = 256


def dot_nn(a, b):
    return lax.dot_general(a, b, (((1,), (0,)), ((), ())), preferred_element_type=F32)


def dot_nt(a, b):
    return lax.dot_general(a, b, (((1,), (1,)), ((), ())), preferred_element_type=F32)


def dot_tn(a, b):
    return lax.dot_general(a, b, (((0,), (0,)), ((), ())), preferred_element_type=F32)


def sds(shape, dtype=BF):
    return jax.ShapeDtypeStruct(shape, dtype)


class Order:
    def __init__(self):
        self.last = None

    def call(self, body, outs, ins, info, name, scratch=(), limit=12, raw_in=False, raw_out=False, deps=(), warm=(), free=False, flops=1):
        ins = list(ins)
        n = len(ins) + 1
        specs = [pl.BlockSpec(memory_space=pltpu.SMEM)]
        specs += [pl.BlockSpec(memory_space=pltpu.HBM if raw_in else VM)] * len(ins)
        extra = list(warm) + list(deps) + ([] if self.last is None or free else [self.last])
        specs += [pl.BlockSpec(memory_space=VM)] * len(warm)
        specs += [pl.BlockSpec(memory_space=pl.ANY)] * (len(extra) - len(warm))

        single = not isinstance(outs, (list, tuple))
        shapes = ([outs] if single else list(outs)) + [sds((8, 128), F32)]
        specs_out = [pl.BlockSpec(memory_space=pltpu.HBM if raw_out else VM)] * (len(shapes) - 1) + [pl.BlockSpec(memory_space=VM)]
        token = n + len(extra) + len(shapes) - 1

        def run(*refs):
            body(*refs[:n], *refs[n + len(extra) : token], *refs[token + 1 :])
            refs[token][...] = jnp.zeros((8, 128), F32)

        res = pl.pallas_call(
            run,
            out_shape=shapes,
            in_specs=specs,
            out_specs=specs_out,
            scratch_shapes=list(scratch),
            compiler_params=pltpu.CompilerParams(vmem_limit_bytes=limit * 1024 * 1024),
            cost_estimate=pl.CostEstimate(flops=flops, bytes_accessed=1, transcendentals=0),
            name=name,
        )(info, *ins, *extra)
        if not free:
            self.last = res[-1]
        return res[0] if single else list(res[:-1])


def low_of(info):
    return lax.rem(info[0], 2)


def rows_of(kind):
    return 2 * CHUNK if kind == "a" else CHUNK


def first_row(info, kind, other=False):
    low = 1 - low_of(info) if other else low_of(info)
    return pl.multiple_of(2 * low * CHUNK if kind == "a" else (4 + low) * CHUNK, CHUNK)


def used_of(info, kind):
    return info[2 + low_of(info)] if kind == "a" else info[4]


def by_chunk(rows, step):
    if rows == CHUNK:
        step(0)
    else:

        @pl.loop(0, rows // CHUNK)
        def _(r):
            step(pl.multiple_of(r * CHUNK, CHUNK))


def norm_stats(summed):
    center = summed - jnp.mean(summed, axis=-1, keepdims=True)
    inverse = lax.rsqrt(jnp.mean(center * center, axis=-1, keepdims=True) + NORM_EPS)
    return center * inverse, inverse


def norm_pull(upstream, normed, inverse, gain):
    scaled = upstream * gain
    return inverse * (
        scaled
        - jnp.mean(scaled, axis=-1, keepdims=True)
        - normed * jnp.mean(scaled * normed, axis=-1, keepdims=True)
    )


def gelu_parts(u):
    cdf = 0.5 * (1.0 + lax.erf(u * (0.5**0.5)))
    pdf = jnp.exp(-0.5 * u * u) * 0.3989422804014327
    return u * cdf, cdf + u * pdf


def adamw_update(gradient, weight_low, first, second, rate, fix_one, fix_two, decay):
    weight = weight_low.astype(F32)
    first_new = BETA_ONE * first + (1.0 - BETA_ONE) * gradient
    second_new = BETA_TWO * second + (1.0 - BETA_TWO) * gradient * gradient
    direction = first_new / fix_one / (jnp.sqrt(second_new / fix_two) + ADAM_EPS)
    weight_new = weight - rate * (direction + decay * weight)
    return (weight_new, first_new, second_new, weight_new.astype(BF))


def pack(order, info, qkv, out):
    rows, local = qkv.shape[1], qkv.shape[2]

    def body(sc, *refs):
        given, (pq, po), (q, o, sems) = refs[:2], refs[2:4], refs[4:]
        copies = [pltpu.make_async_copy(a, b, sems.at[k]) for k, (a, b) in enumerate(zip(given, (q, o)))]
        for c in copies:
            c.start()
        for c in copies:
            c.wait()
        for c in range(3):
            pq[:, c * local : (c + 1) * local] = q[c]
        turned = jnp.transpose(o[...].astype(F32)).astype(BF)
        pq[:, 3 * local :] = turned
        po[...] = turned

    ins = [qkv, out]
    scratch = [VM(x.shape, x.dtype) for x in ins] + [pltpu.SemaphoreType.DMA((2,))]
    return order.call(body, [sds((rows, 4 * local)), sds((rows, local))], ins, info, "pack", scratch=scratch, raw_in=True)


def pack_more(order, info, up, out_there, norm, **kw):
    rows, units, local = up.shape[0], up.shape[1], out_there.shape[1]
    pad = -(units + local) % 128

    def body(sc, u, o, n, p):
        p[:, :units] = u[...]
        p[:, units : units + local] = o[...]
        cols = jnp.concatenate([n[...].astype(F32), jnp.zeros((124, rows), F32)], axis=0)
        p[:, units + local :] = jnp.transpose(cols)[:, :pad].astype(BF)

    return order.call(body, sds((rows, units + local + pad)), [up, out_there, norm], info, "pack_more", **kw)


def stack(order, info, blocks, name, **kw):
    height, width = blocks[0].shape
    count = len(blocks)

    def body(sc, *refs):
        for k in range(count):
            refs[count][k * height : (k + 1) * height, :] = refs[k][...]

    return order.call(body, sds((count * height, width)), blocks, info, name, **kw)


def place(order, info, blocks, marks, name, **kw):
    count = len(marks)
    height, width = sum(b.shape[0] for b in blocks) // count, blocks[0].shape[1]
    n = len(blocks)

    def body(sc, *refs):
        k = 0
        for ref in refs[:n]:
            for r in range(0, ref.shape[0], height):
                at = pl.ds(pl.multiple_of(jnp.bitwise_xor(sc[1], marks[k]) * height, 16), height)
                refs[n][at, :] = ref[r : r + height, :]
                k += 1

    return order.call(body, sds((count * height, width)), blocks, info, name, **kw)


def settle(order, info, u_own, u_oth, q_own, q_oth, units, local, **kw):
    width = u_own.shape[0]
    top = (units + local) // 128 * 128
    row = units + local - top

    def body(sc, a, b, c, d, norms, here, low, high):
        norms[...] = jnp.transpose(a[:, top:].astype(F32))[row : row + 8, :]
        first = sc[0] < 2
        for k, (x, y) in enumerate(((c, a), (d, b))):
            lanes = slice(k * local, (k + 1) * local)
            x, y = x[:, 3 * local :], y[:, units : units + local]
            here[:, lanes] = x
            low[:, lanes] = jnp.where(first, x, y)
            high[:, lanes] = jnp.where(first, y, x)

    outs = [sds((8, width), F32)] + [sds((width, 2 * local))] * 3
    return order.call(body, outs, [u_own, u_oth, q_own, q_oth], info, "settle", **kw)


def attend(order, info, kind, tokens, w_own, w_oth, local, name, **kw):
    heads = local // HD
    both = 2 * local
    kv_rows = 2 * CHUNK
    rows = rows_of(kind)

    def body(sc, x_ref, w0, w1, q_ref, k_ref, v_ref, lse_ref, ctx_ref, part_ref):
        keys = lax.broadcasted_iota(jnp.int32, (1, kv_rows), 1)
        bias = jnp.where(keys < used_of(sc, kind), 0.0, MASK_VALUE)
        for t, w in enumerate((w0, w1)):
            if kind == "c":
                q_ref[t] = (dot_nn(x_ref[pl.ds(first_row(sc, kind), rows), :], w[:, :local]) * 0.125).astype(BF)
                p = dot_nn(x_ref[2 * kv_rows :, :], w[:, local : 3 * local])
                k_ref[t] = p[:, :local].astype(BF)
                v_ref[t] = p[:, local:].astype(BF)
            else:
                p = dot_nn(x_ref[pl.ds(first_row(sc, kind), rows), :], w[:, : 3 * local])
                q_ref[t] = (p[:, :local] * 0.125).astype(BF)
                k_ref[t] = p[:, local : 2 * local].astype(BF)
                v_ref[t] = p[:, 2 * local :].astype(BF)

        @pl.loop(0, 2 * (rows // CHUNK))
        def _(i):
            t = lax.rem(i, 2)
            at = pl.ds(pl.multiple_of(lax.div(i, 2) * CHUNK, CHUNK), CHUNK)
            for h in range(heads):
                lanes = slice(h * HD, (h + 1) * HD)
                s = dot_nt(q_ref[t, at, lanes], k_ref[t, :, lanes]) + bias
                top = jnp.max(s, axis=-1, keepdims=True)
                e = jnp.exp(s - top)
                total = jnp.sum(e, axis=-1, keepdims=True)
                part_ref[t, at, lanes] = dot_nn((e * (1.0 / total)).astype(BF), v_ref[t, :, lanes]).astype(BF)
                lse_ref[t, at, h : h + 1] = top + jnp.log(total)

        for t in range(2):
            ctx_ref[:, t * local : (t + 1) * local] = part_ref[t]

    outs = [sds((2, n, local)) for n in (rows, kv_rows, kv_rows)] + [sds((2, rows, 128), F32), sds((rows, both))]
    return order.call(body, outs, [tokens, w_own, w_oth], info, name, scratch=[VM((2, rows, local), BF)], **kw)


def lift(order, info, kind, tokens, ctx, there, o_low, o_high, u0, u1, norms, units, name, **kw):
    rows, width = rows_of(kind), tokens.shape[1]
    both = 2 * units

    def body(sc, tok, c0, c1, ol, oh, u0, u1, nr, normed_ref, inv_ref, slope_ref, own_ref, send_ref):
        first = sc[0] < 2
        top = first_row(sc, kind)

        def step(r):
            at = pl.ds(r, CHUNK)
            a, b = c0[at, :], c1[at, :]
            attn = dot_nt(jnp.where(first, a, b), ol[...]) + dot_nt(jnp.where(first, b, a), oh[...])
            normed, inverse = norm_stats(tok[pl.ds(pl.multiple_of(top + r, CHUNK), CHUNK), :].astype(F32) + attn)
            normed_ref[at, :] = normed
            inv_ref[at, :] = jnp.broadcast_to(inverse, (CHUNK, 128))
            send_ref[at, :width] = (normed * nr[0:1, :] + nr[1:2, :]).astype(BF)
            for t, u in enumerate((u0, u1)):
                for c in range(0, units, 256):
                    g, s = gelu_parts(dot_nn(send_ref[at, :width], u[:, c : c + 256]))
                    slope_ref[at, t * units + c : t * units + c + 256] = s
                    if t == 0:
                        own_ref[at, c : c + 256] = g.astype(BF)
                    else:
                        send_ref[at, width + c : width + c + 256] = g.astype(BF)

        by_chunk(rows, step)

    outs = [sds((rows, width), F32), sds((rows, 128), F32), sds((rows, both), F32), sds((rows, units)), sds((rows, width + units))]
    return order.call(body, outs, [tokens, ctx, there, o_low, o_high, u0, u1, norms], info, name, **kw)


def drop(order, info, own, sent, d0, d1, name, **kw):
    rows, width = own.shape[0], d0.shape[0]

    def body(sc, own_ref, sent_ref, d0, d1, *parts):
        for k, part_ref in enumerate(parts):
            at = slice(k * CHUNK, (k + 1) * CHUNK)
            part_ref[...] = (dot_nt(own_ref[at, :], d0[...]) + dot_nt(sent_ref[at, width:], d1[...])).astype(BF)

    return order.call(body, [sds((CHUNK, width))] * (rows // CHUNK), [own, sent, d0, d1], info, name, **kw)


def row_scale(info, weights, kind, r):
    length = used_of(info, kind)
    first = r if kind == "a" else low_of(info) * CHUNK
    top = lax.div(first_row(info, kind) + r, 128)
    slot = lax.broadcasted_iota(jnp.int32, (128, 128), 0)
    lane = lax.broadcasted_iota(jnp.int32, (128, 128), 1)
    cols = []
    for k in range(CHUNK // 128):
        keep = (slot == lane) & (slot + (first + k * 128) < length)
        cols.append(jnp.sum(jnp.where(keep, weights[pl.ds(top + k, 1), :], 0.0), axis=-1, keepdims=True))
    return jnp.concatenate(cols, axis=0)


def turn(order, info, kind, row, normed, part, there, go, weights, norms, u0, u1, d0, d1, slope, name, around=(), before=None, **kw):
    width = normed.shape[1]
    units = d0.shape[1]
    skip = around[0].shape[0] if around else 0
    total = skip + CHUNK + (around[1].shape[0] if around else 0)

    def body(sc, nm, g, sw, nr, u0, u1, d0, d1, sl, p0, p1, *refs):
        out_ref, two_ref, own_ref, send_ref, sums_ref, part_ref = refs[-6:]
        if around:
            out_ref[:skip, :] = refs[0][...]
            out_ref[skip + CHUNK :, :] = refs[1][...]
        at = slice(row, row + CHUNK)
        ffn = p0[...].astype(F32) + p1[...].astype(F32)
        n2, inv2 = norm_stats((nm[at, :] * nr[0:1, :] + nr[1:2, :]) + ffn)
        out_ref[skip : skip + CHUNK, :] = (n2 * nr[2:3, :] + nr[3:4, :]).astype(BF)
        up = g[pl.ds(pl.multiple_of(first_row(sc, kind) + row, CHUNK), CHUNK), :].astype(F32) * row_scale(sc, sw, kind, row)
        two = norm_pull(up, n2, inv2, nr[2:3, :])
        sums_ref[0:1, :] = jnp.sum(up * n2, axis=0, keepdims=True)
        sums_ref[1:2, :] = jnp.sum(up, axis=0, keepdims=True)
        two_ref[...] = two
        send_ref[:, :width] = two.astype(BF)
        acc = None
        for t, (u, d) in enumerate(((u0, d0), (u1, d1))):
            to, base = ((own_ref, 0), (send_ref, width))[t]
            for c in range(0, units, 256):
                lanes = slice(base + c, base + c + 256)
                steep = sl[at, t * units + c : t * units + c + 256]
                to[:, lanes] = (dot_nn(send_ref[:, :width], d[:, c : c + 256]) * steep).astype(BF)
                piece = dot_nt(to[:, lanes], u[:, c : c + 256])
                acc = piece if acc is None else acc + piece
        if before is None:
            part_ref[...] = acc.astype(BF)
        else:
            part_ref[:CHUNK, :] = refs[-7][...]
            part_ref[CHUNK:, :] = acc.astype(BF)

    outs = [sds((total, width)), sds((CHUNK, width), F32), sds((CHUNK, units)), sds((CHUNK, width + units))]
    outs += [sds((8, width), F32), sds((CHUNK if before is None else 2 * CHUNK, width))]
    ins = [normed, go, weights, norms, u0, u1, d0, d1, slope, part, there, *around] + ([] if before is None else [before])
    return order.call(body, outs, ins, info, name, **kw)


def split_sides(info, whole, away, here):
    side = lax.rem(info[1], 2)
    height = whole.shape[0] // 8
    for z in range(4):
        rows = slice(z * height, (z + 1) * height)
        for out, s in ((away, 1 - side), (here, side)):
            out[rows, :] = whole[pl.ds(pl.multiple_of((2 * z + s) * height, 16), height), :].astype(out.dtype)


def grads(order, info, pairs, width, units, name, split=True, **kw):
    flat = []
    for p in pairs:
        flat += [x for x in (p[0], p[3]) if not any(x is y for y in flat)]

    def place_of(x):
        return next(k for k, y in enumerate(flat) if x is y)


    def body(sc, *refs):
        ins, outs = refs[: len(flat)], refs[len(flat) :]
        whole = outs[-1]

        @pl.loop(0, width // 256)
        def _(i):
            acc = None
            for x, top, first, y, row, column in pairs:
                left = ins[place_of(x)][top : top + CHUNK, pl.ds(pl.multiple_of(first + i * 256, 256), 256)]
                piece = dot_tn(left, ins[place_of(y)][row : row + CHUNK, column : column + units])
                acc = piece if acc is None else acc + piece
            whole[pl.ds(pl.multiple_of(i * 256, 256), 256), :] = acc

        if split:
            split_sides(sc, whole, outs[1], outs[0])

    if split:
        outs, scratch = [sds((width // 2, units), d) for d in (F32, BF)], [VM((width, units), F32)]
    else:
        outs, scratch = sds((width, units), F32), []
    return order.call(body, outs, flat, info, name, scratch=scratch, **kw)


def attend_back(order, info, kind, two, part, there, normed, inverse, norms, o_here, q, k, v, lse, weights, local, name, **kw):
    heads = local // HD
    rows, kv_rows = q.shape[1], k.shape[1]
    width = norms.shape[1]
    whole = kind == "a"

    n = rows // CHUNK

    def body(sc, *refs):
        twos, p0, p1, refs = refs[:n], refs[n], refs[n + 1], refs[n + 2 :]
        nm, inv, nr, o_ref, q_ref, k_ref, v_ref, lse_ref, *refs = refs
        if whole:
            w0, w1, one_ref, low_ref, pg0, pg1, sums_ref, part_ref, cg_ref, kv_ref, lt_ref, dq_ref = refs
        else:
            one_ref, low_ref, sums_ref, dq_ref, mine_ref, send_ref, cg_ref, kv_ref, lt_ref = refs
        low = low_of(sc)
        sums_ref[...] = jnp.zeros((8, width), F32)
        keys = lax.broadcasted_iota(jnp.int32, (kv_rows, 1), 0)
        bias = jnp.where(keys < used_of(sc, kind), 0.0, MASK_VALUE)
        if whole:
            kv_ref[...] = jnp.zeros((2, kv_rows, 2 * local), F32)

        def step(r):
            at, i = slice(r, r + CHUNK), r // CHUNK
            nrm = nm[at, :]
            grad = twos[i][...] + (p0[at, :].astype(F32) + p1[at, :].astype(F32))
            sums_ref[0:1, :] += jnp.sum(grad * nrm, axis=0, keepdims=True)
            sums_ref[1:2, :] += jnp.sum(grad, axis=0, keepdims=True)
            one = norm_pull(grad, nrm, inv[at, :1], nr[0:1, :])
            one_ref[at, :] = one
            low_ref[at, :] = one.astype(BF)
            for t in range(2):
                cg_ref[t, at, :] = dot_nn(low_ref[at, :], o_ref[:, t * local : (t + 1) * local]).astype(BF)
                lt_ref[t, i] = jnp.transpose(lse_ref[t, at, :])[:8, :]

        for r in range(0, rows, CHUNK):
            step(r)

        def heads_of(r):
            at, i = pl.ds(r, CHUNK), lax.div(r, CHUNK)

            @pl.loop(0, 2)
            def _(t):
                for h in range(heads):
                    lanes = slice(h * HD, (h + 1) * HD)
                    qh, kh, cg = q_ref[t, at, lanes], k_ref[t, :, lanes], cg_ref[t, at, lanes]
                    p = jnp.exp(dot_nt(kh, qh) + bias - lt_ref[t, i, h : h + 1, :])
                    dp = dot_nt(v_ref[t, :, lanes], cg)
                    ds = (p * (dp - jnp.sum(dp * p, axis=0, keepdims=True))).astype(BF)
                    dv = dot_nn(p.astype(BF), cg)
                    dk = dot_nn(ds, qh)
                    dq_ref[t, at, lanes] = (dot_tn(ds, kh) * 0.125).astype(BF)
                    late = slice(local + h * HD, local + (h + 1) * HD)
                    if whole:
                        kv_ref[t, :, lanes] += dk
                        kv_ref[t, :, late] += dv
                    else:
                        kv_ref[t, :, lanes] = dk
                        kv_ref[t, :, late] = dv

        by_chunk(rows, heads_of)
        if whole:
            for t, pg in enumerate((pg0, pg1)):
                pg[:, :local] = dq_ref[t]
                pg[:, local : 3 * local] = kv_ref[t].astype(BF)
            pg1[:, 3 * local :] = jnp.zeros((rows, -(3 * local) % 128), BF)

            def last(r):
                at = pl.ds(r, CHUNK)
                acc = dot_nt(pg0[at, :], w0[:, : 3 * local]) + dot_nt(pg1[at, : 3 * local], w1[:, : 3 * local])
                part_ref[at, :] = acc.astype(BF)

            by_chunk(rows, last)
        else:
            own = pl.ds(pl.multiple_of(low * CHUNK, CHUNK), CHUNK)
            other = pl.ds(pl.multiple_of((1 - low) * CHUNK, CHUNK), CHUNK)
            for t in range(2):
                mine_ref[t] = kv_ref[t, own, :]
            for k, (t, at) in enumerate(((1, own), (1, other), (0, other))):
                send_ref[k * CHUNK : (k + 1) * CHUNK, :] = kv_ref[t, at, :].astype(BF)
            for k in range(2):
                send_ref[3 * CHUNK :, k * local : (k + 1) * local] = dq_ref[1, k * 128 : (k + 1) * 128, :]

    outs = [sds((rows, width), F32), sds((rows, width))]
    scratch = [VM((2, rows, local), BF), VM((2, kv_rows, 2 * local), F32), VM((2, n, 8, CHUNK), F32)]
    if whole:
        outs += [sds((rows, 3 * local)), sds((rows, 3 * local + -(3 * local) % 128)), sds((8, width), F32), sds((rows, width))]
        scratch += [VM((2, rows, local), BF)]
    else:
        outs += [sds((8, width), F32), sds((2, rows, local)), sds((2, CHUNK, 2 * local), F32), sds((3 * CHUNK + 128, 2 * local))]
    ins = [*two, part, there, normed, inverse, norms, o_here, q, k, v, lse] + (list(weights) if whole else [])
    return order.call(body, outs, ins, info, name, scratch=scratch, **kw)


def project_back(order, info, dq, mine, got, w_own, w_oth, local, name, **kw):
    rows, width = dq.shape[1], w_own.shape[0]

    def body(sc, dq_ref, a, g, w0, w1, part_ref, pg):
        acc = None
        for t, w in enumerate((w0, w1)):
            pg[:, :local] = dq_ref[t]
            pg[:, local:] = (a[t] + g[(t + 1) * CHUNK : (t + 2) * CHUNK, :].astype(F32)).astype(BF)
            piece = dot_nt(pg[...], w[:, : 3 * local])
            acc = piece if acc is None else acc + piece
        part_ref[...] = acc.astype(BF)

    scratch = [VM((rows, 3 * local), BF)]
    return order.call(body, sds((rows, width)), [dq, mine, got, w_own, w_oth], info, name, scratch=scratch, **kw)


def grads_out(order, info, lows, ctxs, sums, local, **kw):
    width = lows[0].shape[1]
    n, s1, s2 = len(lows), len(sums[0]), len(sums[1])

    def body(sc, *refs):
        ls, cs = refs[:n], refs[n : 2 * n]
        ones, twos = refs[2 * n : 2 * n + s1], refs[2 * n + s1 : 2 * n + s1 + s2]
        *outs, cols_ref = refs[2 * n + s1 + s2 :]
        one = sum(x[0:2, :] for x in ones)
        two = sum(x[0:2, :] for x in twos)
        cols = jnp.concatenate([one, two, jnp.zeros((124, width), F32)], axis=0)
        cols_ref[...] = jnp.transpose(cols).astype(BF)

        @pl.loop(0, width // 256)
        def _(i):
            rr = pl.ds(pl.multiple_of(i * 256, 256), 256)
            for t, o in enumerate(outs):
                acc = None
                for x, y in zip(ls, cs):
                    piece = dot_tn(x[:, rr], y[:, t * local : (t + 1) * local])
                    acc = piece if acc is None else acc + piece
                o[rr, :local] = acc.astype(o.dtype)
                o[rr, local : local + 128] = cols_ref[rr, :].astype(o.dtype)
                o[rr, local + 128 :] = jnp.zeros((256, 64), o.dtype)

    ins = list(lows) + list(ctxs) + list(sums[0]) + list(sums[1])
    outs = [sds((width, local + 192), d) for d in (F32, BF)]
    return order.call(body, outs, ins, info, "grads_out", scratch=[VM((width, 128), BF)], **kw)


def grads_attn(order, info, tokens, pg_a, got_a, dq, mine, sent, got, split=True, **kw):
    width, local = tokens.shape[1], pg_a.shape[1] // 3
    full = 3 * local + -(3 * local) % 128

    def body(sc, tok, ma, ta, q, m, s, g, *outs):
        *outs, whole, here, there = outs
        here[:, :local] = q[0]
        here[:, local:] = (m[0] + g[CHUNK : 2 * CHUNK, :].astype(F32)).astype(BF)
        for k in range(2):
            there[k * 128 : (k + 1) * 128, :local] = g[3 * CHUNK :, k * local : (k + 1) * local]
        there[:, local:] = (s[2 * CHUNK : 3 * CHUNK, :].astype(F32) + g[:CHUNK, :].astype(F32)).astype(BF)
        at = {k: pl.ds(first_row(sc, *k), rows_of(k[0])) for k in (("a", False), ("c", False), ("a", True), ("c", True))}
        pairs = [(at["a", False], ma), (at["c", False], here), (at["a", True], ta), (at["c", True], there)]

        @pl.loop(0, width // 256)
        def _(i):
            rr = pl.ds(pl.multiple_of(i * 256, 256), 256)
            whole[rr, : 3 * local] = sum(dot_tn(tok[rows, rr], ref[:, : 3 * local]) for rows, ref in pairs)
            whole[rr, 3 * local :] = jnp.zeros((256, full - 3 * local), F32)

        if split:
            split_sides(sc, whole, outs[1], outs[0])
        else:
            outs[0][...] = whole[...]

    outs = [sds((width // 2, full), d) for d in (F32, BF)] if split else sds((width, full), F32)
    scratch = [VM((width, full), F32), VM((CHUNK, 3 * local), BF), VM((CHUNK, 3 * local), BF)]
    return order.call(body, outs, [tokens, pg_a, got_a, dq, mine, sent, got], info, "grads_attn", scratch=scratch, **kw)


def fold_both(order, info, mine, there, name, **kw):
    def body(sc, a, b, here, away, whole):
        whole[...] = a[...] + b[...].astype(F32)
        split_sides(sc, whole, away, here)

    rows, width = mine.shape
    outs = [sds((rows // 2, width), d) for d in (F32, BF)]
    return order.call(body, outs, [mine, there], info, name, scratch=[VM((rows, width), F32)], **kw)


def fold_pair(order, info, mine, there, name, **kw):
    height, width = mine.shape[0] // 4, mine.shape[1]

    def body(sc, a, b, here, away):
        level = lax.shift_right_logical(sc[1], 1)
        for out, ks in ((away, (1, 3)), (here, (0, 2))):
            for i, k in enumerate(ks):
                at = pl.ds(pl.multiple_of(jnp.bitwise_xor(level, k) * height, 16), height)
                out[i * height : (i + 1) * height, :] = (a[at, :] + b[at, :].astype(F32)).astype(out.dtype)

    return order.call(body, [sds((2 * height, width), F32), sds((2 * height, width))], [mine, there], info, name, **kw)


def fold_last(order, info, mine, there, name, **kw):
    height, width = mine.shape[0] // 2, mine.shape[1]

    def body(sc, a, b, here, away):
        away[...] = (a[height:, :] + b[height:, :].astype(F32)).astype(BF)
        here[...] = a[:height, :] + b[:height, :].astype(F32)

    return order.call(body, [sds((height, width), F32), sds((height, width))], [mine, there], info, name, **kw)


def add_rows(order, info, groups, name, **kw):
    def body(sc, *refs):
        at = 0
        for k in range(len(groups)):
            a, b, c = refs[3 * k : 3 * k + 3]
            refs[-1][at : at + a.shape[0], :] = a[...] + (b[...].astype(F32) + c[...].astype(F32))
            at += a.shape[0]

    rows = sum(g[0].shape[0] for g in groups)
    return order.call(body, sds((rows, groups[0][0].shape[1]), F32), [x for g in groups for x in g], info, name, **kw)


def lay_rows(order, info, groups, name, **kw):
    arrays = [x for g in groups for x in g]
    count = 6 * len(groups)

    def body(sc, *refs):
        outs, sems = refs[len(arrays) : -1], refs[-1]
        copies = []
        for n in range(len(arrays)):
            half = 1 - low_of(sc) if n % 2 else low_of(sc)
            for i in range(3):
                row = (2 * half + i) * CHUNK if i < 2 else (4 + half) * CHUNK
                at = pl.ds(pl.multiple_of(row, CHUNK), CHUNK)
                part = refs[n].at[i * CHUNK : (i + 1) * CHUNK, :]
                copies.append(pltpu.make_async_copy(part, outs[n // 2].at[at, :], sems.at[3 * n + i]))
                copies[-1].start()
        for c in copies:
            c.wait()

    outs = [sds((6 * CHUNK, g[0].shape[1]), g[0].dtype) for g in groups]
    return order.call(body, outs, arrays, info, name, scratch=[pltpu.SemaphoreType.DMA((count,))], raw_out=True, **kw)


def update(order, rates, groups, items, name, **kw):
    arrays = [x for it in items for x in it[:3]]
    shapes = [sds(it[0].shape, d) for it in items for d in (F32, F32, F32, BF)]
    pieces = [p for g in groups for p in g]

    def body(sc, *refs):
        ins = refs[len(pieces) : len(pieces) + len(arrays)]
        outs = refs[len(pieces) + len(arrays) :]
        rate, fix_one, fix_two = sc[0], sc[1], sc[2]
        for n, it in enumerate(items):
            w, m, v = ins[3 * n : 3 * n + 3]
            for index, group, first, count, turned in it[4]:
                lanes = slice(first, first + count)
                g = refs[2 * group][:, lanes] + refs[2 * group + 1][:, lanes].astype(F32)
                if turned:
                    g = jnp.transpose(g)[: w.shape[0], :]
                res = adamw_update(g, w[index], m[index], v[index], rate, fix_one, fix_two, it[3])
                for r, o in zip(res, outs[4 * n : 4 * n + 4]):
                    o[index] = r

    return order.call(body, shapes, pieces + arrays, rates, name, **kw)


def swap(x, axis, size, bit):
    return lax.ppermute(x, axis, [(i, i ^ bit) for i in range(size)])


def solution(mesh):
    dp_size = mesh.shape["dp"]
    t_size = mesh.shape["tensor"]

    def core_swap(x):
        return swap(x, "tensor", t_size, 1)

    def far_swap(x):
        return swap(x, "tensor", t_size, 2)

    def dp_swap(x, bit):
        return swap(x, "dp", dp_size, bit)

    def on_device(
        tokens, grad_out, token_weight, lengths, step, qkv_weight, out_weight, up_weight, down_weight,
        norm_params, first_qkv, first_out, first_up, first_down, first_norm, second_qkv, second_out,
        second_up, second_down, second_norm,
    ):
        order = Order()
        rows_d, local = qkv_weight.shape[1], qkv_weight.shape[2]
        units = up_weight.shape[1]
        tok_count = tokens.shape[0]
        direct = dp_size == 8 and rows_d % 16 == 0
        places = jnp.stack([lax.axis_index("tensor"), lax.axis_index("dp")]).astype(jnp.int32)
        info = jnp.concatenate([places, lengths])
        weights = token_weight.reshape(tok_count // 128, 128)
        step_float = step[0].astype(F32)
        rate = PEAK_RATE * jnp.minimum(step_float / WARM_STEPS, (LAST_STEP - step_float) / (LAST_STEP - WARM_STEPS))
        fix_one = 1.0 - BETA_ONE**step_float
        fix_two = 1.0 - BETA_TWO**step_float
        rates = jnp.stack([rate, fix_one, fix_two])
        down_t = down_weight.T

        slots = (0, 2, 4, 6, 1, 3, 5, 7)
        if direct:
            pack_q, pack_o = pack(order, info, qkv_weight, out_weight)
            q_x = dp_swap(pack_q, 1)
            q_z = [dp_swap(pack_q, k) for k in (2, 4, 6)]
            pack_u = pack_more(order, info, up_weight, far_swap(pack_o), norm_params, warm=[tokens])
            q_near = stack(order, info, q_z, "stack_q", deps=[q_x])
            q_far = dp_swap(q_near, 1)
            u_four = stack(order, info, [pack_u] + [dp_swap(pack_u, k) for k in (2, 4, 6)], "stack_u")
            u_x = dp_swap(u_four, 1)
            q_own = place(order, info, [pack_q, q_near, q_x, q_far], slots, "place_q")
            q_oth = core_swap(q_own)
            d_one = dp_swap(down_t, 4)
        else:
            pad = jnp.zeros((rows_d, -(units + local) % 128 - 4), BF)
            pack_q = jnp.concatenate([qkv_weight[0], qkv_weight[1], qkv_weight[2], out_weight.T], axis=1)
            pack_u = jnp.concatenate([up_weight, far_swap(out_weight.T), norm_params.T, pad], axis=1)
            q_own, u_own, d_own = (lax.all_gather(x, "dp", axis=0, tiled=True) for x in (pack_q, pack_u, down_t))
            q_oth = core_swap(q_own)

        q_a, k_a, v_a, lse_a, ctx_a = attend(order, info, "a", tokens, q_own, q_oth, local, "attend_a")
        ctx_a_there = far_swap(ctx_a)
        if direct:
            d_two = stack(order, info, [down_t, d_one], "stack_d")
            d_z = dp_swap(d_two, 2)
        q_c, k_c, v_c, lse_c, ctx_c = attend(order, info, "c", tokens, q_own, q_oth, local, "attend_c")
        ctx_c_there = far_swap(ctx_c)
        if direct:
            d_four = stack(order, info, [d_two, d_z], "stack_d4")
            d_x = dp_swap(d_four, 1)
            u_own = place(order, info, [u_four, u_x], slots, "place_u", deps=[ctx_a_there])
        u_oth = core_swap(u_own)
        norms, o_here, o_low, o_high = settle(order, info, u_own, u_oth, q_own, q_oth, units, local)
        args = (o_low, o_high, u_own, u_oth, norms, units)
        normed_a, inv_a, slope_a, inner_a, sent_a = lift(order, info, "a", tokens, ctx_a, ctx_a_there, *args, "lift_a")
        if direct:
            d_own = place(order, info, [d_four, d_x], (0, 4, 2, 6, 1, 5, 3, 7), "place_d", warm=[grad_out, weights], deps=[ctx_c_there])
        d_oth = core_swap(d_own)
        normed_c, inv_c, slope_c, inner_c, sent_c = lift(order, info, "c", tokens, ctx_c, ctx_c_there, *args, "lift_c")
        part_c = drop(order, info, inner_c, sent_c, d_own, d_oth, "drop_c")
        part_c_there = [far_swap(p) for p in part_c]
        part_a = drop(order, info, inner_a, sent_a, d_own, d_oth, "drop_a")
        part_a_there = [far_swap(p) for p in part_a]
        got_hi_a, got_hi_c = core_swap(sent_a), core_swap(sent_c)
        args = (grad_out, weights, norms, u_own, u_oth, d_own, d_oth)
        res_c, two_c, up_c, fu_c, sums_c2, back_c = turn(
            order, info, "c", 0, normed_c, part_c[0], part_c_there[0], *args, slope_c, "turn_c", deps=[got_hi_a, got_hi_c])
        res_0, two_0, up_0, fu_0, sums_02, back_0 = turn(
            order, info, "a", 0, normed_a, part_a[0], part_a_there[0], *args, slope_a, "turn_0")
        result, two_1, up_1, fu_1, sums_12, back_a = turn(
            order, info, "a", CHUNK, normed_a, part_a[1], part_a_there[1], *args, slope_a, "turn_1", around=(res_0, res_c), before=back_0)
        back_a_there, back_c_there = far_swap(back_a), far_swap(back_c)
        fus = (fu_0, fu_1, fu_c)
        got_fus = [core_swap(x) for x in fus]
        width = tokens.shape[1]
        inners, sents = ((inner_a, 0), (inner_a, CHUNK), (inner_c, 0)), ((sent_a, 0), (sent_a, CHUNK), (sent_c, 0))
        gots = ((got_hi_a, 0), (got_hi_a, CHUNK), (got_hi_c, 0))
        pairs = [(f, 0, 0, x, r, 0) for f, (x, r) in zip(fus, inners)] + [(f, 0, 0, x, r, width) for f, (x, r) in zip(got_fus, gots)]
        grad_d = grads(order, info, pairs, width, units, "grads_d", split=direct)
        ups = (up_0, up_1, up_c)
        pairs = [(x, r, 0, u, 0, 0) for (x, r), u in zip(sents, ups)] + [(x, r, 0, f, 0, width) for (x, r), f in zip(gots, got_fus)]
        grad_u = grads(order, info, pairs, width, units, "grads_u", split=direct)
        res_there = core_swap(result)

        def second_fold(parts, name, **kw):
            here, away = fold_pair(order, info, *parts, "pair_" + name, **kw)
            return here, dp_swap(away, 2)

        def third_fold(pair, name, **kw):
            here, away = fold_last(order, info, *pair, "last_" + name, **kw)
            return here, dp_swap(away, 4)

        if direct:
            fold_d, fold_u = (grad_d[0], dp_swap(grad_d[1], 1)), (grad_u[0], dp_swap(grad_u[1], 1))
        if direct:
            fold_d = second_fold(fold_d, "d", deps=[back_a_there])
        one_a, low_a, pg_a, pg_a_oth, sums_a1, in_a = attend_back(
            order, info, "a", (two_0, two_1), back_a, back_a_there, normed_a, inv_a, norms, o_here, q_a, k_a, v_a, lse_a, (q_own, q_oth), local, "back_a")
        in_a_there = far_swap(in_a)
        got_a = core_swap(pg_a_oth)
        if direct:
            fold_d = third_fold(fold_d, "d")
        one_c, low_c, sums_c1, dq_c, kv_mine, sent = attend_back(
            order, info, "c", (two_c,), back_c, back_c_there, normed_c, inv_c, norms, o_here, q_c, k_c, v_c, lse_c, None, local, "back_c")
        got_c = core_swap(sent)
        if direct:
            fold_u = second_fold(fold_u, "u")
        out_mine, out_oth = grads_out(
            order, info, (low_a, low_c), (ctx_a, ctx_c), ((sums_a1, sums_c1), (sums_02, sums_12, sums_c2)), local)
        out_got = core_swap(out_oth)
        grad_a = grads_attn(order, info, tokens, pg_a, got_a, dq_c, kv_mine, sent, got_c, split=direct)
        everything = slice(None)
        if direct:
            fold_1 = grad_a[0], dp_swap(grad_a[1], 1)
            keep, send = fold_both(order, info, out_mine, out_got, "side_o")
            fold_2 = keep, dp_swap(send, 1)
        in_c = project_back(order, info, dq_c, kv_mine, got_c, q_own, q_oth, local, "project_c")
        in_c_there = far_swap(in_c)
        if direct:
            fold_u = third_fold(fold_u, "u")
            fold_1 = second_fold(fold_1, "qkv", deps=[fold_d[1]])
            fold_2 = second_fold(fold_2, "o")
            n_down = update(order, rates, [fold_d], [
                (down_t, first_down.T, second_down.T, DECAY_RATE, [(everything, 0, 0, units, False)])], "update_d")
            fold_1 = third_fold(fold_1, "qkv", deps=[fold_u[1]])
            fold_2 = third_fold(fold_2, "o")
        gi = add_rows(order, info, [(one_a, in_a, in_a_there), (one_c, in_c, in_c_there)], "add_in")
        gi_there = core_swap(gi)
        if direct:
            n_up = update(order, rates, [fold_u], [
                (up_weight, first_up, second_up, DECAY_RATE, [(everything, 0, 0, units, False)])], "update_u")
        if direct:
            res = update(order, rates, [fold_1, fold_2], [
                (qkv_weight, first_qkv, second_qkv, DECAY_RATE,
                 [(c, 0, c * local, local, False) for c in range(3)]),
                (out_weight, first_out, second_out, DECAY_RATE, [(everything, 1, 0, local, True)]),
                (norm_params, first_norm, second_norm, 0.0, [(everything, 1, local, 128, True)]),
            ], "update_a", flops=100_000_000_000)
            n_down = [x.T for x in n_down]
            n_qkv, n_out, n_norm = res[:4], res[4:8], res[8:]
        input_grad, res_full = lay_rows(order, info, [(gi, gi_there), (result, res_there)], "lay_out")
        if not direct:
            grad_o = out_mine + out_got.astype(F32)
            su, sd, sa, so = (
                lax.psum_scatter(x, "dp", scatter_dimension=0, tiled=True) for x in (grad_u, grad_d, grad_a, grad_o))
            rest = (rate, fix_one, fix_two)
            n_up = adamw_update(su, up_weight, first_up, second_up, *rest, DECAY_RATE)
            n_down = adamw_update(sd.T, down_weight, first_down, second_down, *rest, DECAY_RATE)
            sq = jnp.stack([sa[:, c * local : (c + 1) * local] for c in range(3)])
            n_qkv = adamw_update(sq, qkv_weight, first_qkv, second_qkv, *rest, DECAY_RATE)
            n_out = adamw_update(so[:, :local].T, out_weight, first_out, second_out, *rest, DECAY_RATE)
            n_norm = adamw_update(so[:, local : local + 4].T, norm_params, first_norm, second_norm, *rest, 0.0)
        return (res_full, input_grad, *n_qkv, *n_out, *n_up, *n_down, *n_norm)

    rows = P("dp", None)
    qkv, col, row, norm = P(None, "dp", "tensor"), P("tensor", "dp"), P("dp", "tensor"), P(None, "dp")
    params = (qkv, col, row, col, norm)
    return jax.shard_map(
        on_device,
        mesh=mesh,
        in_specs=(rows, rows, P("dp"), P("dp"), P()) + params * 3,
        out_specs=(rows, rows) + (qkv,) * 4 + (col,) * 4 + (row,) * 4 + (col,) * 4 + (norm,) * 4,
        check_vma=False,
    )
```
